32 devices in a mesh: gx: 2 (over x), gy: 4 (over y, core), gz: 4 (over z).
Axes of the slice: x: 2, y: 2, z: 4, core: 2. Of those that a mesh axis runs over, the one named last changes fastest.
Arguments:
- states: float32 [19, 32, 64, 512], P(None, 'gx', 'gy', 'gz'), may hold values from 0 to 1
- active: int32 [4, 4, 4], P('gx', 'gy', 'gz'), may hold values 0 or 1
- fibre_index: int32 [4, 4, 4], P('gx', 'gy', 'gz'), may hold values from 0 to 63
- fibre_angle: float32 [2, 64], replicated, may hold values from -3.140625 to 3.140625
- conduct: float32 [2, 64], replicated, may hold values from 0.05 to 0.3
- gate_half: float32 [17], replicated, may hold values from 0.1 to 0.9
- gate_slope: float32 [17], replicated, may hold values from 0.05 to 0.3
- gate_tau: float32 [17], replicated, may hold values from 2 to 60
- conductance: float32 [17], replicated, may hold values from 0.005 to 0.05
- reversal: float32 [17], replicated, may hold values from -1 to 1.5
- block_elem: int32 [16, 32, 16], P('gx', 'gy', 'gz'), may hold values from 0 to 8191, as said below
- block_weight: float32 [16, 32, 16], P('gx', 'gy', 'gz'), may hold values from 0.5 to 1.5
- node_disp: float32 [3, 16384], P(None, ('gx', 'gy', 'gz')), may hold values from -0.15 to 0.15
- elem_node: int32 [8, 8192], P(None, ('gx', 'gy', 'gz')), may hold values from 0 to 404, as said below
- elem_fibre: int32 [8192], P(('gx', 'gy', 'gz')), may hold values from 0 to 63
- material: float32 [3], replicated, may hold values from 0.5 to 2
Outputs:
- new_states: float32 [19, 32, 64, 512], P(None, 'gx', 'gy', 'gz')
- fine_disp: float32 [3, 32, 64, 512], P(None, 'gx', 'gy', 'gz')
- node_residual: float32 [3, 16384], P(None, ('gx', 'gy', 'gz'))
The draws below stay inside these ranges and needn't reach their ends.
Inputs may be any that keep to these rules, and one draw needn't show every extreme that they name: `block_elem`: element numbers of the coarse partition: owner device e // 256, local element e % 256. Every element holds exactly one coupling block. Of the coupling blocks of one device at most 16 lie in elements of one owner device, and for every device some owner receives exactly 16 of them. `elem_node`: each column names eight distinct owner-local nodes of a hexahedral element of a structured partition, corner 4 i + 2 j + k at offset (i, j, k); neighbouring elements of one owner share nodes.
All inputs are finite; a program needn't handle non-finite values. No bound on the sum of `active` on one device may be relied on, other than what follows from the above.
Results may differ from the reference program's by a relative error of at most 0.0003.
Values sent between devices are 32-bit elements; how exact they have to be, the bound alone decides.
A program may use at most 64 MiB of HBM per device.

```python
import math
import jax
import jax.numpy as jnp
from jax import lax

NSTATE = 19
NCH = 17
NF = 64
TLX = 8
TLY = 16
TLZ = 128
SBX = 2
SBY = 2
SBZ = 32
FINE_STEPS = 2
ELX = 8
ELY = 8
CX = 16
CY = 16
CZ = 128
NX = 32
NY = 64
NZ = 512
TX = 4
TY = 4
TZ = 4
BX = 16
BY = 32
BZ = 16
ELZ = 4
ELEM_DEV = 256
NODE_DEV = 512
ELEMS = 8192
NODES = 16384


def draw_block_elem(key, part):
    grid_x = NX // CX
    grid_y = NY // CY
    grid_z = NZ // CZ
    device_count = grid_x * grid_y * grid_z
    blocks_x = CX // SBX
    blocks_y = CY // SBY
    blocks_z = CZ // SBZ
    block_count = blocks_x * blocks_y * blocks_z
    capacity = 2 * block_count // device_count
    halfcap = capacity // 2
    slot_count = device_count * capacity
    base = jax.random.fold_in(key, 7)
    first, second, third, fourth = jax.random.split(base, 4)
    shift_full = jax.random.randint(first, (), 0, device_count, dtype=jnp.int32)
    shift_empty = (shift_full + jax.random.randint(second, (), 1, device_count, dtype=jnp.int32)) % device_count
    sigma = jax.random.permutation(third, device_count).astype(jnp.int32)
    distance = (sigma[None, :] - sigma[:, None]) % device_count
    counts = halfcap + halfcap * (distance == shift_full).astype(jnp.int32) - halfcap * (distance == shift_empty).astype(jnp.int32)
    starts = jnp.cumsum(counts, axis=0) - counts

    def owner_perm(index):
        return jax.random.permutation(jax.random.fold_in(fourth, index), ELEM_DEV).astype(jnp.int32)
    perms = jax.vmap(owner_perm)(jnp.arange(device_count, dtype=jnp.int32))

    def one_device(index):
        inner = jax.random.fold_in(jax.random.fold_in(key, 13), index)
        owners = jnp.arange(device_count, dtype=jnp.int32)[:, None]
        ranks = jnp.arange(capacity, dtype=jnp.int32)[None, :]
        valid = ranks < counts[index][:, None]
        where = jnp.clip(starts[index][:, None] + ranks, 0, ELEM_DEV - 1)
        local = perms[owners, where]
        ids = (owners * ELEM_DEV + local).reshape(-1)
        places = jnp.arange(slot_count, dtype=jnp.int32)
        score = jnp.where(valid.reshape(-1), slot_count + places, places)
        unused, chosen = lax.top_k(score, block_count)
        order = jax.random.permutation(inner, block_count)
        return ids[chosen][order].reshape(blocks_x, blocks_y, blocks_z)
    every = jax.vmap(one_device)(jnp.arange(device_count, dtype=jnp.int32))
    every = every.reshape(grid_x, grid_y, grid_z, blocks_x, blocks_y, blocks_z)
    return every.transpose(0, 3, 1, 4, 2, 5).reshape(grid_x * blocks_x, grid_y * blocks_y, grid_z * blocks_z)


def draw_elem_node(key, part):
    device_count = ELEMS // ELEM_DEV
    used = (ELX + 1) * (ELY + 1) * (ELZ + 1)
    corner = jnp.arange(8, dtype=jnp.int32)[:, None]
    cell = jnp.arange(ELEM_DEV, dtype=jnp.int32)[None, :]
    node_x = cell // (ELY * ELZ) + corner // 4
    node_y = cell // ELZ % ELY + corner // 2 % 2
    node_z = cell % ELZ + corner % 2
    structured = (node_x * (ELY + 1) + node_y) * (ELZ + 1) + node_z

    def one_device(index):
        inner = jax.random.fold_in(jax.random.fold_in(key, 11), index)
        first, second = jax.random.split(inner)
        label = jax.random.permutation(first, used).astype(jnp.int32)
        order = jax.random.permutation(second, ELEM_DEV)
        return label[structured][:, order]
    every = jax.vmap(one_device)(jnp.arange(device_count, dtype=jnp.int32))
    return every.transpose(1, 0, 2).reshape(8, device_count * ELEM_DEV)


def place_ends(array, stream_key, low, top_value):
    longest = array.shape.index(max(array.shape))
    spots = []
    for shift in (0, 1):
        where = [jax.random.randint(jax.random.fold_in(stream_key, axis), (), 0, length) for axis, length in enumerate(array.shape)]
        where[longest] = (where[longest] + shift) % array.shape[longest]
        spots.append(tuple(where))
    return array.at[spots[0]].set(low).at[spots[1]].set(top_value)


def block_levels(stream_key, shape, cuts, low, largest):
    factor_of, own = 1.0, jax.random.fold_in(stream_key, 6)
    for dim, shards_of in cuts:
        draws = jnp.exp(jax.random.uniform(jax.random.fold_in(own, dim), (shards_of,), jnp.float32, low / len(cuts), largest / len(cuts)))
        factor_of = factor_of * jnp.repeat(draws, shape[dim] // shards_of).reshape([-1 if axis == dim else 1 for axis in range(len(shape))])
    return factor_of


def scatter_about(own_key, dims, deviation, bound, cuts=(), held_as=jnp.bfloat16):
    level = block_levels(own_key, dims, cuts, -0.22, 0.18) if cuts else 1.0
    drawn = jax.random.normal(own_key, dims, jnp.float32) * deviation * level
    return jnp.minimum(jnp.maximum(drawn, -bound), bound).astype(held_as)


def setup_inputs(seed: int = 0) -> dict:
    arg_keys = jax.random.split(jax.random.key(seed), 17)
    states = jnp.clip(1.0 * jax.random.uniform(arg_keys[0], (NSTATE, NX, NY, NZ), jnp.float32) ** block_levels(arg_keys[0], (NSTATE, NX, NY, NZ), ((1, 2), (2, 4), (3, 4)), -0.2, 0.2), 0.0, 1.0)
    active = place_ends((jax.random.randint(arg_keys[1], (TX, TY, TZ), 0, 4) < 3).astype(jnp.int32), jax.random.fold_in(arg_keys[1], 1), 0, 1)
    fibre_index = place_ends(jax.random.randint(arg_keys[2], (TX, TY, TZ), 0, NF), jax.random.fold_in(arg_keys[2], 1), 0, NF - 1).astype(jnp.int32)
    fibre_angle = jnp.clip(jax.random.uniform(arg_keys[3], (2, NF), jnp.float32, -3.140625, 3.140625), -3.140625, 3.140625)
    conduct = jnp.clip(jnp.exp(jax.random.uniform(arg_keys[4], (2, NF), jnp.float32, math.log(0.05), math.log(0.3))), 0.05, 0.3)
    gate_half = jnp.clip(jax.random.uniform(arg_keys[5], (NCH,), jnp.float32, 0.1, 0.9), 0.1, 0.9)
    gate_slope = jnp.clip(jnp.exp(jax.random.uniform(arg_keys[6], (NCH,), jnp.float32, math.log(0.05), math.log(0.3))), 0.05, 0.3)
    gate_tau = jnp.clip(jnp.exp(jax.random.uniform(arg_keys[7], (NCH,), jnp.float32, math.log(2.0), math.log(60.0))), 2.0, 60.0)
    conductance = jnp.clip(jnp.exp(jax.random.uniform(arg_keys[8], (NCH,), jnp.float32, math.log(0.005), math.log(0.05))), 0.005, 0.05)
    reversal = jnp.clip(jax.random.uniform(arg_keys[9], (NCH,), jnp.float32, -1.0, 1.5), -1.0, 1.5)
    block_elem = draw_block_elem(jax.random.fold_in(arg_keys[16], 71), 0)
    block_weight = jnp.clip(0.5 + 1.0 * jax.random.uniform(arg_keys[11], (BX, BY, BZ), jnp.float32) ** block_levels(arg_keys[11], (BX, BY, BZ), ((0, 2), (1, 4), (2, 4)), -0.2, 0.2), 0.5, 1.5)
    node_disp = scatter_about(arg_keys[12], (3, NODES), 0.05, 0.15, ((1, 32),), jnp.float32)
    elem_node = draw_elem_node(jax.random.fold_in(arg_keys[16], 71), 0)
    elem_fibre = place_ends(jax.random.randint(arg_keys[14], (ELEMS,), 0, NF), jax.random.fold_in(arg_keys[14], 1), 0, NF - 1).astype(jnp.int32)
    material = jnp.clip(jnp.exp(jax.random.uniform(arg_keys[15], (3,), jnp.float32, math.log(0.5), math.log(2.0))), 0.5, 2.0)
    return {"states": states, "active": active, "fibre_index": fibre_index, "fibre_angle": fibre_angle, "conduct": conduct, "gate_half": gate_half, "gate_slope": gate_slope, "gate_tau": gate_tau, "conductance": conductance, "reversal": reversal, "block_elem": block_elem, "block_weight": block_weight, "node_disp": node_disp, "elem_node": elem_node, "elem_fibre": elem_fibre, "material": material}


calcium_keep = 0.9
tension_half = 0.09
highest = lax.Precision.HIGHEST


def fibre_frame(first_angle, second_angle):
    return jnp.stack([jnp.cos(first_angle) * jnp.cos(second_angle), jnp.sin(first_angle) * jnp.cos(second_angle), jnp.sin(second_angle)], 0)


def coefficients(frame, along, across, live_tile):
    spread = along - across
    return jnp.stack([across + spread * frame[0] * frame[0], across + spread * frame[1] * frame[1], across + spread * frame[2] * frame[2], spread * frame[0] * frame[1], spread * frame[0] * frame[2], spread * frame[1] * frame[2]], 0) * live_tile


def expand(tiles):
    return jnp.repeat(jnp.repeat(jnp.repeat(tiles, TLX, 1), TLY, 2), TLZ, 3)


def ionic(states, live, gate_half, gate_slope, gate_tau, conductance, reversal):
    volt = states[0]
    shape = (gate_half.shape[0],) + (1,) * (states.ndim - 1)
    steady = jax.nn.sigmoid((volt[None] - gate_half.reshape(shape)) / gate_slope.reshape(shape))
    keeping = jnp.exp(-1.0 / gate_tau).reshape(shape)
    old_gates = states[1:NSTATE - 1]
    gates = steady + (old_gates - steady) * keeping
    current = jnp.sum(conductance.reshape(shape) * gates * (volt[None] - reversal.reshape(shape)), axis=0)
    vstar = volt - current
    calcium = states[NSTATE - 1] * calcium_keep + (1.0 - calcium_keep) * jax.nn.sigmoid(8.0 * (volt - 0.5))
    alive = live > 0.5
    gates = jnp.where(alive[None], gates, old_gates)
    vstar = jnp.where(alive, vstar, volt)
    calcium = jnp.where(alive, calcium, states[NSTATE - 1])
    return gates, vstar, calcium


def fluxes(padded, coef):
    grad_x = (padded[2:, 1:-1, 1:-1] - padded[:-2, 1:-1, 1:-1]) * 0.5
    grad_y = (padded[1:-1, 2:, 1:-1] - padded[1:-1, :-2, 1:-1]) * 0.5
    grad_z = (padded[1:-1, 1:-1, 2:] - padded[1:-1, 1:-1, :-2]) * 0.5
    return jnp.stack([coef[0] * grad_x + coef[3] * grad_y + coef[4] * grad_z, coef[3] * grad_x + coef[1] * grad_y + coef[5] * grad_z, coef[4] * grad_x + coef[5] * grad_y + coef[2] * grad_z], 0)


def divergence(flux):
    return (flux[0, 2:, 1:-1, 1:-1] - flux[0, :-2, 1:-1, 1:-1]) * 0.5 + (flux[1, 1:-1, 2:, 1:-1] - flux[1, 1:-1, :-2, 1:-1]) * 0.5 + (flux[2, 1:-1, 1:-1, 2:] - flux[2, 1:-1, 1:-1, :-2]) * 0.5


def corner_bits():
    corner = jnp.arange(8, dtype=jnp.int32)
    return jnp.stack([corner // 4, (corner // 2) % 2, corner % 2], 1).astype(jnp.float32)


def shape_gradients():
    return (2.0 * corner_bits() - 1.0) * 0.25


def blend_weights():
    bits = corner_bits()
    place = jnp.arange(SBX * SBY * SBZ, dtype=jnp.int32)
    along_x = ((place // (SBY * SBZ)).astype(jnp.float32) + 0.5) / SBX
    along_y = (((place // SBZ) % SBY).astype(jnp.float32) + 0.5) / SBY
    along_z = ((place % SBZ).astype(jnp.float32) + 0.5) / SBZ
    local = jnp.stack([along_x, along_y, along_z], 0)
    factor = jnp.where(bits[:, :, None] > 0.5, local[None], 1.0 - local[None])
    return factor[:, 0] * factor[:, 1] * factor[:, 2]


def element_forces(corner_disp, frame, tension, material):
    grads = shape_gradients()
    deform = jnp.einsum('iae,aj->ije', corner_disp, grads, precision=highest) + jnp.eye(3, dtype=jnp.float32)[:, :, None]
    cof = jnp.stack([
        jnp.stack([deform[1, 1] * deform[2, 2] - deform[1, 2] * deform[2, 1], deform[1, 2] * deform[2, 0] - deform[1, 0] * deform[2, 2], deform[1, 0] * deform[2, 1] - deform[1, 1] * deform[2, 0]], 0),
        jnp.stack([deform[0, 2] * deform[2, 1] - deform[0, 1] * deform[2, 2], deform[0, 0] * deform[2, 2] - deform[0, 2] * deform[2, 0], deform[0, 1] * deform[2, 0] - deform[0, 0] * deform[2, 1]], 0),
        jnp.stack([deform[0, 1] * deform[1, 2] - deform[0, 2] * deform[1, 1], deform[0, 2] * deform[1, 0] - deform[0, 0] * deform[1, 2], deform[0, 0] * deform[1, 1] - deform[0, 1] * deform[1, 0]], 0)], 0)
    volume = deform[0, 0] * cof[0, 0] + deform[0, 1] * cof[0, 1] + deform[0, 2] * cof[0, 2]
    inverse_t = cof / volume
    stretch = jnp.sum(deform * frame[None], axis=1)
    stress = material[0] * (deform - inverse_t) + material[1] * jnp.log(volume) * inverse_t + material[2] * tension * stretch[:, None] * frame[None]
    return jnp.einsum('ije,aj->iae', stress, grads, precision=highest)


def reference(states, active, fibre_index, fibre_angle, conduct, gate_half, gate_slope, gate_tau, conductance, reversal, block_elem, block_weight, node_disp, elem_node, elem_fibre, material):
    frame = fibre_frame(fibre_angle[0][fibre_index], fibre_angle[1][fibre_index])
    live_tile = (active > 0).astype(jnp.float32)
    coef = expand(coefficients(frame, conduct[0][fibre_index], conduct[1][fibre_index], live_tile))
    live = expand(live_tile[None])[0]
    for step in range(FINE_STEPS):
        gates, vstar, calcium = ionic(states, live, gate_half, gate_slope, gate_tau, conductance, reversal)
        flux = fluxes(jnp.pad(vstar, 1), coef)
        lap = divergence(jnp.pad(flux, ((0, 0), (1, 1), (1, 1), (1, 1))))
        states = jnp.concatenate([(vstar + live * lap)[None], gates, calcium[None]], 0)
    calcium = states[NSTATE - 1]
    tension = calcium * calcium / (calcium * calcium + tension_half)
    block_mean = tension.reshape(BX, SBX, BY, SBY, BZ, SBZ).mean(axis=(1, 3, 5)).reshape(-1)
    block_value = block_weight.reshape(-1) * block_mean
    flat_ids = block_elem.reshape(-1)
    elem_tension = jax.ops.segment_sum(block_value, flat_ids, num_segments=ELEMS)
    owner = jnp.arange(ELEMS, dtype=jnp.int32) // ELEM_DEV
    global_nodes = owner[None, :] * NODE_DEV + elem_node
    corner_disp = node_disp[:, global_nodes]
    elem_frame = fibre_frame(fibre_angle[0][elem_fibre], fibre_angle[1][elem_fibre])
    force = element_forces(corner_disp, elem_frame, elem_tension, material)
    flat_nodes = global_nodes.reshape(-1)
    node_residual = jnp.stack([jax.ops.segment_sum(force[k].reshape(-1), flat_nodes, num_segments=NODES) for k in range(3)], 0)
    block_nodes = (flat_ids // ELEM_DEV)[None, :] * NODE_DEV + elem_node[:, flat_ids]
    block_disp = node_disp[:, block_nodes]
    fine = jnp.einsum('cab,ap->cbp', block_disp, blend_weights(), precision=highest)
    fine_disp = fine.reshape(3, BX, BY, BZ, SBX, SBY, SBZ).transpose(0, 1, 4, 2, 5, 3, 6).reshape(3, NX, NY, NZ)
    return states, fine_disp, node_residual
```

```python
import functools

import jax
import jax.numpy as jnp
from jax import lax
from jax.experimental import pallas as pl
from jax.experimental.pallas import tpu as pltpu
from jax.sharding import PartitionSpec as P

NSTATE = 19
TLX = 8
SBX = 2
SBY = 2
SBZ = 32
FINE_STEPS = 2
AXES = ("gx", "gy", "gz")
MESH = pl.DeviceIdType.MESH
LANES = 128
f32 = jnp.float32
bf16 = jnp.bfloat16
calcium_keep = 0.9
tension_half = 0.09
NN = (((1,), (0,)), ((), ()))
NT = (((1,), (1,)), ((), ()))


def mm(a, b, dims=NN):
    return lax.dot_general(a, b, dims, preferred_element_type=f32)


def parts3(x):
    x1 = x.astype(bf16)
    r1 = x - x1.astype(f32)
    x2 = r1.astype(bf16)
    x3 = (r1 - x2.astype(f32)).astype(bf16)
    return x1, x2, x3


def rows3(x):
    return jnp.concatenate([p.astype(f32) for p in parts3(x)], 0).astype(bf16)


def fold3(y):
    r = y.shape[0] // 3
    return y[:r] + y[r : 2 * r] + y[2 * r :]


def mm_right3(a, x, dims=NN):
    x1, x2, x3 = parts3(x)
    return mm(a, x1, dims) + mm(a, x2, dims) + mm(a, x3, dims)


def iota(shape, dim):
    return lax.broadcasted_iota(jnp.int32, shape, dim)


def column(row):
    pieces = [
        jnp.transpose(jnp.broadcast_to(row[:, i : i + LANES], (LANES, LANES)))
        for i in range(0, row.shape[1], LANES)
    ]
    return pieces[0] if len(pieces) == 1 else jnp.concatenate(pieces, 0)


def onehot(mask):
    return jnp.where(mask, 1.0, 0.0).astype(bf16)


def pick_rows(rows, shape):
    index = iota(shape, 0)
    out = jnp.zeros(shape, f32)
    for i, row in enumerate(rows):
        out = jnp.where(index == i, row, out)
    return out


def lane_gather(x, index):
    return jnp.take_along_axis(x, index, axis=1, mode="promise_in_bounds")


def sigmoid(u):
    return 0.5 * jnp.tanh(0.5 * u) + 0.5


def frame_of(a, b):
    return jnp.cos(a) * jnp.cos(b), jnp.sin(a) * jnp.cos(b), jnp.sin(b)


def body(
    sizes,
    states,
    active,
    fibre_index,
    angle_s,
    angle_v,
    conduct,
    gate_half,
    gate_slope,
    gate_tau,
    conductance,
    reversal,
    ids_ref,
    weight_ref,
    node_disp,
    elem_node,
    elem_fibre,
    material,
    out,
    fine_out,
    resid_out,
    vs,
    flux,
    send_y,
    send_z,
    halo_x,
    halo_y,
    halo_z,
    corner_oh,
    corner_cd,
    slot_oh,
    pick_oh,
    owner_oh,
    rank_oh,
    ids_send,
    ids_got,
    val_send,
    val_got,
    ans_send,
    ans_got,
    face_send_sem,
    face_recv_sem,
    all_send_sem,
    all_recv_sem,
):
    mx, my, mz, seats, elem_count = sizes
    n = mx * my * mz
    nx, ny, nz = states.shape[1:]
    gates_n = NSTATE - 2
    bx, by, bz = nx // SBX, ny // SBY, nz // SBZ
    plane = bx * by
    blocks = plane * bz
    slots = n * seats
    tiles = nx // TLX
    node_count = node_disp.shape[1]
    corners = 8
    cx, cy, cz = (lax.axis_index(a) for a in AXES)
    me = (cx * my + cy) * mz + cz

    def coords(flat):
        return flat // (my * mz), (flat // mz) % my, flat % mz

    barrier = pltpu.get_barrier_semaphore()

    def greet(k, carry):
        pl.semaphore_signal(
            barrier, inc=1, device_id=coords((me + k) % n), device_id_type=MESH
        )
        return carry

    lax.fori_loop(1, n, greet, 0)

    def splat(value):
        return jnp.full((1, 1, LANES), value, f32)

    coef, live = [], []
    for t in range(tiles):
        index = fibre_index[0, 0, t]
        fx, fy, fz = frame_of(splat(angle_s[0, index]), splat(angle_s[1, index]))
        across = splat(conduct[1, index])
        spread = splat(conduct[0, index]) - across
        alive = splat(jnp.where(active[0, 0, t] > 0, 1.0, 0.0).astype(f32))
        live.append(alive)
        coef.append(
            [
                (across + spread * fx * fx) * alive,
                (across + spread * fy * fy) * alive,
                (across + spread * fz * fz) * alive,
                spread * fx * fy * alive,
                spread * fx * fz * alive,
                spread * fy * fz * alive,
            ]
        )

    chunk = 4

    def ionic(source, t):
        alive = live[t] > 0.5

        def step(i, carry):
            at = pl.ds(t * TLX + i * chunk, chunk)
            volt = source[0, at]
            current = jnp.zeros_like(volt)
            for g in range(gates_n):
                inv = 1.0 / splat(gate_slope[g])
                keep = jnp.exp(-1.0 / splat(gate_tau[g]))
                steady = sigmoid((volt - splat(gate_half[g])) * inv)
                old = source[1 + g, at]
                gate = steady + (old - steady) * keep
                current = current + splat(conductance[g]) * gate * (volt - splat(reversal[g]))
                out[1 + g, at] = jnp.where(alive, gate, old)
            old = source[NSTATE - 1, at]
            calcium = old * calcium_keep + (1.0 - calcium_keep) * sigmoid(8.0 * (volt - 0.5))
            out[NSTATE - 1, at] = jnp.where(alive, calcium, old)
            vs[at] = jnp.where(alive, volt - current, volt)
            return carry

        lax.fori_loop(0, TLX // chunk, step, 0)

    def face_copies(stage, low_x, high_x):
        near = [(cx, mx), (cy, my), (cz, mz)]
        made = []
        for dim in range(3):
            for side in range(2):
                if dim == 0:
                    src = high_x if side == 0 else low_x
                    dst = halo_x.at[stage, side]
                elif dim == 1:
                    src, dst = send_y.at[stage, side], halo_y.at[stage, side]
                else:
                    src, dst = send_z.at[stage, side], halo_z.at[stage, side]
                at, count = near[dim]
                to = [cx, cy, cz]
                to[dim] = (at + (1 if side == 0 else count - 1)) % count
                made.append(
                    pltpu.make_async_remote_copy(
                        src_ref=src,
                        dst_ref=dst,
                        send_sem=face_send_sem.at[stage, 2 * dim + side],
                        recv_sem=face_recv_sem.at[stage, 2 * dim + side],
                        device_id=tuple(to),
                        device_id_type=MESH,
                    )
                )
        return made

    def flat_z(a):
        return jnp.transpose(a.reshape(nx * ny, nz))

    def send_faces(stage, a_y, a_z, low_x, high_x):
        send_y[stage, 0] = a_y[:, ny - 1 : ny, :]
        send_y[stage, 1] = a_y[:, 0:1, :]
        turned = flat_z(a_z)
        send_z[stage, 0] = turned[nz - 1 : nz, :]
        send_z[stage, 1] = turned[0:1, :]
        copies = face_copies(stage, low_x, high_x)
        for c in copies:
            c.start()
        return copies

    def masked(value, inside):
        return jnp.where(inside, value, 0.0)

    def diff_x(a, stage):
        low = masked(halo_x[stage, 0], cx > 0)[None]
        high = masked(halo_x[stage, 1], cx < mx - 1)[None]
        up = jnp.concatenate([a[1:], high], 0)
        down = jnp.concatenate([low, a[:-1]], 0)
        return (up - down) * 0.5

    def diff_y(a, stage):
        low = masked(halo_y[stage, 0], cy > 0)
        high = masked(halo_y[stage, 1], cy < my - 1)
        row = iota((1, ny, nz), 1)
        down = jnp.where(row == 0, low, pltpu.roll(a, 1, 1))
        up = jnp.where(row == ny - 1, high, pltpu.roll(a, ny - 1, 1))
        return (up - down) * 0.5

    def diff_z(a, stage):
        low = masked(halo_z[stage, 0], cz > 0)
        high = masked(halo_z[stage, 1], cz < mz - 1)
        row = iota((nz, nx * ny), 0)
        edge = jnp.where(row == 0, low, jnp.where(row == nz - 1, high, 0.0))
        edge = jnp.transpose(edge).reshape(nx, ny, nz)
        lane = iota((1, 1, nz), 2)
        down = jnp.where(lane == 0, edge, pltpu.roll(a, 1, 2))
        up = jnp.where(lane == nz - 1, edge, pltpu.roll(a, nz - 1, 2))
        return (up - down) * 0.5

    def make_flux(stage):
        v = vs[...]
        gx, gy, gz = diff_x(v, stage), diff_y(v, stage), diff_z(v, stage)
        for t in range(tiles):
            at = slice(t * TLX, (t + 1) * TLX)
            xx, yy, zz, xy, xz, yz = coef[t]
            a, b, c = gx[at], gy[at], gz[at]
            flux[0, at] = xx * a + xy * b + xz * c
            flux[1, at] = xy * a + yy * b + yz * c
            flux[2, at] = xz * a + yz * b + zz * c

    def finish(stage):
        lap = diff_x(flux[0], stage) + diff_y(flux[1], stage) + diff_z(flux[2], stage)
        for t in range(tiles):
            at = slice(t * TLX, (t + 1) * TLX)
            out[0, at] = vs[at] + live[t] * lap[at]

    def all_copy(k, kind, src, dst):
        return pltpu.make_async_remote_copy(
            src_ref=src.at[(me + k) % n],
            dst_ref=dst.at[me],
            send_sem=all_send_sem.at[kind, k],
            recv_sem=all_recv_sem.at[kind, k],
            device_id=coords((me + k) % n),
            device_id_type=MESH,
        )

    def all_start(kind, src, dst):
        dst[pl.ds(me, 1)] = src[pl.ds(me, 1)]

        def go(k, carry):
            all_copy(k, kind, src, dst).start()
            return carry

        lax.fori_loop(1, n, go, 0)

    def all_wait(kind, src, dst):
        def go(k, carry):
            pltpu.make_async_remote_copy(
                src_ref=src.at[(me + k) % n],
                dst_ref=dst.at[(me + n - k) % n],
                send_sem=all_send_sem.at[kind, k],
                recv_sem=all_recv_sem.at[kind, k],
                device_id=coords((me + k) % n),
                device_id_type=MESH,
            ).wait()
            return carry

        lax.fori_loop(1, n, go, 0)

    per_row = LANES // seats
    groups = slots // LANES

    def lanes_of(got):
        pieces = []
        for g in range(groups):
            pieces.append(
                lax.fori_loop(
                    0,
                    per_row,
                    lambda r, acc, g=g: acc + got[g * per_row + r],
                    jnp.zeros((1, LANES), f32),
                )
            )
        return jnp.concatenate(pieces, 1)

    for t in range(tiles):
        ionic(states, t)
    shift = elem_count.bit_length() - 1

    def flat_row(ref):
        place = lax.rem(iota((by, blocks), 1), plane)
        spread = jnp.zeros((bz, blocks), f32)
        for i in range(bx):
            put = onehot(place == iota((by, blocks), 0) + i * by)
            for part in parts3(ref[i].astype(f32)):
                spread = spread + mm(part, put)
        mine = iota((bz, blocks), 1) // plane == iota((bz, blocks), 0)
        return jnp.sum(jnp.where(mine, spread, 0.0), axis=0, keepdims=True)

    ids = flat_row(ids_ref).astype(jnp.int32)
    weight_col = column(flat_row(weight_ref))
    owner = lax.shift_right_logical(ids, shift)
    local = ids - owner * elem_count
    owner_col = column(owner.astype(f32))
    owner_f = owner.astype(f32)
    owner_cols = jnp.concatenate([owner_col] * (blocks // LANES), 1)
    earlier = (owner_cols == owner_f) & (iota((blocks, blocks), 1) < iota((blocks, blocks), 0))
    rank = jnp.sum(jnp.where(earlier, 1.0, 0.0), axis=1, keepdims=True)
    offset = ((me % per_row) * seats).astype(f32)
    rank_hit = onehot(iota((blocks, LANES), 1).astype(f32) == rank + offset)
    rank_oh[...] = rank_hit
    owned = owner == iota((n, blocks), 0)
    owner_oh[...] = onehot(owned)
    slot_col = owner_col[:, 0:1] * seats + rank
    slot_oh[...] = onehot(iota((blocks, slots), 1).astype(f32) == slot_col)
    wanted = jnp.where(owned, local.astype(f32) + 1.0, 0.0).astype(bf16)
    ids_send[...] = mm(wanted, rank_hit).reshape(n, 1, LANES)

    pl.semaphore_wait(barrier, n - 1)
    v0 = vs[...]
    stage0 = send_faces(0, v0, v0, vs.at[0], vs.at[nx - 1])
    all_start(0, ids_send, ids_got)

    index = elem_node[...]
    for h in range(0, elem_count, LANES):
        ix = index[:, h : h + LANES]
        low, high = ix % LANES, ix // LANES
        for i in range(3):
            value = jnp.zeros((corners, LANES), f32)
            for g in range(node_count // LANES):
                row = jnp.broadcast_to(node_disp[i : i + 1, g * LANES : (g + 1) * LANES], (corners, LANES))
                value = jnp.where(high == g, lane_gather(row, low), value)
            corner_cd[i, :, h : h + LANES] = value
    for q in range(corners):
        hit = onehot(iota((node_count, elem_count), 0) == elem_node[q : q + 1, :])
        corner_oh[q] = hit

    for c in stage0:
        c.wait()
    make_flux(0)
    stage1 = send_faces(1, flux[1], flux[2], flux.at[0, 0], flux.at[0, nx - 1])

    all_wait(0, ids_send, ids_got)
    asked = column(lanes_of(ids_got)) - 1.0
    asked = jnp.concatenate([asked] * (elem_count // LANES), 1)
    pick_oh[...] = onehot(iota((slots, elem_count), 1).astype(f32) == asked)
    table = jnp.concatenate(
        [corner_cd[...].reshape(corners * 3, elem_count), jnp.zeros((LANES - corners * 3, elem_count), f32)],
        0,
    )
    ans_send[...] = mm_right3(pick_oh[...], table, NT).reshape(n, seats, LANES)
    all_start(1, ans_send, ans_got)

    for c in stage1:
        c.wait()
    finish(1)
    for t in range(tiles):
        ionic(out, t)
    v1 = vs[...]
    stage2 = send_faces(2, v1, v1, vs.at[0], vs.at[nx - 1])

    calcium = out[NSTATE - 1]
    square = calcium * calcium
    pull = (square / (square + tension_half)).reshape(bx, SBX, ny, nz)
    pull = (pull[:, 0] + pull[:, 1]).reshape(bx * ny, nz)
    pair = onehot(iota((plane, bx * ny), 1) // SBY == iota((plane, bx * ny), 0))
    pooled = mm_right3(pair, pull)
    strip = onehot(iota((nz, LANES), 0) // SBZ == iota((nz, LANES), 1))
    pooled = fold3(mm(rows3(pooled), strip)) * (1.0 / (SBX * SBY * SBZ))
    worth = jnp.concatenate(
        [
            jnp.broadcast_to(pooled[:, b : b + 1], (plane, LANES))
            for b in range(bz)
        ],
        0,
    )
    worth = jnp.where(rank_oh[...].astype(f32) > 0.5, worth * weight_col, 0.0)
    val_send[...] = mm_right3(owner_oh[...], worth).reshape(n, 1, LANES)
    all_start(2, val_send, val_got)

    angle = angle_v[...]
    fx, fy, fz = frame_of(angle[0:1, :], angle[1:2, :])
    entries = angle.shape[1]
    fibres = pick_rows([fx, fy, fz], (8, entries))
    which = onehot(iota((entries, elem_count), 0) == elem_fibre[...])
    frames = fold3(mm(rows3(fibres), which))
    frame = [frames[i : i + 1, :] for i in range(3)]
    grads = [
        [((2 * (q // 4) - 1) / 4), ((2 * (q // 2 % 2) - 1) / 4), ((2 * (q % 2) - 1) / 4)]
        for q in range(corners)
    ]
    sums = [sum(corner_cd[:, q, :] * grads[q][j] for q in range(corners)) for j in range(3)]
    d = [
        [sums[j][i : i + 1, :] + (1.0 if i == j else 0.0) for j in range(3)] for i in range(3)
    ]
    cof = [
        [
            d[(i + 1) % 3][(j + 1) % 3] * d[(i + 2) % 3][(j + 2) % 3]
            - d[(i + 1) % 3][(j + 2) % 3] * d[(i + 2) % 3][(j + 1) % 3]
            for j in range(3)
        ]
        for i in range(3)
    ]
    volume = d[0][0] * cof[0][0] + d[0][1] * cof[0][1] + d[0][2] * cof[0][2]
    inverse = 1.0 / volume
    logv = jnp.log(volume)
    shear, bulk, scale = material[0], material[1], material[2]
    passive = [
        [
            shear * (d[i][j] - cof[i][j] * inverse) + bulk * logv * (cof[i][j] * inverse)
            for j in range(3)
        ]
        for i in range(3)
    ]
    stretch = [
        scale * (d[i][0] * frame[0] + d[i][1] * frame[1] + d[i][2] * frame[2]) for i in range(3)
    ]

    for c in stage2:
        c.wait()
    make_flux(2)
    stage3 = send_faces(3, flux[1], flux[2], flux.at[0, 0], flux.at[0, nx - 1])

    all_wait(1, ans_send, ans_got)
    returned = ans_got[...].reshape(slots, LANES)
    near = mm_right3(slot_oh[...], returned)
    lane = iota((plane, nz), 1)
    strip_of = lane // SBZ
    xi = ((lane % SBZ).astype(f32) + 0.5) / SBZ
    for c in range(3):
        lines = []
        for ij in range(4):
            ends = []
            for k in range(2):
                col = c * 8 + 2 * ij + k
                value = jnp.zeros((plane, nz), f32)
                for b in range(bz):
                    value = jnp.where(
                        strip_of == b, near[b * plane : (b + 1) * plane, col : col + 1], value
                    )
                ends.append(value)
            lines.append(ends[0] * (1.0 - xi) + ends[1] * xi)
        for iv in range(SBX):
            wx = (iv + 0.5) / SBX
            for jv in range(SBY):
                wy = (jv + 0.5) / SBY
                value = (
                    lines[0] * ((1 - wx) * (1 - wy))
                    + lines[1] * ((1 - wx) * wy)
                    + lines[2] * (wx * (1 - wy))
                    + lines[3] * (wx * wy)
                )
                for p in range(bx):
                    fine_out[c, SBX * p + iv, pl.ds(jv, by, stride=SBY), :] = value[
                        p * by : (p + 1) * by
                    ]

    for c in stage3:
        c.wait()
    finish(3)

    all_wait(2, val_send, val_got)
    arrived = jnp.broadcast_to(lanes_of(val_got), (8, slots))
    tension = fold3(mm(rows3(arrived), pick_oh[...]))[0:1, :]
    total = jnp.zeros((24, node_count), f32)
    stress = [
        [passive[i][j] + tension * stretch[i] * frame[j] for j in range(3)] for i in range(3)
    ]
    for q in range(corners):
        force = pick_rows(
            [
                stress[i][0] * grads[q][0] + stress[i][1] * grads[q][1] + stress[i][2] * grads[q][2]
                for i in range(3)
            ],
            (8, elem_count),
        )
        total = total + mm(rows3(force), corner_oh[q], NT)
    resid_out[...] = fold3(total)[0:3, :]


def shards(
    states,
    active,
    fibre_index,
    fibre_angle,
    conduct,
    gate_half,
    gate_slope,
    gate_tau,
    conductance,
    reversal,
    block_elem,
    block_weight,
    node_disp,
    elem_node,
    elem_fibre,
    material,
):
    mx, my, mz = (lax.axis_size(a) for a in AXES)
    n = mx * my * mz
    elem_count = elem_node.shape[1]
    node_count = node_disp.shape[1]
    nx, ny, nz = states.shape[1:]
    bx, by, bz = block_elem.shape
    blocks = bx * by * bz
    seats = max(2 * blocks // n, 8)
    slots = n * seats
    ids = block_elem.transpose(0, 2, 1)
    weight = block_weight.transpose(0, 2, 1)
    vmem = pl.BlockSpec(memory_space=pltpu.VMEM)
    smem = pl.BlockSpec(memory_space=pltpu.SMEM)
    stages = 2 * FINE_STEPS
    return pl.pallas_call(
        functools.partial(body, (mx, my, mz, seats, elem_count)),
        out_shape=(
            jax.ShapeDtypeStruct(states.shape, f32),
            jax.ShapeDtypeStruct((3, nx, ny, nz), f32),
            jax.ShapeDtypeStruct((3, node_count), f32),
        ),
        in_specs=[vmem, smem, smem, smem, vmem] + [smem] * 6 + [vmem] * 5 + [smem],
        out_specs=(vmem, vmem, vmem),
        scratch_shapes=[
            pltpu.VMEM((nx, ny, nz), f32),
            pltpu.VMEM((3, nx, ny, nz), f32),
            pltpu.VMEM((stages, 2, nx, 1, nz), f32),
            pltpu.VMEM((stages, 2, 1, nx * ny), f32),
            pltpu.VMEM((stages, 2, ny, nz), f32),
            pltpu.VMEM((stages, 2, nx, 1, nz), f32),
            pltpu.VMEM((stages, 2, 1, nx * ny), f32),
            pltpu.VMEM((8, node_count, elem_count), bf16),
            pltpu.VMEM((3, 8, elem_count), f32),
            pltpu.VMEM((blocks, slots), bf16),
            pltpu.VMEM((slots, elem_count), bf16),
            pltpu.VMEM((n, blocks), bf16),
            pltpu.VMEM((blocks, LANES), bf16),
            pltpu.VMEM((n, 1, LANES), f32),
            pltpu.VMEM((n, 1, LANES), f32),
            pltpu.VMEM((n, 1, LANES), f32),
            pltpu.VMEM((n, 1, LANES), f32),
            pltpu.VMEM((n, seats, LANES), f32),
            pltpu.VMEM((n, seats, LANES), f32),
            pltpu.SemaphoreType.DMA((stages, 6)),
            pltpu.SemaphoreType.DMA((stages, 6)),
            pltpu.SemaphoreType.DMA((3, n)),
            pltpu.SemaphoreType.DMA((3, n)),
        ],
        compiler_params=pltpu.CompilerParams(
            collective_id=0, has_side_effects=True, vmem_limit_bytes=20 * 1024 * 1024
        ),
        name="step",
    )(*(pltpu.with_memory_space_constraint(a, pltpu.HBM) for a in (
        states,
        active.transpose(1, 2, 0),
        fibre_index.transpose(1, 2, 0),
        fibre_angle,
        fibre_angle,
        conduct,
        gate_half,
        gate_slope,
        gate_tau,
        conductance,
        reversal,
        ids,
        weight,
        node_disp,
        elem_node,
        elem_fibre.reshape(1, elem_count),
        material,
    )))


def solution(mesh):
    in_specs = (
        P(None, "gx", "gy", "gz"),
        P("gx", "gy", "gz"),
        P("gx", "gy", "gz"),
        P(),
        P(),
        P(),
        P(),
        P(),
        P(),
        P(),
        P("gx", "gy", "gz"),
        P("gx", "gy", "gz"),
        P(None, ("gx", "gy", "gz")),
        P(None, ("gx", "gy", "gz")),
        P(("gx", "gy", "gz")),
        P(),
    )
    out_specs = (P(None, "gx", "gy", "gz"), P(None, "gx", "gy", "gz"), P(None, ("gx", "gy", "gz")))
    return jax.shard_map(shards, mesh=mesh, in_specs=in_specs, out_specs=out_specs, check_vma=False)
```

```python
import functools

import jax
import jax.numpy as jnp
from jax import lax
from jax.experimental import pallas as pl
from jax.experimental.pallas import tpu as pltpu
from jax.sharding import PartitionSpec as P

NSTATE = 19
TLX = 8
SBX = 2
SBY = 2
SBZ = 32
FINE_STEPS = 2
AXES = ("gx", "gy", "gz")
MESH = pl.DeviceIdType.MESH
LANES = 128
SUB = 8
GROUPS = 4
CORNERS = 8
f32 = jnp.float32
bf16 = jnp.bfloat16
i32 = jnp.int32
calcium_keep = 0.9
tension_half = 0.09
NN = (((1,), (0,)), ((), ()))
NT = (((1,), (1,)), ((), ()))
DIRS = (
    [tuple(side if d == dim else 0 for d in range(3)) for dim in range(3) for side in (-1, 1)]
    + [(a, b, 0) for a in (-1, 1) for b in (-1, 1)]
    + [(a, 0, b) for a in (-1, 1) for b in (-1, 1)]
    + [(0, a, b) for a in (-1, 1) for b in (-1, 1)]
)
OPPOSITE = [DIRS.index(tuple(-c for c in d)) for d in DIRS]


def mm(a, b, dims=NN):
    return lax.dot_general(a, b, dims, preferred_element_type=f32)


def parts(x, count):
    out = []
    for _ in range(count):
        out.append(x.astype(bf16).astype(f32))
        x = x - out[-1]
    return out


def iota(shape, dim):
    return lax.broadcasted_iota(i32, shape, dim)


def onehot(mask):
    return jnp.where(mask, 1.0, 0.0).astype(bf16)


def pick_rows(rows, shape):
    index = iota(shape, 0)
    out = jnp.zeros(shape, f32)
    for i, row in rows.items():
        out = jnp.where(index == i, row, out)
    return out


def lane_gather(x, index):
    return jnp.take_along_axis(x, index, axis=1, mode="promise_in_bounds")


def wide(row, rows=SUB):
    return jnp.broadcast_to(row, (rows, row.shape[1]))


def gather_wide(tables, index):
    low, high = index % LANES, index // LANES
    out = lane_gather(tables[0], low)
    for h in range(1, len(tables)):
        out = jnp.where(high == h, lane_gather(tables[h], low), out)
    return out


def lane_pieces(x):
    return [x[:, h : h + LANES] for h in range(0, x.shape[1], LANES)]


def sub_sum(x):
    return jnp.sum(x, axis=0, keepdims=True)


def body(
    sizes,
    states,
    active,
    fibre_index,
    angle_s,
    angle_v,
    conduct,
    gate_half,
    gate_slope,
    gate_tau,
    conductance,
    reversal,
    ids_ref,
    weight_ref,
    node_disp,
    elem_node,
    elem_fibre,
    material,
    out,
    fine_out,
    resid_out,
    held,
    vs,
    flux,
    gate_const,
    tile_const,
    mine_coef,
    send_y,
    send_z,
    send_xy,
    send_row,
    halo_x,
    halo_y,
    halo_z,
    edge_xy,
    edge_xz,
    edge_yz,
    halo_coef,
    turned,
    slot_pos,
    inverse,
    ids_send,
    ids_got,
    val_send,
    val_got,
    ans_send,
    ans_got,
    load_sem,
    face_send_sem,
    face_recv_sem,
    coef_send_sem,
    coef_recv_sem,
    all_send_sem,
    all_recv_sem,
):
    mx, my, mz, seats, nx, ny = sizes
    nz = states.shape[3]
    n = mx * my * mz
    gates_n = NSTATE - 2
    strips = nx * ny // SUB
    bx, by, bz = nx // SBX, ny // SBY, nz // SBZ
    plane = bx * by
    blocks = plane * bz
    tiles = nx // TLX
    node_count = node_disp.shape[1]
    elem_count = elem_node.shape[1]
    rows_each = seats // GROUPS
    slots = n * rows_each
    per_group = LANES // rows_each
    slot_groups = slots // LANES
    cx, cy, cz = (lax.axis_index(a) for a in AXES)
    me = (cx * my + cy) * mz + cz
    at = (cx, cy, cz)
    counts = (mx, my, mz)

    def others():
        steps = [
            (a, b, c) for a in range(mx) for b in range(my) for c in range(mz) if a or b or c
        ]

        def far(step):
            return sum(max(s, m - s) if s else 0 for s, m in zip(step, counts))

        return sorted(steps, key=far, reverse=True)

    wrapped = [[jnp.where(p + s >= m, p + s - m, p + s) for s in range(m)] for p, m in zip(at, counts)]

    def each_other(go):
        if n <= 64:
            for step in others():
                go(tuple(wrapped[d][s] for d, s in enumerate(step)))
        else:

            def one(k, carry):
                flat = (me + k) % n
                go((flat // (my * mz), (flat // mz) % my, flat % mz))
                return carry

            lax.fori_loop(1, n, one, 0)

    for ref in (halo_x, halo_y, halo_z, edge_xy, edge_xz, edge_yz, halo_coef):
        ref[...] = jnp.zeros(ref.shape, f32)

    barrier = pltpu.get_barrier_semaphore()
    each_other(
        lambda to: pl.semaphore_signal(barrier, inc=1, device_id=to, device_id_type=MESH)
    )

    chunk = TLX * ny // SUB // 2
    loads = [
        pltpu.make_async_copy(
            states.at[:, pl.ds(i * chunk, chunk)],
            held.at[:, pl.ds(i * chunk, chunk)],
            load_sem.at[i],
        )
        for i in range(strips // chunk)
    ]
    for load in loads:
        load.start()

    def splat(value):
        return jnp.full((SUB, LANES), value, f32)

    angles = jnp.concatenate(
        [angle_v[...], jnp.zeros((2, LANES - angle_v.shape[1]), f32)], 1
    ) if angle_v.shape[1] < LANES else angle_v[...]
    rows = {0: angles[0:1], 1: angles[1:2]}
    across, spread, alive = [], [], []
    for t in range(tiles):
        index = fibre_index[0, 0, t]
        rows[2 + t] = jnp.full((1, LANES), angle_s[0, index], f32)
        rows[2 + tiles + t] = jnp.full((1, LANES), angle_s[1, index], f32)
        across.append(jnp.full((1, LANES), conduct[1, index], f32))
        spread.append(jnp.full((1, LANES), conduct[0, index], f32) - across[t])
        alive.append(jnp.where(active[0, 0, t] > 0, 1.0, 0.0).astype(f32))
    stack = pick_rows(rows, (SUB, LANES))
    cosine, sine = jnp.cos(stack), jnp.sin(stack)

    def frame_of(a, b):
        ca, sa = cosine[a : a + 1], sine[a : a + 1]
        cb, sb = cosine[b : b + 1], sine[b : b + 1]
        return ca * cb, sa * cb, sb

    for t in range(tiles):
        fx, fy, fz = frame_of(2 + t, 2 + tiles + t)
        scale = alive[t] * 0.25
        entries = [
            across[t] + spread[t] * fx * fx,
            across[t] + spread[t] * fy * fy,
            across[t] + spread[t] * fz * fz,
            spread[t] * fx * fy,
            spread[t] * fx * fz,
            spread[t] * fy * fz,
        ]
        mine_coef[t * SUB : (t + 1) * SUB] = pick_rows(
            {k: e * scale for k, e in enumerate(entries)}, (SUB, LANES)
        )

    for g in range(gates_n):
        slope = 0.5 / splat(gate_slope[g])
        gate_const[g, 0] = slope
        gate_const[g, 1] = slope * gate_half[g]
        keep = jnp.exp(-1.0 / splat(gate_tau[g]))
        share = 0.5 * (1.0 - keep)
        cond = splat(conductance[g])
        for t in range(tiles):
            live = splat(alive[t]) > 0.5
            tile_const[t, g, 0] = jnp.where(live, keep, 1.0)
            tile_const[t, g, 1] = jnp.where(live, share, 0.0)
            tile_const[t, g, 2] = jnp.where(live, cond, 0.0)
            tile_const[t, g, 3] = jnp.where(live, cond * reversal[g], 0.0)

    def live_calcium(t):
        live = splat(alive[t]) > 0.5
        keep = jnp.where(live, calcium_keep, 1.0)
        share = jnp.where(live, 0.5 * (1.0 - calcium_keep), 0.0)
        return keep, share

    def calcium_of(old, volt, t):
        keep, share = live_calcium(t)
        return old * keep + (jnp.tanh(4.0 * volt - 2.0) * share + share)

    def ionic(source, stage, i, t):
        where = pl.ds(i * chunk, chunk)
        volt = source[0, where]
        total = jnp.zeros_like(volt)
        shift = jnp.zeros_like(volt)
        for g in range(gates_n):
            bend = jnp.tanh(volt * gate_const[g, 0] - gate_const[g, 1])
            share = tile_const[t, g, 1]
            gate = source[1 + g, where] * tile_const[t, g, 0] + (bend * share + share)
            out[1 + g, where] = gate
            total = total + gate * tile_const[t, g, 2]
            shift = shift + gate * tile_const[t, g, 3]
        star = volt - (volt * total - shift)
        vs[stage, pl.ds(i * chunk * SUB, chunk * SUB)] = star.reshape(chunk * SUB, LANES)

    flat_in = (bx * bz, by)
    raw = jnp.concatenate(
        parts(ids_ref[...].astype(f32).reshape(flat_in), 3), 0
    ).astype(bf16)
    lane_b = iota((by, blocks), 1)
    put = onehot(lane_b % by == iota((by, blocks), 0))
    spread_ids = mm(raw, put)
    part = bx * bz
    spread_ids = spread_ids[:part] + spread_ids[part : 2 * part] + spread_ids[2 * part :]
    row_b, col_b = iota((part, blocks), 0), iota((part, blocks), 1)
    here = (row_b // bz == (col_b % plane) // by) & (row_b % bz == col_b // plane)
    ids = sub_sum(jnp.where(here, spread_ids, 0.0)).astype(i32)
    shift = elem_count.bit_length() - 1
    owner = lax.shift_right_logical(ids, shift)
    local = ids - owner * elem_count
    owned = onehot(owner == iota((n, blocks), 0))
    before = onehot(iota((blocks, blocks), 0) < iota((blocks, blocks), 1))
    seen = mm(owned, before)
    rank = sub_sum(owned.astype(f32) * seen).astype(i32)
    group, seat_row = rank % GROUPS, rank // GROUPS
    offset = (me % per_group) * rows_each
    hit = iota((n * GROUPS, blocks), 0) == owner * GROUPS + group
    place = onehot(iota((LANES, blocks), 0) == seat_row + offset)
    sent = jnp.concatenate(
        [
            jnp.where(hit, (local + 1).astype(f32), 0.0),
            jnp.where(hit, (iota((1, blocks), 1) + 1).astype(f32), 0.0),
        ],
        0,
    ).astype(bf16)
    sent = mm(sent, place, NT)
    ids_send[...] = sent[: n * GROUPS].reshape(n, GROUPS, LANES)
    block_at = sent[n * GROUPS :].astype(i32) - 1
    in_plane = block_at % plane
    slot_pos[...] = jnp.where(
        block_at >= 0,
        (block_at // plane // 2) * LANES
        + (in_plane // by) * ny
        + (in_plane % by) * SBY
        + (block_at // plane) % 2,
        -1,
    )
    back_row = owner * rows_each + seat_row

    raw = jnp.concatenate(parts(weight_ref[...].reshape(flat_in), 2), 0).astype(bf16)
    put = onehot(iota((by, bx * ny), 1) % ny == iota((by, bx * ny), 0) * SBY)
    spread_w = mm(raw, put)
    spread_w = (spread_w[:part] + spread_w[part:]).reshape(bx, bz, bx * ny)
    here = iota((bx, bz, bx * ny), 0) == iota((bx, bz, bx * ny), 2) // ny
    weights = jnp.sum(jnp.where(here, spread_w, 0.0), axis=0)
    weights = jnp.concatenate([weights, jnp.zeros((SUB - bz, bx * ny), f32)], 0)
    weights = weights * (1.0 / (SBX * SBY * SBZ))

    for i, load in enumerate(loads):
        load.wait()
    for t in range(tiles):

        def first(i, carry, t=t):
            ionic(held, 0, i, t)
            here = pl.ds(i * chunk, chunk)
            out[NSTATE - 1, here] = calcium_of(held[NSTATE - 1, here], held[0, here], t)
            return carry

        lax.fori_loop(2 * t, 2 * t + 2, first, 0)

    def source_of(stage, i):
        d = DIRS[i]
        if i < 2:
            return vs.at[stage, pl.ds(0 if d[0] < 0 else (nx - 2) * ny, 2 * ny)]
        if i < 4:
            return send_y.at[stage, i - 2]
        if i < 6:
            return send_z.at[stage, i - 4]
        if i < 10:
            return send_xy.at[stage, i - 6]
        return send_row.at[stage, 0 if d[2] < 0 else 1]

    def target_of(stage, i):
        if i < 2:
            return halo_x.at[stage, i]
        if i < 4:
            return halo_y.at[stage, i - 2]
        if i < 6:
            return halo_z.at[stage, i - 4]
        if i < 10:
            return edge_xy.at[stage, i - 6]
        if i < 14:
            return edge_xz.at[stage, i - 10]
        return edge_yz.at[stage, i - 14]

    def exists(i):
        ok = None
        for p, step, m in zip(at, DIRS[i], counts):
            if step:
                inside = p > 0 if step < 0 else p < m - 1
                ok = inside if ok is None else ok & inside
        return ok

    def device(i):
        return tuple(p + step for p, step in zip(at, DIRS[i]))

    order = list(range(len(DIRS) - 1, -1, -1))

    def prepare(stage):
        for side in range(2):
            for layer in range(2):
                y = layer if side == 0 else ny - 2 + layer
                send_y[stage, side, layer] = vs[stage, pl.ds(y, nx, stride=ny), :]
        for a in range(2):
            for b in range(2):
                row = (nx - 1) * a * ny + (ny - 1) * b
                send_xy[stage, 2 * a + b] = vs[stage, row : row + 1, :]
        columns = jnp.transpose(vs[stage])
        send_z[stage, 0] = columns[0:2]
        send_z[stage, 1] = columns[nz - 2 : nz]
        send_row[stage, 0] = columns[0:1]
        send_row[stage, 1] = columns[nz - 1 : nz]

    def send(stage):
        for i in order:

            @pl.when(exists(i))
            def _(i=i):
                pltpu.make_async_remote_copy(
                    src_ref=source_of(stage, i),
                    dst_ref=target_of(stage, OPPOSITE[i]),
                    send_sem=face_send_sem.at[stage, i],
                    recv_sem=face_recv_sem.at[stage, OPPOSITE[i]],
                    device_id=device(i),
                    device_id_type=MESH,
                ).start()

    def receive(stage):
        for i in range(len(DIRS)):

            @pl.when(exists(i))
            def _(i=i):
                pltpu.make_async_remote_copy(
                    src_ref=source_of(stage, i),
                    dst_ref=target_of(stage, i),
                    send_sem=face_send_sem.at[stage, i],
                    recv_sem=face_recv_sem.at[stage, i],
                    device_id=device(i),
                    device_id_type=MESH,
                ).wait()

    def coef_copy(i, landed):
        return pltpu.make_async_remote_copy(
            src_ref=mine_coef,
            dst_ref=halo_coef.at[landed],
            send_sem=coef_send_sem.at[i],
            recv_sem=coef_recv_sem.at[landed],
            device_id=device(i),
            device_id_type=MESH,
        )

    def all_start(kind, src, dst):
        dst[pl.ds(me, 1)] = src[pl.ds(me, 1)]

        def go(to):
            flat = (to[0] * my + to[1]) * mz + to[2]
            pltpu.make_async_remote_copy(
                src_ref=src.at[flat],
                dst_ref=dst.at[me],
                send_sem=all_send_sem.at[kind],
                recv_sem=all_recv_sem.at[kind],
                device_id=to,
                device_id_type=MESH,
            ).start()

        each_other(go)

    def all_wait(kind, src, dst):
        pltpu.make_async_remote_copy(
            src_ref=src.at[pl.ds(0, n - 1)],
            dst_ref=dst.at[pl.ds(0, n - 1)],
            send_sem=all_send_sem.at[kind],
            recv_sem=all_recv_sem.at[kind],
            device_id=at,
            device_id_type=MESH,
        ).wait()

    def coef_row(ref, t, k):
        return ref[t * SUB + k : t * SUB + k + 1, :]

    def diffuse(stage):
        v = vs[stage].reshape(nx, ny, nz)
        lane = iota((1, nz), 1)
        flat = nx * ny
        lane_f = iota((SUB, flat), 1)

        def both(low, high):
            return pick_rows({0: low, 1: high}, (SUB, flat))

        near = both(halo_z[stage, 0, 1:2], halo_z[stage, 1, 0:1])
        gz = both(
            send_row[stage, 0] - halo_z[stage, 0, 0:1],
            halo_z[stage, 1, 1:2] - send_row[stage, 1],
        )
        xz = [both(edge_xz[stage, 2 * a], edge_xz[stage, 2 * a + 1]) for a in range(2)]
        yz = [both(edge_yz[stage, 2 * a], edge_yz[stage, 2 * a + 1]) for a in range(2)]
        up = pltpu.roll(jnp.where(lane_f < ny, xz[1], near), flat - ny, 1)
        down = pltpu.roll(jnp.where(lane_f >= flat - ny, xz[0], near), ny, 1)
        gx = up - down
        up = jnp.where(
            lane_f % ny == ny - 1, pltpu.roll(yz[1], ny - 1, 1), pltpu.roll(near, flat - 1, 1)
        )
        down = jnp.where(
            lane_f % ny == 0, pltpu.roll(yz[0], flat - ny + 1, 1), pltpu.roll(near, 1, 1)
        )
        gy = up - down

        def coef_z(k):
            return both(
                *(
                    jnp.concatenate(
                        [coef_row(halo_coef.at[4 + s], t, k) for t in range(tiles)], 1
                    )
                    for s in range(2)
                )
            )

        fz = coef_z(4) * gx + coef_z(5) * gy + coef_z(2) * gz
        blank = jnp.zeros((SUB, flat), f32)
        half = nz // 2
        pieces = [blank] * (nz // SUB)
        pieces[0] = pick_rows(
            {0: near[0:1], **{1 + i: edge_xz[stage, i] for i in range(4)}}, (SUB, flat)
        )
        pieces[half // SUB - 1] = pick_rows({SUB - 1: fz[1:2]}, (SUB, flat))
        pieces[half // SUB] = pick_rows(
            {0: fz[0:1], **{1 + i: edge_yz[stage, i] for i in range(4)}}, (SUB, flat)
        )
        pieces[-1] = pick_rows({SUB - 1: near[1:2]}, (SUB, flat))
        turned[...] = jnp.transpose(jnp.concatenate(pieces, 0))

        def along_z(a, low, high):
            return jnp.where(lane == nz - 1, high, pltpu.roll(a, nz - 1, 1)) - jnp.where(
                lane == 0, low, pltpu.roll(a, 1, 1)
            )

        def along_rows(a, low, high):
            row = iota(a.shape, 0)
            m = a.shape[0]
            return jnp.where(row == m - 1, high, pltpu.roll(a, m - 1, 0)) - jnp.where(
                row == 0, low, pltpu.roll(a, 1, 0)
            )

        px, fx_out = [], []
        for s in range(2):
            close = halo_x[stage, s, ny:] if s == 0 else halo_x[stage, s, :ny]
            distant = halo_x[stage, s, :ny] if s == 0 else halo_x[stage, s, ny:]
            gx = v[0] - distant if s == 0 else distant - v[nx - 1]
            gy = along_rows(close, edge_xy[stage, 2 * s], edge_xy[stage, 2 * s + 1])
            first = (nx - 1) * ny if s == 0 else 0
            edge = turned[first : first + ny, :]
            c = 1 + 2 * s
            gz = along_z(close, edge[:, c : c + 1], edge[:, c + 1 : c + 2])
            t = tiles - 1 if s == 0 else 0
            k = [coef_row(halo_coef.at[s], t, j) for j in (0, 3, 4)]
            px.append(close)
            fx_out.append(k[0] * gx + k[1] * gy + k[2] * gz)
        py, fy_out = [], []
        for s in range(2):
            close, distant = halo_y[stage, s, 1 - s], halo_y[stage, s, s]
            own = vs[stage, pl.ds(0 if s == 0 else ny - 1, nx, stride=ny), :]
            gy = own - distant if s == 0 else distant - own
            gx = along_rows(close, edge_xy[stage, s], edge_xy[stage, 2 + s])
            edge = turned[pl.ds(ny - 1 if s == 0 else 0, nx, stride=ny), :]
            c = half + 1 + 2 * s
            gz = along_z(close, edge[:, c : c + 1], edge[:, c + 1 : c + 2])

            def coef_y(j, s=s):
                return jnp.concatenate(
                    [wide(coef_row(halo_coef.at[2 + s], t, j), TLX) for t in range(tiles)], 0
                )

            py.append(close)
            fy_out.append(coef_y(3) * gx + coef_y(1) * gy + coef_y(5) * gz)

        def diff_x(a, low, high):
            return jnp.concatenate([a[1:], high[None]], 0) - jnp.concatenate([low[None], a[:-1]], 0)

        def diff_y(a, low, high):
            row = iota((1, ny, nz), 1)
            up = jnp.where(row == ny - 1, high.reshape(nx, 1, nz), pltpu.roll(a, ny - 1, 1))
            down = jnp.where(row == 0, low.reshape(nx, 1, nz), pltpu.roll(a, 1, 1))
            return up - down

        def diff_z(a, edge):
            lane = iota((1, 1, nz), 2)
            up = jnp.where(lane == nz - 1, edge, pltpu.roll(a, nz - 1, 2))
            down = jnp.where(lane == 0, edge, pltpu.roll(a, 1, 2))
            return up - down

        edges = turned[...].reshape(nx, ny, nz)
        gx, gy, gz = diff_x(v, *px), diff_y(v, *py), diff_z(v, edges)
        for t in range(tiles):
            span = slice(t * TLX, (t + 1) * TLX)
            xx, yy, zz, xy, xz_, yz_ = (
                coef_row(mine_coef, t, k).reshape(1, 1, LANES) for k in range(6)
            )
            a, b, c = gx[span], gy[span], gz[span]
            flux[0, span] = xx * a + xy * b + xz_ * c
            flux[1, span] = xy * a + yy * b + yz_ * c
            flux[2, span] = xz_ * a + yz_ * b + zz * c
        edges = pltpu.roll(edges, half, 2)
        lap = (
            diff_x(flux[0], *fx_out)
            + diff_y(flux[1], *fy_out)
            + diff_z(flux[2], edges)
        )
        for t in range(tiles):
            span = slice(t * TLX, (t + 1) * TLX)
            new = v[span] + lap[span] * alive[t]
            where = pl.ds(t * TLX * ny // SUB, TLX * ny // SUB)
            out[0, where] = new.reshape(TLX * ny // SUB, SUB, LANES)

    prepare(0)
    pl.semaphore_wait(barrier, n - 1)
    send(0)
    for i in range(6):

        @pl.when(exists(i))
        def _(i=i):
            coef_copy(i, OPPOSITE[i]).start()

    all_start(0, ids_send, ids_got)

    nodes = elem_node[...]
    disp = []
    for c in range(3):
        table = [
            wide(node_disp[c : c + 1, g : g + LANES]) for g in range(0, node_count, LANES)
        ]
        disp.append([gather_wide(table, ix) for ix in lane_pieces(nodes)])
    fx, fy, fz = frame_of(0, 1)
    table = [pick_rows({0: fx, 1: fy, 2: fz}, (SUB, LANES))]
    frame8 = [gather_wide(table, wide(ix)) for ix in lane_pieces(elem_fibre[...])]
    corner = iota((CORNERS, LANES), 0)
    signs = [
        jnp.where((corner // (4 >> j)) % 2 == 1, 0.25, -0.25) for j in range(3)
    ]
    shear, bulk, scale = material[0], material[1], material[2]
    passive, pulled = [], []
    for h in range(elem_count // LANES):
        frame = [frame8[h][i : i + 1] for i in range(3)]
        d = [
            [
                sub_sum(disp[i][h] * signs[j]) + (1.0 if i == j else 0.0)
                for j in range(3)
            ]
            for i in range(3)
        ]
        cof = [
            [
                d[(i + 1) % 3][(j + 1) % 3] * d[(i + 2) % 3][(j + 2) % 3]
                - d[(i + 1) % 3][(j + 2) % 3] * d[(i + 2) % 3][(j + 1) % 3]
                for j in range(3)
            ]
            for i in range(3)
        ]
        volume = d[0][0] * cof[0][0] + d[0][1] * cof[0][1] + d[0][2] * cof[0][2]
        reciprocal = 1.0 / volume
        logv = jnp.log(volume)
        stress = [
            [
                shear * (d[i][j] - cof[i][j] * reciprocal)
                + bulk * logv * (cof[i][j] * reciprocal)
                for j in range(3)
            ]
            for i in range(3)
        ]
        stretch = [
            scale * (d[i][0] * frame[0] + d[i][1] * frame[1] + d[i][2] * frame[2])
            for i in range(3)
        ]
        along = sum(wide(frame[j]) * signs[j] for j in range(3))
        passive.append([sum(wide(stress[i][j]) * signs[j] for j in range(3)) for i in range(3)])
        pulled.append([wide(stretch[i]) * along for i in range(3)])

    found = jnp.zeros((CORNERS, node_count), f32)
    lane_e = (iota((CORNERS, elem_count), 1) + 1).astype(f32)
    for q in range(CORNERS):
        named = onehot(iota((node_count, elem_count), 0) == nodes[q : q + 1, :])
        mine = jnp.where(iota((CORNERS, elem_count), 0) == q, lane_e, 0.0).astype(bf16)
        found = found + mm(mine, named, NT)
    inverse[...] = found.astype(i32) - 1

    receive(0)
    for i in range(6):

        @pl.when(exists(i))
        def _(i=i):
            coef_copy(i, i).wait()

    diffuse(0)

    pulls = []
    for t in range(tiles):
        where = pl.ds(t * TLX * ny // SUB, TLX * ny // SUB)
        calcium = calcium_of(out[NSTATE - 1, where], out[0, where], t)
        out[NSTATE - 1, where] = calcium
        square = calcium * calcium
        pulls.append(square / (square + tension_half))
    pull = jnp.concatenate(pulls, 0).reshape(bx, SBX, ny, nz)
    pull = (pull[:, 0] + pull[:, 1]).reshape(bx * ny, nz)
    strip = onehot(iota((SUB, nz), 1) // SBZ == iota((SUB, nz), 0))
    high = pull.astype(bf16)
    rest = (pull - high.astype(f32)).astype(bf16)
    pooled = mm(strip, high, NT) + mm(strip, rest, NT)
    lanes_p = bx * ny
    value = (pooled + pltpu.roll(pooled, lanes_p - 1, 1)) * weights
    even = iota((1, lanes_p), 1) % 2 == 0
    odd_value = pltpu.roll(value, 1, 1)
    tables = [
        wide(jnp.where(even, value[b : b + 1], odd_value[b + 1 : b + 2]))
        for b in range(0, bz, 2)
    ]
    for r in range(0, n * GROUPS, SUB):
        where = slot_pos[r : r + SUB]
        picked = jnp.where(where >= 0, gather_wide(tables, jnp.maximum(where, 0)), 0.0)
        val_send[r // GROUPS : (r + SUB) // GROUPS] = picked.reshape(
            SUB // GROUPS, GROUPS, LANES
        )
    all_start(1, val_send, val_got)

    def second(t):
        def go(i, carry):
            ionic(out, 1, i, t)
            return carry

        lax.fori_loop(2 * t, 2 * t + 2, go, 0)

    second(0)

    all_wait(0, ids_send, ids_got)
    asked = []
    for g in range(slot_groups):
        total = ids_got[g * per_group]
        for m in range(1, per_group):
            total = total + ids_got[g * per_group + m]
        asked.append(total)
        index = jnp.maximum(total.astype(i32) - 1, 0)
        rows_out = []
        for k in range(GROUPS):
            where = wide(index[k : k + 1])
            rows_out += [gather_wide(disp[c], where) for c in range(3)]
            rows_out.append(jnp.zeros((SUB, LANES), f32))
        answer = jnp.transpose(jnp.concatenate(rows_out, 0))
        ans_send[g * per_group : (g + 1) * per_group] = answer.reshape(
            per_group, rows_each, LANES
        )
    all_start(2, ans_send, ans_got)
    for t in range(1, tiles):
        second(t)
    prepare(1)
    send(1)

    code = jnp.zeros((LANES, elem_count), f32)
    for g in range(slot_groups):
        column = jnp.transpose(
            jnp.concatenate([asked[g], jnp.zeros((LANES - GROUPS, LANES), f32)], 0)
        )
        ident = (iota((LANES, elem_count), 1) + 1).astype(f32)
        row = iota((LANES, elem_count), 0).astype(f32)
        for k in range(GROUPS):
            code = jnp.where(
                column[:, k : k + 1] == ident, row + float((g * GROUPS + k) * LANES), code
            )
    slot_of = sub_sum(code).astype(i32)

    all_wait(2, ans_send, ans_got)
    columns = [
        jnp.transpose(
            ans_got[g * per_group : (g + 1) * per_group].reshape(LANES, LANES)
        )
        for g in range(slot_groups)
    ]
    span = 32
    halves = []
    for h in range(blocks // LANES):
        cut = slice(h * LANES, (h + 1) * LANES)
        where, which = wide(back_row[:, cut]), wide(group[:, cut])
        rows_in = []
        for c in range(3):
            value = None
            for k in range(GROUPS):
                first = k * span + c * SUB
                found = gather_wide([col[first : first + SUB] for col in columns], where)
                value = found if value is None else jnp.where(which == k, found, value)
            value = 0.75 * value + 0.25 * pltpu.roll(value, 4, 0)
            swapped = jnp.where(
                iota((SUB, LANES), 0) // 2 % 2 == 1,
                pltpu.roll(value, 2, 0),
                pltpu.roll(value, SUB - 2, 0),
            )
            rows_in.append(0.75 * value + 0.25 * swapped)
        rows_in.append(jnp.zeros((SUB, LANES), f32))
        halves.append(jnp.concatenate(rows_in, 0))
    stacked = []
    for b in range(bz):
        lane0 = b * plane
        piece = halves[lane0 // LANES]
        stacked.append(
            pltpu.roll(piece, LANES - lane0 % LANES, 1) if lane0 % LANES else piece
        )
    around = jnp.transpose(jnp.concatenate(stacked, 0))
    lane = iota((SUB, nz), 1)
    strip_lane = lane // SBZ * span
    xi = ((lane % SBZ).astype(f32) + 0.5) / SBZ
    for p in range(bx):
        near = around[p * by : (p + 1) * by]
        for c in range(3):
            for iv in range(SBX):
                for jv in range(SBY):
                    first = c * SUB + 4 * iv + 2 * jv
                    low = lane_gather(near, strip_lane + first)
                    high = lane_gather(near, strip_lane + first + 1)
                    fine_out[c, SBX * p + iv, pl.ds(jv, by, stride=SBY), :] = (
                        low + (high - low) * xi
                    )

    receive(1)
    diffuse(1)

    all_wait(1, val_send, val_got)
    tables = []
    for g in range(slot_groups):
        total = val_got[g * per_group]
        for m in range(1, per_group):
            total = total + val_got[g * per_group + m]
        tables += [wide(total[k : k + 1]) for k in range(GROUPS)]
    tension = [gather_wide(tables, wide(ix)) for ix in lane_pieces(slot_of)]
    force = [
        [passive[h][i] + tension[h] * pulled[h][i] for h in range(elem_count // LANES)]
        for i in range(3)
    ]
    for g in range(0, node_count, LANES):
        where = inverse[:, g : g + LANES]
        index = jnp.maximum(where, 0)
        for i in range(3):
            got = jnp.where(where >= 0, gather_wide(force[i], index), 0.0)
            resid_out[i : i + 1, g : g + LANES] = sub_sum(got)


def write_out(*refs):
    count = (len(refs) - 1) // 2
    sems = refs[-1]
    copies = [
        pltpu.make_async_copy(refs[i], refs[count + i], sems.at[i]) for i in range(count)
    ]
    for c in copies:
        c.start()
    for c in copies:
        c.wait()


def shards(
    states,
    active,
    fibre_index,
    fibre_angle,
    conduct,
    gate_half,
    gate_slope,
    gate_tau,
    conductance,
    reversal,
    block_elem,
    block_weight,
    node_disp,
    elem_node,
    elem_fibre,
    material,
):
    mx, my, mz = (lax.axis_size(a) for a in AXES)
    n = mx * my * mz
    elem_count = elem_node.shape[1]
    node_count = node_disp.shape[1]
    nx, ny, nz = states.shape[1:]
    bx, by, bz = block_elem.shape
    blocks = bx * by * bz
    seats = max(2 * blocks // n, 8)
    rows_each = seats // GROUPS
    tiles = nx // TLX
    strips = nx * ny // SUB
    ids = block_elem.transpose(0, 2, 1)
    weight = block_weight.transpose(0, 2, 1)
    vmem = pl.BlockSpec(memory_space=pltpu.VMEM)
    smem = pl.BlockSpec(memory_space=pltpu.SMEM)
    hbm = pl.BlockSpec(memory_space=pltpu.HBM)
    gates_n = NSTATE - 2
    ways = len(DIRS)
    operands = (
        states.reshape(NSTATE, strips, SUB, nz),
        active.transpose(1, 2, 0),
        fibre_index.transpose(1, 2, 0),
        fibre_angle,
        fibre_angle,
        conduct,
        gate_half,
        gate_slope,
        gate_tau,
        conductance,
        reversal,
        ids,
        weight,
        node_disp,
        elem_node,
        elem_fibre.reshape(1, elem_count),
        material,
    )
    stage = FINE_STEPS
    shapes = (
        jax.ShapeDtypeStruct((NSTATE, strips, SUB, nz), f32),
        jax.ShapeDtypeStruct((3, nx, ny, nz), f32),
        jax.ShapeDtypeStruct((3, node_count), f32),
    )
    results = pl.pallas_call(
        functools.partial(body, (mx, my, mz, seats, nx, ny)),
        out_shape=shapes,
        in_specs=[hbm, smem, smem, smem, vmem] + [smem] * 6 + [vmem] * 5 + [smem],
        out_specs=(vmem, vmem, vmem),
        scratch_shapes=[
            pltpu.VMEM((NSTATE, strips, SUB, nz), f32),
            pltpu.VMEM((stage, nx * ny, nz), f32),
            pltpu.VMEM((3, nx, ny, nz), f32),
            pltpu.VMEM((gates_n, 2, SUB, LANES), f32),
            pltpu.VMEM((tiles, gates_n, 4, SUB, LANES), f32),
            pltpu.VMEM((tiles * SUB, LANES), f32),
            pltpu.VMEM((stage, 2, 2, nx, nz), f32),
            pltpu.VMEM((stage, 2, 2, nx * ny), f32),
            pltpu.VMEM((stage, 4, 1, nz), f32),
            pltpu.VMEM((stage, 2, 1, nx * ny), f32),
            pltpu.VMEM((stage, 2, 2 * ny, nz), f32),
            pltpu.VMEM((stage, 2, 2, nx, nz), f32),
            pltpu.VMEM((stage, 2, 2, nx * ny), f32),
            pltpu.VMEM((stage, 4, 1, nz), f32),
            pltpu.VMEM((stage, 4, 1, nx * ny), f32),
            pltpu.VMEM((stage, 4, 1, nx * ny), f32),
            pltpu.VMEM((6, tiles * SUB, LANES), f32),
            pltpu.VMEM((nx * ny, nz), f32),
            pltpu.VMEM((n * GROUPS, LANES), i32),
            pltpu.VMEM((CORNERS, node_count), i32),
            pltpu.VMEM((n, GROUPS, LANES), f32),
            pltpu.VMEM((n, GROUPS, LANES), f32),
            pltpu.VMEM((n, GROUPS, LANES), f32),
            pltpu.VMEM((n, GROUPS, LANES), f32),
            pltpu.VMEM((n, rows_each, LANES), f32),
            pltpu.VMEM((n, rows_each, LANES), f32),
            pltpu.SemaphoreType.DMA((2 * tiles,)),
            pltpu.SemaphoreType.DMA((stage, ways)),
            pltpu.SemaphoreType.DMA((stage, ways)),
            pltpu.SemaphoreType.DMA((6,)),
            pltpu.SemaphoreType.DMA((6,)),
            pltpu.SemaphoreType.DMA((3,)),
            pltpu.SemaphoreType.DMA((3,)),
        ],
        compiler_params=pltpu.CompilerParams(
            collective_id=0, has_side_effects=True, vmem_limit_bytes=20 * 1024 * 1024
        ),
        name="step",
    )(*(pltpu.with_memory_space_constraint(a, pltpu.HBM) for a in operands))
    results = pl.pallas_call(
        write_out,
        out_shape=shapes,
        in_specs=[vmem] * 3,
        out_specs=(hbm,) * 3,
        scratch_shapes=[pltpu.SemaphoreType.DMA((3,))],
        compiler_params=pltpu.CompilerParams(vmem_limit_bytes=20 * 1024 * 1024),
        name="write",
    )(*results)
    return results[0].reshape(states.shape), results[1], results[2]


def solution(mesh):
    in_specs = (
        P(None, "gx", "gy", "gz"),
        P("gx", "gy", "gz"),
        P("gx", "gy", "gz"),
        P(),
        P(),
        P(),
        P(),
        P(),
        P(),
        P(),
        P("gx", "gy", "gz"),
        P("gx", "gy", "gz"),
        P(None, ("gx", "gy", "gz")),
        P(None, ("gx", "gy", "gz")),
        P(("gx", "gy", "gz")),
        P(),
    )
    out_specs = (P(None, "gx", "gy", "gz"), P(None, "gx", "gy", "gz"), P(None, ("gx", "gy", "gz")))
    return jax.shard_map(shards, mesh=mesh, in_specs=in_specs, out_specs=out_specs, check_vma=False)
```

```python
import functools

import jax
import jax.numpy as jnp
from jax import lax
from jax.experimental import pallas as pl
from jax.experimental.pallas import tpu as pltpu
from jax.sharding import PartitionSpec as P

NSTATE = 19
TLX = 8
SBX = 2
SBY = 2
SBZ = 32
FINE_STEPS = 2
AXES = ("gx", "gy", "gz")
MESH = pl.DeviceIdType.MESH
LANES = 128
SUB = 8
GROUPS = 4
CORNERS = 8
PIECES = 4
f32 = jnp.float32
bf16 = jnp.bfloat16
i32 = jnp.int32
calcium_keep = 0.9
tension_half = 0.09
NN = (((1,), (0,)), ((), ()))
NT = (((1,), (1,)), ((), ()))
DIRS = (
    [tuple(side if d == dim else 0 for d in range(3)) for dim in range(3) for side in (-1, 1)]
    + [(a, b, 0) for a in (-1, 1) for b in (-1, 1)]
    + [(a, 0, b) for a in (-1, 1) for b in (-1, 1)]
    + [(0, a, b) for a in (-1, 1) for b in (-1, 1)]
)
OPPOSITE = [DIRS.index(tuple(-c for c in d)) for d in DIRS]


def mm(a, b, dims=NN):
    return lax.dot_general(a, b, dims, preferred_element_type=f32)


def parts(x, count):
    out = []
    for _ in range(count):
        out.append(x.astype(bf16).astype(f32))
        x = x - out[-1]
    return out


def iota(shape, dim):
    return lax.broadcasted_iota(i32, shape, dim)


def onehot(mask):
    return jnp.where(mask, 1.0, 0.0).astype(bf16)


def pick_rows(rows, shape):
    index = iota(shape, 0)
    out = jnp.zeros(shape, f32)
    for i, row in rows.items():
        out = jnp.where(index == i, row, out)
    return out


def lane_gather(x, index):
    return jnp.take_along_axis(x, index, axis=1, mode="promise_in_bounds")


def wide(row, rows=SUB):
    return jnp.broadcast_to(row, (rows, row.shape[1]))


def gather_wide(tables, index):
    low, high = index % LANES, index // LANES
    out = lane_gather(tables[0], low)
    for h in range(1, len(tables)):
        out = jnp.where(high == h, lane_gather(tables[h], low), out)
    return out


def lane_pieces(x):
    return [x[:, h : h + LANES] for h in range(0, x.shape[1], LANES)]


def sub_sum(x):
    return jnp.sum(x, axis=0, keepdims=True)


def body(
    sizes,
    *refs,
):
    mx, my, mz, seats, nx, ny = sizes
    operands, refs = refs[:17], refs[17:]
    states = operands[0]
    out, resid_out, answers_out, wanted_out = refs[:4]
    small, refs = refs[4:20], refs[20:]
    (
        active,
        fibre_index,
        angle_s,
        angle_v,
        conduct,
        gate_half,
        gate_slope,
        gate_tau,
        conductance,
        reversal,
        ids_ref,
        weight_ref,
        node_disp,
        elem_node,
        elem_fibre,
        material,
    ) = small
    (
        held,
        vs,
        flux,
        gate_const,
        tile_const,
        mine_coef,
        send_y,
        send_z,
        send_xy,
        send_row,
        halo_x,
        halo_y,
        halo_z,
        edge_xy,
        edge_xz,
        edge_yz,
        halo_coef,
        turned,
        slot_pos,
        inverse,
        ids_send,
        ids_got,
        val_send,
        val_got,
        ans_send,
        ans_got,
        load_sem,
        small_sem,
        face_send_sem,
        face_recv_sem,
        coef_send_sem,
        coef_recv_sem,
        all_send_sem,
        all_recv_sem,
    ) = refs
    nz = states.shape[3]
    n = mx * my * mz
    gates_n = NSTATE - 2
    strips = nx * ny // SUB
    bx, by, bz = nx // SBX, ny // SBY, nz // SBZ
    plane = bx * by
    blocks = plane * bz
    tiles = nx // TLX
    node_count = node_disp.shape[1]
    elem_count = elem_node.shape[1]
    rows_each = seats // GROUPS
    slots = n * rows_each
    per_group = LANES // rows_each
    slot_groups = slots // LANES
    cx, cy, cz = (lax.axis_index(a) for a in AXES)
    me = (cx * my + cy) * mz + cz
    at = (cx, cy, cz)
    counts = (mx, my, mz)

    def others():
        steps = [
            (a, b, c) for a in range(mx) for b in range(my) for c in range(mz) if a or b or c
        ]

        def far(step):
            return sum(max(s, m - s) if s else 0 for s, m in zip(step, counts))

        return sorted(steps, key=far, reverse=True)

    wrapped = [[jnp.where(p + s >= m, p + s - m, p + s) for s in range(m)] for p, m in zip(at, counts)]

    def each_other(go):
        if n <= 64:
            for step in others():
                go(tuple(wrapped[d][s] for d, s in enumerate(step)))
        else:

            def one(k, carry):
                flat = (me + k) % n
                go((flat // (my * mz), (flat // mz) % my, flat % mz))
                return carry

            lax.fori_loop(1, n, one, 0)

    chunk = TLX * ny // SUB // 2

    def load(i):
        here = pl.ds(i * chunk, chunk)
        return pltpu.make_async_copy(states.at[:, here], held.at[:, here], load_sem.at[i])

    small_loads = [
        pltpu.make_async_copy(src, dst, small_sem.at[i])
        for i, (src, dst) in enumerate(zip(operands[1:], small))
    ]
    for c in small_loads:
        c.start()
    for i in range(strips // chunk):
        load(i).start()

    for ref in (halo_x, halo_y, halo_z, edge_xy, edge_xz, edge_yz, halo_coef):
        ref[...] = jnp.zeros(ref.shape, f32)

    barrier = pltpu.get_barrier_semaphore()
    each_other(
        lambda to: pl.semaphore_signal(barrier, inc=1, device_id=to, device_id_type=MESH)
    )

    for c in small_loads:
        c.wait()

    def splat(value):
        return jnp.full((SUB, LANES), value, f32)

    angles = jnp.concatenate(
        [angle_v[...], jnp.zeros((2, LANES - angle_v.shape[1]), f32)], 1
    ) if angle_v.shape[1] < LANES else angle_v[...]
    rows = {0: angles[0:1], 1: angles[1:2]}
    across, spread, alive = [], [], []
    for t in range(tiles):
        index = fibre_index[0, 0, t]
        rows[2 + t] = jnp.full((1, LANES), angle_s[0, index], f32)
        rows[2 + tiles + t] = jnp.full((1, LANES), angle_s[1, index], f32)
        across.append(jnp.full((1, LANES), conduct[1, index], f32))
        spread.append(jnp.full((1, LANES), conduct[0, index], f32) - across[t])
        alive.append(jnp.where(active[0, 0, t] > 0, 1.0, 0.0).astype(f32))
    stack = pick_rows(rows, (SUB, LANES))
    cosine, sine = jnp.cos(stack), jnp.sin(stack)

    def frame_of(a, b):
        ca, sa = cosine[a : a + 1], sine[a : a + 1]
        cb, sb = cosine[b : b + 1], sine[b : b + 1]
        return ca * cb, sa * cb, sb

    for t in range(tiles):
        fx, fy, fz = frame_of(2 + t, 2 + tiles + t)
        scale = alive[t] * 0.25
        entries = [
            across[t] + spread[t] * fx * fx,
            across[t] + spread[t] * fy * fy,
            across[t] + spread[t] * fz * fz,
            spread[t] * fx * fy,
            spread[t] * fx * fz,
            spread[t] * fy * fz,
        ]
        mine_coef[t * SUB : (t + 1) * SUB] = pick_rows(
            {k: e * scale for k, e in enumerate(entries)}, (SUB, LANES)
        )

    for g in range(gates_n):
        slope = 0.5 / splat(gate_slope[g])
        gate_const[g, 0] = slope
        gate_const[g, 1] = slope * gate_half[g]
        keep = jnp.exp(-1.0 / splat(gate_tau[g]))
        share = 0.5 * (1.0 - keep)
        cond = splat(conductance[g])
        for t in range(tiles):
            live = splat(alive[t]) > 0.5
            tile_const[t, g, 0] = jnp.where(live, keep, 1.0)
            tile_const[t, g, 1] = jnp.where(live, share, 0.0)
            tile_const[t, g, 2] = jnp.where(live, cond, 0.0)
            tile_const[t, g, 3] = jnp.where(live, cond * reversal[g], 0.0)

    def live_calcium(t):
        live = splat(alive[t]) > 0.5
        keep = jnp.where(live, calcium_keep, 1.0)
        share = jnp.where(live, 0.5 * (1.0 - calcium_keep), 0.0)
        return keep, share

    def calcium_of(old, volt, t):
        keep, share = live_calcium(t)
        return old * keep + (jnp.tanh(4.0 * volt - 2.0) * share + share)

    def ionic(source, stage, i, t):
        where = pl.ds(i * chunk, chunk)
        volt = source[0, where]
        total = jnp.zeros_like(volt)
        shift = jnp.zeros_like(volt)
        for g in range(gates_n):
            bend = jnp.tanh(volt * gate_const[g, 0] - gate_const[g, 1])
            share = tile_const[t, g, 1]
            gate = source[1 + g, where] * tile_const[t, g, 0] + (bend * share + share)
            out[1 + g, where] = gate
            total = total + gate * tile_const[t, g, 2]
            shift = shift + gate * tile_const[t, g, 3]
        star = volt - (volt * total - shift)
        vs[stage, pl.ds(i * chunk * SUB, chunk * SUB)] = star.reshape(chunk * SUB, LANES)

    flat_in = (bx * bz, by)
    raw = jnp.concatenate(
        parts(ids_ref[...].astype(f32).reshape(flat_in), 3), 0
    ).astype(bf16)
    lane_b = iota((by, blocks), 1)
    put = onehot(lane_b % by == iota((by, blocks), 0))
    spread_ids = mm(raw, put)
    part = bx * bz
    spread_ids = spread_ids[:part] + spread_ids[part : 2 * part] + spread_ids[2 * part :]
    row_b, col_b = iota((part, blocks), 0), iota((part, blocks), 1)
    here = (row_b // bz == (col_b % plane) // by) & (row_b % bz == col_b // plane)
    ids = sub_sum(jnp.where(here, spread_ids, 0.0)).astype(i32)
    shift = elem_count.bit_length() - 1
    owner = lax.shift_right_logical(ids, shift)
    local = ids - owner * elem_count
    owned = onehot(owner == iota((n, blocks), 0))
    before = onehot(iota((blocks, blocks), 0) < iota((blocks, blocks), 1))
    seen = mm(owned, before)
    rank = sub_sum(owned.astype(f32) * seen).astype(i32)
    group, seat_row = rank % GROUPS, rank // GROUPS
    offset = (me % per_group) * rows_each
    hit = iota((n * GROUPS, blocks), 0) == owner * GROUPS + group
    place = onehot(iota((LANES, blocks), 0) == seat_row + offset)
    sent = jnp.concatenate(
        [
            jnp.where(hit, (local + 1).astype(f32), 0.0),
            jnp.where(hit, (iota((1, blocks), 1) + 1).astype(f32), 0.0),
        ],
        0,
    ).astype(bf16)
    sent = mm(sent, place, NT)
    ids_send[...] = sent[: n * GROUPS].reshape(n, GROUPS, LANES)
    block_at = sent[n * GROUPS :].astype(i32) - 1
    in_plane = block_at % plane
    slot_pos[...] = jnp.where(
        block_at >= 0,
        (block_at // plane // 2) * LANES
        + (in_plane // by) * ny
        + (in_plane % by) * SBY
        + (block_at // plane) % 2,
        -1,
    )
    back_row = owner * rows_each + seat_row

    raw = jnp.concatenate(parts(weight_ref[...].reshape(flat_in), 2), 0).astype(bf16)
    put = onehot(iota((by, bx * ny), 1) % ny == iota((by, bx * ny), 0) * SBY)
    spread_w = mm(raw, put)
    spread_w = (spread_w[:part] + spread_w[part:]).reshape(bx, bz, bx * ny)
    here = iota((bx, bz, bx * ny), 0) == iota((bx, bz, bx * ny), 2) // ny
    weights = jnp.sum(jnp.where(here, spread_w, 0.0), axis=0)
    weights = jnp.concatenate([weights, jnp.zeros((SUB - bz, bx * ny), f32)], 0)
    weights = weights * (1.0 / (SBX * SBY * SBZ))

    for t in range(tiles):

        def first(i, carry, t=t):
            load(i).wait()
            ionic(held, 0, i, t)
            here = pl.ds(i * chunk, chunk)
            out[NSTATE - 1, here] = calcium_of(held[NSTATE - 1, here], held[0, here], t)
            return carry

        lax.fori_loop(2 * t, 2 * t + 2, first, 0)

    def source_of(stage, i):
        d = DIRS[i]
        if i < 2:
            return vs.at[stage, pl.ds(0 if d[0] < 0 else (nx - 2) * ny, 2 * ny)]
        if i < 4:
            return send_y.at[stage, i - 2]
        if i < 6:
            return send_z.at[stage, i - 4]
        if i < 10:
            return send_xy.at[stage, i - 6]
        return send_row.at[stage, 0 if d[2] < 0 else 1]

    def target_of(stage, i):
        if i < 2:
            return halo_x.at[stage, i]
        if i < 4:
            return halo_y.at[stage, i - 2]
        if i < 6:
            return halo_z.at[stage, i - 4]
        if i < 10:
            return edge_xy.at[stage, i - 6]
        if i < 14:
            return edge_xz.at[stage, i - 10]
        return edge_yz.at[stage, i - 14]

    def exists(i):
        ok = None
        for p, step, m in zip(at, DIRS[i], counts):
            if step:
                inside = p > 0 if step < 0 else p < m - 1
                ok = inside if ok is None else ok & inside
        return ok

    def device(i):
        return tuple(p + step for p, step in zip(at, DIRS[i]))

    order = list(range(len(DIRS) - 1, -1, -1))

    def prepare(stage):
        for side in range(2):
            for layer in range(2):
                y = layer if side == 0 else ny - 2 + layer
                send_y[stage, side, layer] = vs[stage, pl.ds(y, nx, stride=ny), :]
        for a in range(2):
            for b in range(2):
                row = (nx - 1) * a * ny + (ny - 1) * b
                send_xy[stage, 2 * a + b] = vs[stage, row : row + 1, :]
        columns = jnp.transpose(vs[stage])
        send_z[stage, 0] = columns[0:2]
        send_z[stage, 1] = columns[nz - 2 : nz]
        send_row[stage, 0] = columns[0:1]
        send_row[stage, 1] = columns[nz - 1 : nz]

    def send(stage):
        for i in order:

            @pl.when(exists(i))
            def _(i=i):
                pltpu.make_async_remote_copy(
                    src_ref=source_of(stage, i),
                    dst_ref=target_of(stage, OPPOSITE[i]),
                    send_sem=face_send_sem.at[stage, i],
                    recv_sem=face_recv_sem.at[stage, OPPOSITE[i]],
                    device_id=device(i),
                    device_id_type=MESH,
                ).start()

    def receive(stage):
        for i in range(len(DIRS)):

            @pl.when(exists(i))
            def _(i=i):
                pltpu.make_async_remote_copy(
                    src_ref=source_of(stage, i),
                    dst_ref=target_of(stage, i),
                    send_sem=face_send_sem.at[stage, i],
                    recv_sem=face_recv_sem.at[stage, i],
                    device_id=device(i),
                    device_id_type=MESH,
                ).wait()

    def coef_copy(i, landed):
        return pltpu.make_async_remote_copy(
            src_ref=mine_coef,
            dst_ref=halo_coef.at[landed],
            send_sem=coef_send_sem.at[i],
            recv_sem=coef_recv_sem.at[landed],
            device_id=device(i),
            device_id_type=MESH,
        )

    def all_start(kind, src, dst):
        dst[pl.ds(me, 1)] = src[pl.ds(me, 1)]

        def go(to):
            flat = (to[0] * my + to[1]) * mz + to[2]
            pltpu.make_async_remote_copy(
                src_ref=src.at[flat],
                dst_ref=dst.at[me],
                send_sem=all_send_sem.at[kind],
                recv_sem=all_recv_sem.at[kind],
                device_id=to,
                device_id_type=MESH,
            ).start()

        each_other(go)

    def all_wait(kind, src, dst):
        pltpu.make_async_remote_copy(
            src_ref=src.at[pl.ds(0, n - 1)],
            dst_ref=dst.at[pl.ds(0, n - 1)],
            send_sem=all_send_sem.at[kind],
            recv_sem=all_recv_sem.at[kind],
            device_id=at,
            device_id_type=MESH,
        ).wait()

    def coef_row(ref, t, k):
        return ref[t * SUB + k : t * SUB + k + 1, :]

    def diffuse(stage):
        v = vs[stage].reshape(nx, ny, nz)
        lane = iota((1, nz), 1)
        flat = nx * ny
        lane_f = iota((SUB, flat), 1)

        def both(low, high):
            return pick_rows({0: low, 1: high}, (SUB, flat))

        near = both(halo_z[stage, 0, 1:2], halo_z[stage, 1, 0:1])
        gz = both(
            send_row[stage, 0] - halo_z[stage, 0, 0:1],
            halo_z[stage, 1, 1:2] - send_row[stage, 1],
        )
        xz = [both(edge_xz[stage, 2 * a], edge_xz[stage, 2 * a + 1]) for a in range(2)]
        yz = [both(edge_yz[stage, 2 * a], edge_yz[stage, 2 * a + 1]) for a in range(2)]
        up = pltpu.roll(jnp.where(lane_f < ny, xz[1], near), flat - ny, 1)
        down = pltpu.roll(jnp.where(lane_f >= flat - ny, xz[0], near), ny, 1)
        gx = up - down
        up = jnp.where(
            lane_f % ny == ny - 1, pltpu.roll(yz[1], ny - 1, 1), pltpu.roll(near, flat - 1, 1)
        )
        down = jnp.where(
            lane_f % ny == 0, pltpu.roll(yz[0], flat - ny + 1, 1), pltpu.roll(near, 1, 1)
        )
        gy = up - down

        def coef_z(k):
            return both(
                *(
                    jnp.concatenate(
                        [coef_row(halo_coef.at[4 + s], t, k) for t in range(tiles)], 1
                    )
                    for s in range(2)
                )
            )

        fz = coef_z(4) * gx + coef_z(5) * gy + coef_z(2) * gz
        blank = jnp.zeros((SUB, flat), f32)
        half = nz // 2
        pieces = [blank] * (nz // SUB)
        pieces[0] = pick_rows(
            {0: near[0:1], **{1 + i: edge_xz[stage, i] for i in range(4)}}, (SUB, flat)
        )
        pieces[half // SUB - 1] = pick_rows({SUB - 1: fz[1:2]}, (SUB, flat))
        pieces[half // SUB] = pick_rows(
            {0: fz[0:1], **{1 + i: edge_yz[stage, i] for i in range(4)}}, (SUB, flat)
        )
        pieces[-1] = pick_rows({SUB - 1: near[1:2]}, (SUB, flat))
        turned[...] = jnp.transpose(jnp.concatenate(pieces, 0))

        def along_z(a, low, high):
            return jnp.where(lane == nz - 1, high, pltpu.roll(a, nz - 1, 1)) - jnp.where(
                lane == 0, low, pltpu.roll(a, 1, 1)
            )

        def along_rows(a, low, high):
            row = iota(a.shape, 0)
            m = a.shape[0]
            return jnp.where(row == m - 1, high, pltpu.roll(a, m - 1, 0)) - jnp.where(
                row == 0, low, pltpu.roll(a, 1, 0)
            )

        px, fx_out = [], []
        for s in range(2):
            close = halo_x[stage, s, ny:] if s == 0 else halo_x[stage, s, :ny]
            distant = halo_x[stage, s, :ny] if s == 0 else halo_x[stage, s, ny:]
            gx = v[0] - distant if s == 0 else distant - v[nx - 1]
            gy = along_rows(close, edge_xy[stage, 2 * s], edge_xy[stage, 2 * s + 1])
            first = (nx - 1) * ny if s == 0 else 0
            edge = turned[first : first + ny, :]
            c = 1 + 2 * s
            gz = along_z(close, edge[:, c : c + 1], edge[:, c + 1 : c + 2])
            t = tiles - 1 if s == 0 else 0
            k = [coef_row(halo_coef.at[s], t, j) for j in (0, 3, 4)]
            px.append(close)
            fx_out.append(k[0] * gx + k[1] * gy + k[2] * gz)
        py, fy_out = [], []
        for s in range(2):
            close, distant = halo_y[stage, s, 1 - s], halo_y[stage, s, s]
            own = vs[stage, pl.ds(0 if s == 0 else ny - 1, nx, stride=ny), :]
            gy = own - distant if s == 0 else distant - own
            gx = along_rows(close, edge_xy[stage, s], edge_xy[stage, 2 + s])
            edge = turned[pl.ds(ny - 1 if s == 0 else 0, nx, stride=ny), :]
            c = half + 1 + 2 * s
            gz = along_z(close, edge[:, c : c + 1], edge[:, c + 1 : c + 2])

            def coef_y(j, s=s):
                return jnp.concatenate(
                    [wide(coef_row(halo_coef.at[2 + s], t, j), TLX) for t in range(tiles)], 0
                )

            py.append(close)
            fy_out.append(coef_y(3) * gx + coef_y(1) * gy + coef_y(5) * gz)

        def diff_x(a, low, high):
            return jnp.concatenate([a[1:], high[None]], 0) - jnp.concatenate([low[None], a[:-1]], 0)

        def diff_y(a, low, high):
            row = iota((1, ny, nz), 1)
            up = jnp.where(row == ny - 1, high.reshape(nx, 1, nz), pltpu.roll(a, ny - 1, 1))
            down = jnp.where(row == 0, low.reshape(nx, 1, nz), pltpu.roll(a, 1, 1))
            return up - down

        def diff_z(a, edge):
            lane = iota((1, 1, nz), 2)
            up = jnp.where(lane == nz - 1, edge, pltpu.roll(a, nz - 1, 2))
            down = jnp.where(lane == 0, edge, pltpu.roll(a, 1, 2))
            return up - down

        edges = turned[...].reshape(nx, ny, nz)
        gx, gy, gz = diff_x(v, *px), diff_y(v, *py), diff_z(v, edges)
        for t in range(tiles):
            span = slice(t * TLX, (t + 1) * TLX)
            xx, yy, zz, xy, xz_, yz_ = (
                coef_row(mine_coef, t, k).reshape(1, 1, LANES) for k in range(6)
            )
            a, b, c = gx[span], gy[span], gz[span]
            flux[0, span] = xx * a + xy * b + xz_ * c
            flux[1, span] = xy * a + yy * b + yz_ * c
            flux[2, span] = xz_ * a + yz_ * b + zz * c
        edges = pltpu.roll(edges, half, 2)
        lap = (
            diff_x(flux[0], *fx_out)
            + diff_y(flux[1], *fy_out)
            + diff_z(flux[2], edges)
        )
        for t in range(tiles):
            span = slice(t * TLX, (t + 1) * TLX)
            new = v[span] + lap[span] * alive[t]
            where = pl.ds(t * TLX * ny // SUB, TLX * ny // SUB)
            out[0, where] = new.reshape(TLX * ny // SUB, SUB, LANES)

    prepare(0)
    pl.semaphore_wait(barrier, n - 1)
    all_start(0, ids_send, ids_got)
    send(0)
    for i in range(6):

        @pl.when(exists(i))
        def _(i=i):
            coef_copy(i, OPPOSITE[i]).start()


    nodes = elem_node[...]
    disp = []
    for c in range(3):
        table = [
            wide(node_disp[c : c + 1, g : g + LANES]) for g in range(0, node_count, LANES)
        ]
        disp.append([gather_wide(table, ix) for ix in lane_pieces(nodes)])
    fx, fy, fz = frame_of(0, 1)
    table = [pick_rows({0: fx, 1: fy, 2: fz}, (SUB, LANES))]
    frame8 = [gather_wide(table, wide(ix)) for ix in lane_pieces(elem_fibre[...])]
    corner = iota((CORNERS, LANES), 0)
    signs = [
        jnp.where((corner // (4 >> j)) % 2 == 1, 0.25, -0.25) for j in range(3)
    ]
    shear, bulk, scale = material[0], material[1], material[2]
    passive, pulled = [], []
    for h in range(elem_count // LANES):
        frame = [frame8[h][i : i + 1] for i in range(3)]
        d = [
            [
                sub_sum(disp[i][h] * signs[j]) + (1.0 if i == j else 0.0)
                for j in range(3)
            ]
            for i in range(3)
        ]
        cof = [
            [
                d[(i + 1) % 3][(j + 1) % 3] * d[(i + 2) % 3][(j + 2) % 3]
                - d[(i + 1) % 3][(j + 2) % 3] * d[(i + 2) % 3][(j + 1) % 3]
                for j in range(3)
            ]
            for i in range(3)
        ]
        volume = d[0][0] * cof[0][0] + d[0][1] * cof[0][1] + d[0][2] * cof[0][2]
        reciprocal = 1.0 / volume
        logv = jnp.log(volume)
        stress = [
            [
                shear * (d[i][j] - cof[i][j] * reciprocal)
                + bulk * logv * (cof[i][j] * reciprocal)
                for j in range(3)
            ]
            for i in range(3)
        ]
        stretch = [
            scale * (d[i][0] * frame[0] + d[i][1] * frame[1] + d[i][2] * frame[2])
            for i in range(3)
        ]
        along = sum(wide(frame[j]) * signs[j] for j in range(3))
        passive.append([sum(wide(stress[i][j]) * signs[j] for j in range(3)) for i in range(3)])
        pulled.append([wide(stretch[i]) * along for i in range(3)])

    found = jnp.zeros((CORNERS, node_count), f32)
    lane_e = (iota((CORNERS, elem_count), 1) + 1).astype(f32)
    for q in range(CORNERS):
        named = onehot(iota((node_count, elem_count), 0) == nodes[q : q + 1, :])
        mine = jnp.where(iota((CORNERS, elem_count), 0) == q, lane_e, 0.0).astype(bf16)
        found = found + mm(mine, named, NT)
    inverse[...] = found.astype(i32) - 1

    receive(0)
    for i in range(6):

        @pl.when(exists(i))
        def _(i=i):
            coef_copy(i, i).wait()

    diffuse(0)

    pulls = []
    for t in range(tiles):
        where = pl.ds(t * TLX * ny // SUB, TLX * ny // SUB)
        calcium = calcium_of(out[NSTATE - 1, where], out[0, where], t)
        out[NSTATE - 1, where] = calcium
        square = calcium * calcium
        pulls.append(square / (square + tension_half))
    pull = jnp.concatenate(pulls, 0).reshape(bx, SBX, ny, nz)
    pull = (pull[:, 0] + pull[:, 1]).reshape(bx * ny, nz)
    strip = onehot(iota((SUB, nz), 1) // SBZ == iota((SUB, nz), 0))
    high = pull.astype(bf16)
    rest = (pull - high.astype(f32)).astype(bf16)
    pooled = mm(strip, high, NT) + mm(strip, rest, NT)
    lanes_p = bx * ny
    value = (pooled + pltpu.roll(pooled, lanes_p - 1, 1)) * weights
    even = iota((1, lanes_p), 1) % 2 == 0
    odd_value = pltpu.roll(value, 1, 1)
    tables = [
        wide(jnp.where(even, value[b : b + 1], odd_value[b + 1 : b + 2]))
        for b in range(0, bz, 2)
    ]
    for r in range(0, n * GROUPS, SUB):
        where = slot_pos[r : r + SUB]
        picked = jnp.where(where >= 0, gather_wide(tables, jnp.maximum(where, 0)), 0.0)
        val_send[r // GROUPS : (r + SUB) // GROUPS] = picked.reshape(
            SUB // GROUPS, GROUPS, LANES
        )
    all_start(1, val_send, val_got)

    def second(t):
        def go(i, carry):
            ionic(out, 1, i, t)
            return carry

        lax.fori_loop(2 * t, 2 * t + 2, go, 0)

    all_wait(0, ids_send, ids_got)
    asked = []
    for g in range(slot_groups):
        total = ids_got[g * per_group]
        for m in range(1, per_group):
            total = total + ids_got[g * per_group + m]
        asked.append(total)
        index = jnp.maximum(total.astype(i32) - 1, 0)
        rows_out = []
        for k in range(GROUPS):
            where = wide(index[k : k + 1])
            rows_out += [gather_wide(disp[c], where) for c in range(3)]
            rows_out.append(jnp.zeros((SUB, LANES), f32))
        answer = jnp.transpose(jnp.concatenate(rows_out, 0))
        ans_send[g * per_group : (g + 1) * per_group] = answer.reshape(
            per_group, rows_each, LANES
        )
    all_start(2, ans_send, ans_got)
    for t in range(tiles):
        second(t)
    prepare(1)
    send(1)

    code = jnp.zeros((LANES, elem_count), f32)
    for g in range(slot_groups):
        column = jnp.transpose(
            jnp.concatenate([asked[g], jnp.zeros((LANES - GROUPS, LANES), f32)], 0)
        )
        ident = (iota((LANES, elem_count), 1) + 1).astype(f32)
        row = iota((LANES, elem_count), 0).astype(f32)
        for k in range(GROUPS):
            code = jnp.where(
                column[:, k : k + 1] == ident, row + float((g * GROUPS + k) * LANES), code
            )
    slot_of = sub_sum(code).astype(i32)

    receive(1)
    diffuse(1)

    all_wait(1, val_send, val_got)
    tables = []
    for g in range(slot_groups):
        total = val_got[g * per_group]
        for m in range(1, per_group):
            total = total + val_got[g * per_group + m]
        tables += [wide(total[k : k + 1]) for k in range(GROUPS)]
    tension = [gather_wide(tables, wide(ix)) for ix in lane_pieces(slot_of)]
    force = [
        [passive[h][i] + tension[h] * pulled[h][i] for h in range(elem_count // LANES)]
        for i in range(3)
    ]
    for g in range(0, node_count, LANES):
        where = inverse[:, g : g + LANES]
        index = jnp.maximum(where, 0)
        for i in range(3):
            got = jnp.where(where >= 0, gather_wide(force[i], index), 0.0)
            resid_out[i : i + 1, g : g + LANES] = sub_sum(got)

    wanted_out[0:1] = back_row
    wanted_out[1:2] = group
    all_wait(2, ans_send, ans_got)
    answers_out[...] = ans_got[...]


def write_out(states, resid, answers, wanted, states_out, fine_out, resid_out, fine, sems):
    n, rows_each = answers.shape[:2]
    nx, ny, nz = fine.shape[1:]
    bx, by, bz = nx // SBX, ny // SBY, nz // SBZ
    plane = bx * by
    blocks = plane * bz
    per_group = LANES // rows_each
    slot_groups = n * rows_each // LANES
    copies = [
        pltpu.make_async_copy(states, states_out, sems.at[0]),
        pltpu.make_async_copy(resid, resid_out, sems.at[1]),
    ]
    for c in copies:
        c.start()

    def fine_copy(i):
        here = pl.ds(i * nx // PIECES, nx // PIECES)
        return pltpu.make_async_copy(fine.at[:, here], fine_out.at[:, here], sems.at[2 + i])

    columns = [
        jnp.transpose(
            answers[g * per_group : (g + 1) * per_group].reshape(LANES, LANES)
        )
        for g in range(slot_groups)
    ]
    span = 32
    halves = []
    for h in range(blocks // LANES):
        cut = slice(h * LANES, (h + 1) * LANES)
        where, which = wide(wanted[0:1, cut]), wide(wanted[1:2, cut])
        rows_in = []
        for c in range(3):
            value = None
            for k in range(GROUPS):
                first = k * span + c * SUB
                found = gather_wide([col[first : first + SUB] for col in columns], where)
                value = found if value is None else jnp.where(which == k, found, value)
            value = 0.75 * value + 0.25 * pltpu.roll(value, 4, 0)
            swapped = jnp.where(
                iota((SUB, LANES), 0) // 2 % 2 == 1,
                pltpu.roll(value, 2, 0),
                pltpu.roll(value, SUB - 2, 0),
            )
            rows_in.append(0.75 * value + 0.25 * swapped)
        rows_in.append(jnp.zeros((SUB, LANES), f32))
        halves.append(jnp.concatenate(rows_in, 0))
    stacked = []
    for b in range(bz):
        lane0 = b * plane
        piece = halves[lane0 // LANES]
        stacked.append(
            pltpu.roll(piece, LANES - lane0 % LANES, 1) if lane0 % LANES else piece
        )
    around = jnp.transpose(jnp.concatenate(stacked, 0))
    lane = iota((SUB, nz), 1)
    strip_lane = lane // SBZ * span
    xi = ((lane % SBZ).astype(f32) + 0.5) / SBZ
    for p in range(bx):
        near = around[p * by : (p + 1) * by]
        for c in range(3):
            for iv in range(SBX):
                for jv in range(SBY):
                    first = c * SUB + 4 * iv + 2 * jv
                    low = lane_gather(near, strip_lane + first)
                    high = lane_gather(near, strip_lane + first + 1)
                    fine[c, SBX * p + iv, pl.ds(jv, by, stride=SBY), :] = (
                        low + (high - low) * xi
                    )
        if (p + 1) % (bx // PIECES) == 0:
            fine_copy(p // (bx // PIECES)).start()
    for i in range(PIECES):
        fine_copy(i).wait()
    for c in copies:
        c.wait()


def shards(
    states,
    active,
    fibre_index,
    fibre_angle,
    conduct,
    gate_half,
    gate_slope,
    gate_tau,
    conductance,
    reversal,
    block_elem,
    block_weight,
    node_disp,
    elem_node,
    elem_fibre,
    material,
):
    mx, my, mz = (lax.axis_size(a) for a in AXES)
    n = mx * my * mz
    elem_count = elem_node.shape[1]
    node_count = node_disp.shape[1]
    nx, ny, nz = states.shape[1:]
    bx, by, bz = block_elem.shape
    blocks = bx * by * bz
    seats = max(2 * blocks // n, 8)
    rows_each = seats // GROUPS
    tiles = nx // TLX
    strips = nx * ny // SUB
    ids = block_elem.transpose(0, 2, 1)
    weight = block_weight.transpose(0, 2, 1)
    vmem = pl.BlockSpec(memory_space=pltpu.VMEM)
    hbm = pl.BlockSpec(memory_space=pltpu.HBM)
    gates_n = NSTATE - 2
    ways = len(DIRS)
    operands = (
        states.reshape(NSTATE, strips, SUB, nz),
        active.transpose(1, 2, 0),
        fibre_index.transpose(1, 2, 0),
        fibre_angle,
        fibre_angle,
        conduct,
        gate_half,
        gate_slope,
        gate_tau,
        conductance,
        reversal,
        ids,
        weight,
        node_disp,
        elem_node,
        elem_fibre.reshape(1, elem_count),
        material,
    )
    stage = FINE_STEPS
    states_shape = jax.ShapeDtypeStruct((NSTATE, strips, SUB, nz), f32)
    fine_shape = jax.ShapeDtypeStruct((3, nx, ny, nz), f32)
    resid_shape = jax.ShapeDtypeStruct((3, node_count), f32)
    in_smem = [True] * 3 + [False] + [True] * 6 + [False] * 5 + [True]
    results = pl.pallas_call(
        functools.partial(body, (mx, my, mz, seats, nx, ny)),
        out_shape=(
            states_shape,
            resid_shape,
            jax.ShapeDtypeStruct((n, rows_each, LANES), f32),
            jax.ShapeDtypeStruct((2, blocks), i32),
        ),
        in_specs=[hbm] * len(operands),
        out_specs=(vmem,) * 4,
        scratch_shapes=[
            (pltpu.SMEM if scalar else pltpu.VMEM)(x.shape, x.dtype)
            for scalar, x in zip(in_smem, operands[1:])
        ]
        + [
            pltpu.VMEM((NSTATE, strips, SUB, nz), f32),
            pltpu.VMEM((stage, nx * ny, nz), f32),
            pltpu.VMEM((3, nx, ny, nz), f32),
            pltpu.VMEM((gates_n, 2, SUB, LANES), f32),
            pltpu.VMEM((tiles, gates_n, 4, SUB, LANES), f32),
            pltpu.VMEM((tiles * SUB, LANES), f32),
            pltpu.VMEM((stage, 2, 2, nx, nz), f32),
            pltpu.VMEM((stage, 2, 2, nx * ny), f32),
            pltpu.VMEM((stage, 4, 1, nz), f32),
            pltpu.VMEM((stage, 2, 1, nx * ny), f32),
            pltpu.VMEM((stage, 2, 2 * ny, nz), f32),
            pltpu.VMEM((stage, 2, 2, nx, nz), f32),
            pltpu.VMEM((stage, 2, 2, nx * ny), f32),
            pltpu.VMEM((stage, 4, 1, nz), f32),
            pltpu.VMEM((stage, 4, 1, nx * ny), f32),
            pltpu.VMEM((stage, 4, 1, nx * ny), f32),
            pltpu.VMEM((6, tiles * SUB, LANES), f32),
            pltpu.VMEM((nx * ny, nz), f32),
            pltpu.VMEM((n * GROUPS, LANES), i32),
            pltpu.VMEM((CORNERS, node_count), i32),
            pltpu.VMEM((n, GROUPS, LANES), f32),
            pltpu.VMEM((n, GROUPS, LANES), f32),
            pltpu.VMEM((n, GROUPS, LANES), f32),
            pltpu.VMEM((n, GROUPS, LANES), f32),
            pltpu.VMEM((n, rows_each, LANES), f32),
            pltpu.VMEM((n, rows_each, LANES), f32),
            pltpu.SemaphoreType.DMA((2 * tiles,)),
            pltpu.SemaphoreType.DMA((len(operands) - 1,)),
            pltpu.SemaphoreType.DMA((stage, ways)),
            pltpu.SemaphoreType.DMA((stage, ways)),
            pltpu.SemaphoreType.DMA((6,)),
            pltpu.SemaphoreType.DMA((6,)),
            pltpu.SemaphoreType.DMA((3,)),
            pltpu.SemaphoreType.DMA((3,)),
        ],
        compiler_params=pltpu.CompilerParams(
            collective_id=0, has_side_effects=True, vmem_limit_bytes=20 * 1024 * 1024
        ),
        name="step",
    )(*(pltpu.with_memory_space_constraint(a, pltpu.HBM) for a in operands))
    results = pl.pallas_call(
        write_out,
        out_shape=(states_shape, fine_shape, resid_shape),
        in_specs=[vmem] * 4,
        out_specs=(hbm,) * 3,
        scratch_shapes=[
            pltpu.VMEM((3, nx, ny, nz), f32),
            pltpu.SemaphoreType.DMA((2 + PIECES,)),
        ],
        compiler_params=pltpu.CompilerParams(vmem_limit_bytes=20 * 1024 * 1024),
        name="write",
    )(*results)
    return results[0].reshape(states.shape), results[1], results[2]


def solution(mesh):
    in_specs = (
        P(None, "gx", "gy", "gz"),
        P("gx", "gy", "gz"),
        P("gx", "gy", "gz"),
        P(),
        P(),
        P(),
        P(),
        P(),
        P(),
        P(),
        P("gx", "gy", "gz"),
        P("gx", "gy", "gz"),
        P(None, ("gx", "gy", "gz")),
        P(None, ("gx", "gy", "gz")),
        P(("gx", "gy", "gz")),
        P(),
    )
    out_specs = (P(None, "gx", "gy", "gz"), P(None, "gx", "gy", "gz"), P(None, ("gx", "gy", "gz")))
    return jax.shard_map(shards, mesh=mesh, in_specs=in_specs, out_specs=out_specs, check_vma=False)
```

```python
import functools

import jax
import jax.numpy as jnp
from jax import lax
from jax.experimental import pallas as pl
from jax.experimental.pallas import tpu as pltpu
from jax.sharding import PartitionSpec as P

NSTATE = 19
TLX = 8
SBX = 2
SBY = 2
SBZ = 32
FINE_STEPS = 2
AXES = ("gx", "gy", "gz")
MESH = pl.DeviceIdType.MESH
LANES = 128
SUB = 8
CORNERS = 8
ROWS = 4
PIECES = 4
f32 = jnp.float32
bf16 = jnp.bfloat16
i32 = jnp.int32
calcium_keep = 0.9
tension_half = 0.09
NN = (((1,), (0,)), ((), ()))
NT = (((1,), (1,)), ((), ()))
DIRS = (
    [tuple(side if d == dim else 0 for d in range(3)) for dim in range(3) for side in (-1, 1)]
    + [(a, b, 0) for a in (-1, 1) for b in (-1, 1)]
    + [(a, 0, b) for a in (-1, 1) for b in (-1, 1)]
    + [(0, a, b) for a in (-1, 1) for b in (-1, 1)]
)
OPPOSITE = [DIRS.index(tuple(-c for c in d)) for d in DIRS]


def mm(a, b, dims=NN):
    return lax.dot_general(a, b, dims, preferred_element_type=f32)


def parts(x, count):
    out = []
    for _ in range(count):
        out.append(x.astype(bf16).astype(f32))
        x = x - out[-1]
    return out


def iota(shape, dim):
    return lax.broadcasted_iota(i32, shape, dim)


def onehot(mask):
    return jnp.where(mask, 1.0, 0.0).astype(bf16)


def pick_rows(rows, shape):
    index = iota(shape, 0)
    out = jnp.zeros(shape, f32)
    for i, row in rows.items():
        out = jnp.where(index == i, row, out)
    return out


def lane_gather(x, index):
    return jnp.take_along_axis(x, index, axis=1, mode="promise_in_bounds")


def wide(row, rows=SUB):
    return jnp.broadcast_to(row, (rows, row.shape[1]))


def gather_wide(tables, index):
    low, high = index % LANES, index // LANES
    out = lane_gather(tables[0], low)
    for h in range(1, len(tables)):
        out = jnp.where(high == h, lane_gather(tables[h], low), out)
    return out


def lane_pieces(x):
    return [x[:, h : h + LANES] for h in range(0, x.shape[1], LANES)]


def row_totals(got, per_row, row):
    totals = []
    for r in range(0, got.shape[0], per_row):
        total = got[r, row : row + 1]
        for m in range(1, per_row):
            total = total + got[r + m, row : row + 1]
        totals.append(total)
    return totals


def sub_sum(x):
    return jnp.sum(x, axis=0, keepdims=True)


def body(
    sizes,
    *refs,
):
    mx, my, mz, seats, nx, ny = sizes
    operands, refs = refs[:17], refs[17:]
    states = operands[0]
    out, answers_out, wanted_out, inverse, forces_out = refs[:5]
    small, refs = refs[5:21], refs[21:]
    (
        active,
        fibre_index,
        angle_s,
        angle_v,
        conduct,
        gate_half,
        gate_slope,
        gate_tau,
        conductance,
        reversal,
        ids_ref,
        weight_ref,
        node_disp,
        elem_node,
        elem_fibre,
        material,
    ) = small
    (
        held,
        vs,
        flux,
        gate_const,
        tile_const,
        sums,
        bends,
        mine_coef,
        send_y,
        send_z,
        send_xy,
        send_row,
        halo_x,
        halo_y,
        halo_z,
        edge_xy,
        edge_xz,
        edge_yz,
        halo_coef,
        tally,
        turned,
        slot_pos,
        ids_send,
        ids_got,
        ans_send,
        ans_got,
        load_sem,
        small_sem,
        face_send_sem,
        face_recv_sem,
        coef_send_sem,
        coef_recv_sem,
        all_send_sem,
        all_recv_sem,
    ) = refs
    nz = states.shape[3]
    n = mx * my * mz
    gates_n = NSTATE - 2
    strips = nx * ny // SUB
    bx, by, bz = nx // SBX, ny // SBY, nz // SBZ
    plane = bx * by
    blocks = plane * bz
    tiles = nx // TLX
    node_count = node_disp.shape[1]
    elem_count = elem_node.shape[1]
    per_group = LANES // ROWS
    slot_groups = n // per_group
    per_row = LANES // seats
    slot_rows = n // per_row
    cx, cy, cz = (lax.axis_index(a) for a in AXES)
    me = (cx * my + cy) * mz + cz
    at = (cx, cy, cz)
    counts = (mx, my, mz)

    def others():
        steps = [
            (a, b, c) for a in range(mx) for b in range(my) for c in range(mz) if a or b or c
        ]

        def far(step):
            return sum(
                (1 if d == 1 else max(s, m - s)) if s else 0
                for d, (s, m) in enumerate(zip(step, counts))
            )

        return sorted(steps, key=far, reverse=True)

    wrapped = [[jnp.where(p + s >= m, p + s - m, p + s) for s in range(m)] for p, m in zip(at, counts)]

    def each_other(go):
        if n <= 64:
            for step in others():
                go(tuple(wrapped[d][s] for d, s in enumerate(step)))
        else:

            def one(k, carry):
                flat = (me + k) % n
                go((flat // (my * mz), (flat // mz) % my, flat % mz))
                return carry

            lax.fori_loop(1, n, one, 0)

    chunk = TLX * ny // SUB // 2

    def load(i):
        here = pl.ds(i * chunk, chunk)
        return pltpu.make_async_copy(states.at[:, here], held.at[:, here], load_sem.at[i])

    small_loads = [
        pltpu.make_async_copy(src, dst, small_sem.at[i])
        for i, (src, dst) in enumerate(zip(operands[1:], small))
    ]
    for c in small_loads:
        c.start()
    for i in range(strips // chunk):
        load(i).start()

    for ref in (halo_x, halo_y, halo_z, edge_xy, edge_xz, edge_yz):
        used = ref.shape[1] // 2
        ref[:, :used] = jnp.zeros((ref.shape[0], used) + ref.shape[2:], f32)
    halo_coef[:6] = jnp.zeros((6,) + halo_coef.shape[1:], f32)

    barrier = pltpu.get_barrier_semaphore()
    each_other(
        lambda to: pl.semaphore_signal(barrier, inc=1, device_id=to, device_id_type=MESH)
    )

    for c in small_loads:
        c.wait()

    def splat(value):
        return jnp.full((SUB, LANES), value, f32)

    angles = jnp.concatenate(
        [angle_v[...], jnp.zeros((2, LANES - angle_v.shape[1]), f32)], 1
    ) if angle_v.shape[1] < LANES else angle_v[...]
    rows = {0: angles[0:1], 1: angles[1:2]}
    across, spread, alive = [], [], []
    for t in range(tiles):
        index = fibre_index[0, 0, t]
        rows[2 + t] = jnp.full((1, LANES), angle_s[0, index], f32)
        rows[2 + tiles + t] = jnp.full((1, LANES), angle_s[1, index], f32)
        across.append(jnp.full((1, LANES), conduct[1, index], f32))
        spread.append(jnp.full((1, LANES), conduct[0, index], f32) - across[t])
        alive.append(jnp.where(active[0, 0, t] > 0, 1.0, 0.0).astype(f32))
    stack = pick_rows(rows, (SUB, LANES))
    cosine, sine = jnp.cos(stack), jnp.sin(stack)

    def frame_of(a, b):
        ca, sa = cosine[a : a + 1], sine[a : a + 1]
        cb, sb = cosine[b : b + 1], sine[b : b + 1]
        return ca * cb, sa * cb, sb

    for t in range(tiles):
        fx, fy, fz = frame_of(2 + t, 2 + tiles + t)
        scale = alive[t] * 0.25
        entries = [
            across[t] + spread[t] * fx * fx,
            across[t] + spread[t] * fy * fy,
            across[t] + spread[t] * fz * fz,
            spread[t] * fx * fy,
            spread[t] * fx * fz,
            spread[t] * fy * fz,
        ]
        mine_coef[t * SUB : (t + 1) * SUB] = pick_rows(
            {k: e * scale for k, e in enumerate(entries)}, (SUB, LANES)
        )

    for g in range(gates_n):
        slope = 0.5 / splat(gate_slope[g])
        gate_const[g, 0] = slope
        gate_const[g, 1] = slope * gate_half[g]
        keep = jnp.exp(-1.0 / splat(gate_tau[g]))
        share = 0.5 * (1.0 - keep)
        cond = splat(conductance[g])
        for t in range(tiles):
            live = splat(alive[t]) > 0.5
            tile_const[t, g, 0] = jnp.where(live, keep, 1.0)
            tile_const[t, g, 1] = jnp.where(live, share, 0.0)
            tile_const[t, g, 2] = jnp.where(live, cond, 0.0)
            pull = cond * reversal[g]
            tile_const[t, g, 3] = jnp.where(live, pull, 0.0)
            tile_const[t, g, 4] = jnp.where(live, cond * share, 0.0)
            tile_const[t, g, 5] = jnp.where(live, pull * share, 0.0)

    def live_calcium(t):
        live = splat(alive[t]) > 0.5
        keep = jnp.where(live, calcium_keep, 1.0)
        share = jnp.where(live, 0.5 * (1.0 - calcium_keep), 0.0)
        return keep, share

    def calcium_of(old, volt, t):
        keep, share = live_calcium(t)
        return old * keep + (jnp.tanh(4.0 * volt - 2.0) * share + share)

    def ionic(i, t):
        where = pl.ds(i * chunk, chunk)
        volt = held[0, where]
        total = jnp.zeros_like(volt)
        shift = jnp.zeros_like(volt)
        for g in range(gates_n):
            bend = jnp.tanh(volt * gate_const[g, 0] - gate_const[g, 1])
            share = tile_const[t, g, 1]
            gate = held[1 + g, where] * tile_const[t, g, 0] + (bend * share + share)
            out[1 + g, where] = gate
            total = total + gate * tile_const[t, g, 2]
            shift = shift + gate * tile_const[t, g, 3]
        star = volt - (volt * total - shift)
        vs[0, pl.ds(i * chunk * SUB, chunk * SUB)] = star.reshape(chunk * SUB, LANES)

    def ionic_before(i, t):
        where = pl.ds(i * chunk, chunk)
        total = jnp.zeros((chunk, SUB, LANES), f32)
        shift = jnp.zeros((chunk, SUB, LANES), f32)
        for g in range(gates_n):
            kept = out[1 + g, where] * tile_const[t, g, 0] + tile_const[t, g, 1]
            out[1 + g, where] = kept
            total = total + kept * tile_const[t, g, 2]
            shift = shift + kept * tile_const[t, g, 3]
        sums[0, where] = total
        sums[1, where] = shift

    def ionic_between(i, t):
        where = pl.ds(i * chunk, chunk)
        volt = out[0, where]
        total = sums[0, where]
        shift = sums[1, where]
        for g in range(gates_n):
            bend = jnp.tanh(volt * gate_const[g, 0] - gate_const[g, 1])
            bends[g, where] = bend
            total = total + bend * tile_const[t, g, 4]
            shift = shift + bend * tile_const[t, g, 5]
        star = volt - (volt * total - shift)
        vs[1, pl.ds(i * chunk * SUB, chunk * SUB)] = star.reshape(chunk * SUB, LANES)

    def ionic_after(i, t):
        where = pl.ds(i * chunk, chunk)
        for g in range(gates_n):
            out[1 + g, where] = out[1 + g, where] + bends[g, where] * tile_const[t, g, 1]

    def over_chunks(step):
        for t in range(tiles):

            def go(i, carry, t=t):
                step(i, t)
                return carry

            lax.fori_loop(2 * t, 2 * t + 2, go, 0)

    flat_in = (bx * bz, by)
    raw = jnp.concatenate(
        parts(ids_ref[...].astype(f32).reshape(flat_in), 3), 0
    ).astype(bf16)
    lane_b = iota((by, blocks), 1)
    put = onehot(lane_b % by == iota((by, blocks), 0))
    spread_ids = mm(raw, put)
    part = bx * bz
    spread_ids = spread_ids[:part] + spread_ids[part : 2 * part] + spread_ids[2 * part :]
    row_b, col_b = iota((part, blocks), 0), iota((part, blocks), 1)
    here = (row_b // bz == (col_b % plane) // by) & (row_b % bz == col_b // plane)
    ids = sub_sum(jnp.where(here, spread_ids, 0.0)).astype(i32)
    shift = elem_count.bit_length() - 1
    owner = lax.shift_right_logical(ids, shift)
    local = ids - owner * elem_count
    owned = onehot(owner == iota((n, blocks), 0))
    before = onehot(iota((blocks, blocks), 0) < iota((blocks, blocks), 1))
    seen = mm(owned, before)
    rank = sub_sum(owned.astype(f32) * seen).astype(i32)
    offset = (me % per_row) * seats
    hit = owner == iota((n, blocks), 0)
    place = onehot(iota((LANES, blocks), 0) == rank + offset)
    sent = jnp.concatenate(
        [
            jnp.where(hit, (local + 1).astype(f32), 0.0),
            jnp.where(hit, (iota((1, blocks), 1) + 1).astype(f32), 0.0),
        ],
        0,
    ).astype(bf16)
    sent = mm(sent, place, NT)
    ids_send[...] = sent[:n].reshape(n, 1, LANES)
    block_at = sent[n:].astype(i32) - 1
    in_plane = block_at % plane
    slot_pos[...] = jnp.where(
        block_at >= 0,
        (block_at // plane // 2) * LANES
        + (in_plane // by) * ny
        + (in_plane % by) * SBY
        + (block_at // plane) % 2,
        -1,
    )
    wanted_out[0:1] = owner
    wanted_out[1:2] = rank

    raw = jnp.concatenate(parts(weight_ref[...].reshape(flat_in), 2), 0).astype(bf16)
    put = onehot(iota((by, bx * ny), 1) % ny == iota((by, bx * ny), 0) * SBY)
    spread_w = mm(raw, put)
    spread_w = (spread_w[:part] + spread_w[part:]).reshape(bx, bz, bx * ny)
    here = iota((bx, bz, bx * ny), 0) == iota((bx, bz, bx * ny), 2) // ny
    weights = jnp.sum(jnp.where(here, spread_w, 0.0), axis=0)
    weights = jnp.concatenate([weights, jnp.zeros((SUB - bz, bx * ny), f32)], 0)
    weights = weights * (1.0 / (SBX * SBY * SBZ))

    def first(i, t):
        load(i).wait()
        ionic(i, t)
        here = pl.ds(i * chunk, chunk)
        out[NSTATE - 1, here] = calcium_of(held[NSTATE - 1, here], held[0, here], t)

    over_chunks(first)

    def source_of(stage, i):
        d = DIRS[i]
        if i < 2:
            return vs.at[stage, pl.ds(0 if d[0] < 0 else (nx - 2) * ny, 2 * ny)]
        if i < 4:
            return send_y.at[stage, i - 2]
        if i < 6:
            return send_z.at[stage, i - 4]
        if i < 10:
            return send_xy.at[stage, i - 6]
        return send_row.at[stage, 0 if d[2] < 0 else 1]

    families = (
        [(halo_x, 0, 2), (halo_y, 2, 2), (halo_z, 4, 2)]
        + [(edge_xy, 6, 4), (edge_xz, 10, 4), (edge_yz, 14, 4)]
    )

    def exists(i):
        ok = None
        for p, step, m in zip(at, DIRS[i], counts):
            if step:
                inside = p > 0 if step < 0 else p < m - 1
                ok = inside if ok is None else ok & inside
        return ok

    def route(i):
        ok = exists(i)
        swap = next(d for d in (1, 0, 2) if DIRS[i][d] == 0)
        to = []
        for d, (p, step) in enumerate(zip(at, DIRS[i])):
            if step:
                p = jnp.where(ok, p + step, p)
            elif d == swap:
                p = jnp.where(ok, p, p + 1 - 2 * (p % 2))
            to.append(p)
        return tuple(to), ok

    order = list(range(len(DIRS) - 1, -1, -1))

    def prepare(stage):
        for side in range(2):
            for layer in range(2):
                y = layer if side == 0 else ny - 2 + layer
                send_y[stage, side, layer] = vs[stage, pl.ds(y, nx, stride=ny), :]
        for a in range(2):
            for b in range(2):
                row = (nx - 1) * a * ny + (ny - 1) * b
                send_xy[stage, 2 * a + b] = vs[stage, row : row + 1, :]
        columns = jnp.transpose(vs[stage])
        send_z[stage, 0] = columns[0:2]
        send_z[stage, 1] = columns[nz - 2 : nz]
        send_row[stage, 0] = columns[0:1]
        send_row[stage, 1] = columns[nz - 1 : nz]

    def send(stage):
        for i in order:
            ref, first, count = next(f for f in families if f[1] <= i < f[1] + f[2])
            to, ok = route(i)
            slot = jnp.where(ok, OPPOSITE[i] - first, count + i - first)
            pltpu.make_async_remote_copy(
                src_ref=source_of(stage, i),
                dst_ref=ref.at[stage, slot],
                send_sem=face_send_sem.at[stage],
                recv_sem=face_recv_sem.at[stage],
                device_id=to,
                device_id_type=MESH,
            ).start()

    def receive(stage):
        pltpu.make_async_remote_copy(
            src_ref=tally,
            dst_ref=tally,
            send_sem=face_send_sem.at[stage],
            recv_sem=face_recv_sem.at[stage],
            device_id=at,
            device_id_type=MESH,
        ).wait()

    def send_coef():
        for i in range(6):
            to, ok = route(i)
            pltpu.make_async_remote_copy(
                src_ref=mine_coef,
                dst_ref=halo_coef.at[jnp.where(ok, OPPOSITE[i], 6 + i)],
                send_sem=coef_send_sem,
                recv_sem=coef_recv_sem,
                device_id=to,
                device_id_type=MESH,
            ).start()

    def receive_coef():
        pltpu.make_async_remote_copy(
            src_ref=halo_coef.at[pl.ds(0, 6)],
            dst_ref=halo_coef.at[pl.ds(0, 6)],
            send_sem=coef_send_sem,
            recv_sem=coef_recv_sem,
            device_id=at,
            device_id_type=MESH,
        ).wait()

    def all_start(kind, src, dst):
        dst[pl.ds(me, 1)] = src[pl.ds(me, 1)]

        def go(to):
            flat = (to[0] * my + to[1]) * mz + to[2]
            pltpu.make_async_remote_copy(
                src_ref=src.at[flat],
                dst_ref=dst.at[me],
                send_sem=all_send_sem.at[kind],
                recv_sem=all_recv_sem.at[kind],
                device_id=to,
                device_id_type=MESH,
            ).start()

        each_other(go)

    def all_wait(kind, src, dst):
        pltpu.make_async_remote_copy(
            src_ref=src.at[pl.ds(0, n - 1)],
            dst_ref=dst.at[pl.ds(0, n - 1)],
            send_sem=all_send_sem.at[kind],
            recv_sem=all_recv_sem.at[kind],
            device_id=at,
            device_id_type=MESH,
        ).wait()

    def coef_row(ref, t, k):
        return ref[t * SUB + k : t * SUB + k + 1, :]

    def diffuse(stage):
        v = vs[stage].reshape(nx, ny, nz)
        lane = iota((1, nz), 1)
        flat = nx * ny
        lane_f = iota((SUB, flat), 1)

        def both(low, high):
            return pick_rows({0: low, 1: high}, (SUB, flat))

        near = both(halo_z[stage, 0, 1:2], halo_z[stage, 1, 0:1])
        gz = both(
            send_row[stage, 0] - halo_z[stage, 0, 0:1],
            halo_z[stage, 1, 1:2] - send_row[stage, 1],
        )
        xz = [both(edge_xz[stage, 2 * a], edge_xz[stage, 2 * a + 1]) for a in range(2)]
        yz = [both(edge_yz[stage, 2 * a], edge_yz[stage, 2 * a + 1]) for a in range(2)]
        up = pltpu.roll(jnp.where(lane_f < ny, xz[1], near), flat - ny, 1)
        down = pltpu.roll(jnp.where(lane_f >= flat - ny, xz[0], near), ny, 1)
        gx = up - down
        up = jnp.where(
            lane_f % ny == ny - 1, pltpu.roll(yz[1], ny - 1, 1), pltpu.roll(near, flat - 1, 1)
        )
        down = jnp.where(
            lane_f % ny == 0, pltpu.roll(yz[0], flat - ny + 1, 1), pltpu.roll(near, 1, 1)
        )
        gy = up - down

        def coef_z(k):
            return both(
                *(
                    jnp.concatenate(
                        [coef_row(halo_coef.at[4 + s], t, k) for t in range(tiles)], 1
                    )
                    for s in range(2)
                )
            )

        fz = coef_z(4) * gx + coef_z(5) * gy + coef_z(2) * gz
        blank = jnp.zeros((SUB, flat), f32)
        half = nz // 2
        pieces = [blank] * (nz // SUB)
        pieces[0] = pick_rows(
            {0: near[0:1], **{1 + i: edge_xz[stage, i] for i in range(4)}}, (SUB, flat)
        )
        pieces[half // SUB - 1] = pick_rows({SUB - 1: fz[1:2]}, (SUB, flat))
        pieces[half // SUB] = pick_rows(
            {0: fz[0:1], **{1 + i: edge_yz[stage, i] for i in range(4)}}, (SUB, flat)
        )
        pieces[-1] = pick_rows({SUB - 1: near[1:2]}, (SUB, flat))
        turned[...] = jnp.transpose(jnp.concatenate(pieces, 0))

        def along_z(a, low, high):
            return jnp.where(lane == nz - 1, high, pltpu.roll(a, nz - 1, 1)) - jnp.where(
                lane == 0, low, pltpu.roll(a, 1, 1)
            )

        def along_rows(a, low, high):
            row = iota(a.shape, 0)
            m = a.shape[0]
            return jnp.where(row == m - 1, high, pltpu.roll(a, m - 1, 0)) - jnp.where(
                row == 0, low, pltpu.roll(a, 1, 0)
            )

        px, fx_out = [], []
        for s in range(2):
            close = halo_x[stage, s, ny:] if s == 0 else halo_x[stage, s, :ny]
            distant = halo_x[stage, s, :ny] if s == 0 else halo_x[stage, s, ny:]
            gx = v[0] - distant if s == 0 else distant - v[nx - 1]
            gy = along_rows(close, edge_xy[stage, 2 * s], edge_xy[stage, 2 * s + 1])
            first = (nx - 1) * ny if s == 0 else 0
            edge = turned[first : first + ny, :]
            c = 1 + 2 * s
            gz = along_z(close, edge[:, c : c + 1], edge[:, c + 1 : c + 2])
            t = tiles - 1 if s == 0 else 0
            k = [coef_row(halo_coef.at[s], t, j) for j in (0, 3, 4)]
            px.append(close)
            fx_out.append(k[0] * gx + k[1] * gy + k[2] * gz)
        py, fy_out = [], []
        for s in range(2):
            close, distant = halo_y[stage, s, 1 - s], halo_y[stage, s, s]
            own = vs[stage, pl.ds(0 if s == 0 else ny - 1, nx, stride=ny), :]
            gy = own - distant if s == 0 else distant - own
            gx = along_rows(close, edge_xy[stage, s], edge_xy[stage, 2 + s])
            edge = turned[pl.ds(ny - 1 if s == 0 else 0, nx, stride=ny), :]
            c = half + 1 + 2 * s
            gz = along_z(close, edge[:, c : c + 1], edge[:, c + 1 : c + 2])

            def coef_y(j, s=s):
                return jnp.concatenate(
                    [wide(coef_row(halo_coef.at[2 + s], t, j), TLX) for t in range(tiles)], 0
                )

            py.append(close)
            fy_out.append(coef_y(3) * gx + coef_y(1) * gy + coef_y(5) * gz)

        def diff_x(a, low, high):
            return jnp.concatenate([a[1:], high[None]], 0) - jnp.concatenate([low[None], a[:-1]], 0)

        def diff_y(a, low, high):
            row = iota((1, ny, nz), 1)
            up = jnp.where(row == ny - 1, high.reshape(nx, 1, nz), pltpu.roll(a, ny - 1, 1))
            down = jnp.where(row == 0, low.reshape(nx, 1, nz), pltpu.roll(a, 1, 1))
            return up - down

        def diff_z(a, edge):
            lane = iota((1, 1, nz), 2)
            up = jnp.where(lane == nz - 1, edge, pltpu.roll(a, nz - 1, 2))
            down = jnp.where(lane == 0, edge, pltpu.roll(a, 1, 2))
            return up - down

        edges = turned[...].reshape(nx, ny, nz)
        gx, gy, gz = diff_x(v, *px), diff_y(v, *py), diff_z(v, edges)
        for t in range(tiles):
            span = slice(t * TLX, (t + 1) * TLX)
            xx, yy, zz, xy, xz_, yz_ = (
                coef_row(mine_coef, t, k).reshape(1, 1, LANES) for k in range(6)
            )
            a, b, c = gx[span], gy[span], gz[span]
            flux[0, span] = xx * a + xy * b + xz_ * c
            flux[1, span] = xy * a + yy * b + yz_ * c
            flux[2, span] = xz_ * a + yz_ * b + zz * c
        edges = pltpu.roll(edges, half, 2)
        lap = (
            diff_x(flux[0], *fx_out)
            + diff_y(flux[1], *fy_out)
            + diff_z(flux[2], edges)
        )
        for t in range(tiles):
            span = slice(t * TLX, (t + 1) * TLX)
            new = v[span] + lap[span] * alive[t]
            where = pl.ds(t * TLX * ny // SUB, TLX * ny // SUB)
            out[0, where] = new.reshape(TLX * ny // SUB, SUB, LANES)

    prepare(0)
    pl.semaphore_wait(barrier, n - 1)
    all_start(0, ids_send, ids_got)
    send(0)
    send_coef()


    over_chunks(ionic_before)
    nodes = elem_node[...]
    disp = []
    for c in range(3):
        table = [
            wide(node_disp[c : c + 1, g : g + LANES]) for g in range(0, node_count, LANES)
        ]
        disp.append([gather_wide(table, ix) for ix in lane_pieces(nodes)])
    fx, fy, fz = frame_of(0, 1)
    table = [pick_rows({0: fx, 1: fy, 2: fz}, (SUB, LANES))]
    frame8 = [gather_wide(table, wide(ix)) for ix in lane_pieces(elem_fibre[...])]
    corner = iota((CORNERS, LANES), 0)
    signs = [
        jnp.where((corner // (4 >> j)) % 2 == 1, 0.25, -0.25) for j in range(3)
    ]
    shear, bulk, scale = material[0], material[1], material[2]
    for h in range(elem_count // LANES):
        frame = [frame8[h][i : i + 1] for i in range(3)]
        d = [
            [
                sub_sum(disp[i][h] * signs[j]) + (1.0 if i == j else 0.0)
                for j in range(3)
            ]
            for i in range(3)
        ]
        cof = [
            [
                d[(i + 1) % 3][(j + 1) % 3] * d[(i + 2) % 3][(j + 2) % 3]
                - d[(i + 1) % 3][(j + 2) % 3] * d[(i + 2) % 3][(j + 1) % 3]
                for j in range(3)
            ]
            for i in range(3)
        ]
        volume = d[0][0] * cof[0][0] + d[0][1] * cof[0][1] + d[0][2] * cof[0][2]
        reciprocal = 1.0 / volume
        logv = jnp.log(volume)
        stress = [
            [
                shear * (d[i][j] - cof[i][j] * reciprocal)
                + bulk * logv * (cof[i][j] * reciprocal)
                for j in range(3)
            ]
            for i in range(3)
        ]
        stretch = [
            scale * (d[i][0] * frame[0] + d[i][1] * frame[1] + d[i][2] * frame[2])
            for i in range(3)
        ]
        along = sum(wide(frame[j]) * signs[j] for j in range(3))
        cut = slice(h * LANES, (h + 1) * LANES)
        for i in range(3):
            forces_out[i, :, cut] = sum(wide(stress[i][j]) * signs[j] for j in range(3))
            forces_out[3 + i, :, cut] = wide(stretch[i]) * along

    found = jnp.zeros((CORNERS, node_count), f32)
    lane_e = (iota((CORNERS, elem_count), 1) + 1).astype(f32)
    for q in range(CORNERS):
        named = onehot(iota((node_count, elem_count), 0) == nodes[q : q + 1, :])
        mine = jnp.where(iota((CORNERS, elem_count), 0) == q, lane_e, 0.0).astype(bf16)
        found = found + mm(mine, named, NT)
    inverse[...] = found.astype(i32) - 1

    receive(0)
    receive_coef()
    diffuse(0)

    pulls = []
    for t in range(tiles):
        where = pl.ds(t * TLX * ny // SUB, TLX * ny // SUB)
        calcium = calcium_of(out[NSTATE - 1, where], out[0, where], t)
        out[NSTATE - 1, where] = calcium
        square = calcium * calcium
        pulls.append(square / (square + tension_half))
    pull = jnp.concatenate(pulls, 0).reshape(bx, SBX, ny, nz)
    pull = (pull[:, 0] + pull[:, 1]).reshape(bx * ny, nz)
    strip = onehot(iota((SUB, nz), 1) // SBZ == iota((SUB, nz), 0))
    high = pull.astype(bf16)
    rest = (pull - high.astype(f32)).astype(bf16)
    pooled = mm(strip, high, NT) + mm(strip, rest, NT)
    lanes_p = bx * ny
    value = (pooled + pltpu.roll(pooled, lanes_p - 1, 1)) * weights
    even = iota((1, lanes_p), 1) % 2 == 0
    odd_value = pltpu.roll(value, 1, 1)
    tables = [
        wide(jnp.where(even, value[b : b + 1], odd_value[b + 1 : b + 2]))
        for b in range(0, bz, 2)
    ]
    value_rows = []
    for r in range(0, n, SUB):
        where = slot_pos[r : r + SUB]
        value_rows.append(
            jnp.where(where >= 0, gather_wide(tables, jnp.maximum(where, 0)), 0.0)
        )

    all_wait(0, ids_send, ids_got)
    asked = row_totals(ids_got, per_row, 0)
    asked_wide = [wide(row) for row in asked]
    place = iota((SUB, LANES), 1)
    which = place % ROWS
    for g in range(slot_groups):
        device_at = g * per_group + place // ROWS
        rows_out = []
        for seat in range(seats):
            source = (device_at % per_row) * seats + seat
            where = None
            for r in range(g * per_group // per_row, -(-(g + 1) * per_group // per_row)):
                found = lane_gather(asked_wide[r], source)
                where = (
                    found if where is None else jnp.where(device_at // per_row == r, found, where)
                )
            where = jnp.maximum(where.astype(i32) - 1, 0)
            low, high = where % LANES, where // LANES
            value = None
            for c in range(3):
                for h in range(elem_count // LANES):
                    found = lane_gather(disp[c][h], low)
                    value = (
                        found
                        if value is None
                        else jnp.where((which == c) & (high == h), found, value)
                    )
            rows_out.append(value)
        rows_out += [jnp.zeros((SUB, LANES), f32)] * (LANES // SUB - seats)
        answer = jnp.transpose(jnp.concatenate(rows_out, 0))
        ans_send[g * per_group : (g + 1) * per_group] = answer.reshape(per_group, ROWS, LANES)
    for r in range(0, n, SUB):
        ans_send[r : r + SUB, 3:4] = value_rows[r // SUB].reshape(SUB, 1, LANES)
    all_start(1, ans_send, ans_got)
    over_chunks(ionic_between)
    prepare(1)
    send(1)
    over_chunks(ionic_after)

    code = jnp.zeros((LANES, elem_count), f32)
    ident = (iota((LANES, elem_count), 1) + 1).astype(f32)
    row = iota((LANES, elem_count), 0).astype(f32)
    column = jnp.transpose(
        jnp.concatenate(asked + [jnp.zeros((LANES - slot_rows, LANES), f32)], 0)
    )
    for r in range(slot_rows):
        code = jnp.where(column[:, r : r + 1] == ident, row + float(r * LANES), code)
    wanted_out[2:3] = sub_sum(code).astype(i32)

    receive(1)
    diffuse(1)

    all_wait(1, ans_send, ans_got)
    answers_out[...] = ans_got[...]


def write_out(
    seats,
    states,
    answers,
    wanted,
    inverse,
    forces,
    states_out,
    fine_out,
    resid_out,
    fine,
    resid,
    sems,
):
    n = answers.shape[0]
    nx, ny, nz = fine.shape[1:]
    bx, by, bz = nx // SBX, ny // SBY, nz // SBZ
    plane = bx * by
    blocks = plane * bz
    per_group = LANES // ROWS
    slot_groups = n // per_group
    elem_count = forces.shape[2]
    copies = [
        pltpu.make_async_copy(states, states_out, sems.at[0]),
        pltpu.make_async_copy(resid, resid_out, sems.at[1]),
    ]
    copies[0].start()

    def fine_copy(i):
        here = pl.ds(i * nx // PIECES, nx // PIECES)
        return pltpu.make_async_copy(fine.at[:, here], fine_out.at[:, here], sems.at[2 + i])

    tables = [wide(row) for row in row_totals(answers, LANES // seats, 3)]
    tension = [gather_wide(tables, wide(ix)) for ix in lane_pieces(wanted[2:3])]
    force = [
        [
            forces[i, :, h * LANES : (h + 1) * LANES]
            + tension[h] * forces[3 + i, :, h * LANES : (h + 1) * LANES]
            for h in range(elem_count // LANES)
        ]
        for i in range(3)
    ]
    for g in range(0, inverse.shape[1], LANES):
        where = inverse[:, g : g + LANES]
        index = jnp.maximum(where, 0)
        for i in range(3):
            got = jnp.where(where >= 0, gather_wide(force[i], index), 0.0)
            resid[i : i + 1, g : g + LANES] = sub_sum(got)
    copies[1].start()

    columns = [
        jnp.transpose(answers[g * per_group : (g + 1) * per_group].reshape(LANES, LANES))
        for g in range(slot_groups)
    ]
    span = 32
    halves = []
    for h in range(blocks // LANES):
        cut = slice(h * LANES, (h + 1) * LANES)
        owner, rank = wide(wanted[0:1, cut]), wide(wanted[1:2, cut])
        rows_in = []
        for c in range(3):
            value = None
            for seat in range(seats):
                pieces = [col[seat * SUB : (seat + 1) * SUB] for col in columns]
                found = gather_wide(pieces, owner * ROWS + c)
                value = found if value is None else jnp.where(rank == seat, found, value)
            value = 0.75 * value + 0.25 * pltpu.roll(value, 4, 0)
            swapped = jnp.where(
                iota((SUB, LANES), 0) // 2 % 2 == 1,
                pltpu.roll(value, 2, 0),
                pltpu.roll(value, SUB - 2, 0),
            )
            rows_in.append(0.75 * value + 0.25 * swapped)
        rows_in.append(jnp.zeros((SUB, LANES), f32))
        halves.append(jnp.concatenate(rows_in, 0))
    stacked = []
    for b in range(bz):
        lane0 = b * plane
        piece = halves[lane0 // LANES]
        stacked.append(
            pltpu.roll(piece, LANES - lane0 % LANES, 1) if lane0 % LANES else piece
        )
    around = jnp.transpose(jnp.concatenate(stacked, 0))
    lane = iota((SUB, nz), 1)
    strip_lane = lane // SBZ * span
    xi = ((lane % SBZ).astype(f32) + 0.5) / SBZ
    for p in range(bx):
        near = around[p * by : (p + 1) * by]
        for c in range(3):
            for iv in range(SBX):
                for jv in range(SBY):
                    first = c * SUB + 4 * iv + 2 * jv
                    low = lane_gather(near, strip_lane + first)
                    high = lane_gather(near, strip_lane + first + 1)
                    fine[c, SBX * p + iv, pl.ds(jv, by, stride=SBY), :] = (
                        low + (high - low) * xi
                    )
        if (p + 1) % (bx // PIECES) == 0:
            fine_copy(p // (bx // PIECES)).start()
    for i in range(PIECES):
        fine_copy(i).wait()
    for c in copies:
        c.wait()


def shards(
    states,
    active,
    fibre_index,
    fibre_angle,
    conduct,
    gate_half,
    gate_slope,
    gate_tau,
    conductance,
    reversal,
    block_elem,
    block_weight,
    node_disp,
    elem_node,
    elem_fibre,
    material,
):
    mx, my, mz = (lax.axis_size(a) for a in AXES)
    n = mx * my * mz
    elem_count = elem_node.shape[1]
    node_count = node_disp.shape[1]
    nx, ny, nz = states.shape[1:]
    bx, by, bz = block_elem.shape
    blocks = bx * by * bz
    seats = max(2 * blocks // n, 8)
    tiles = nx // TLX
    strips = nx * ny // SUB
    ids = block_elem.transpose(0, 2, 1)
    weight = block_weight.transpose(0, 2, 1)
    vmem = pl.BlockSpec(memory_space=pltpu.VMEM)
    hbm = pl.BlockSpec(memory_space=pltpu.HBM)
    gates_n = NSTATE - 2
    halo_floats = 4 * (nx + ny + 1) * nz + 12 * nx * ny
    operands = (
        states.reshape(NSTATE, strips, SUB, nz),
        active.transpose(1, 2, 0),
        fibre_index.transpose(1, 2, 0),
        fibre_angle,
        fibre_angle,
        conduct,
        gate_half,
        gate_slope,
        gate_tau,
        conductance,
        reversal,
        ids,
        weight,
        node_disp,
        elem_node,
        elem_fibre.reshape(1, elem_count),
        material,
    )
    stage = FINE_STEPS
    states_shape = jax.ShapeDtypeStruct((NSTATE, strips, SUB, nz), f32)
    fine_shape = jax.ShapeDtypeStruct((3, nx, ny, nz), f32)
    resid_shape = jax.ShapeDtypeStruct((3, node_count), f32)
    in_smem = [True] * 3 + [False] + [True] * 6 + [False] * 5 + [True]
    results = pl.pallas_call(
        functools.partial(body, (mx, my, mz, seats, nx, ny)),
        out_shape=(
            states_shape,
            jax.ShapeDtypeStruct((n, ROWS, LANES), f32),
            jax.ShapeDtypeStruct((3, blocks), i32),
            jax.ShapeDtypeStruct((CORNERS, node_count), i32),
            jax.ShapeDtypeStruct((6, CORNERS, elem_count), f32),
        ),
        in_specs=[hbm] * len(operands),
        out_specs=(vmem,) * 5,
        scratch_shapes=[
            (pltpu.SMEM if scalar else pltpu.VMEM)(x.shape, x.dtype)
            for scalar, x in zip(in_smem, operands[1:])
        ]
        + [
            pltpu.VMEM((NSTATE, strips, SUB, nz), f32),
            pltpu.VMEM((stage, nx * ny, nz), f32),
            pltpu.VMEM((3, nx, ny, nz), f32),
            pltpu.VMEM((gates_n, 2, SUB, LANES), f32),
            pltpu.VMEM((tiles, gates_n, 6, SUB, LANES), f32),
            pltpu.VMEM((2, strips, SUB, nz), f32),
            pltpu.VMEM((gates_n, strips, SUB, nz), f32),
            pltpu.VMEM((tiles * SUB, LANES), f32),
            pltpu.VMEM((stage, 2, 2, nx, nz), f32),
            pltpu.VMEM((stage, 2, 2, nx * ny), f32),
            pltpu.VMEM((stage, 4, 1, nz), f32),
            pltpu.VMEM((stage, 2, 1, nx * ny), f32),
            pltpu.VMEM((stage, 4, 2 * ny, nz), f32),
            pltpu.VMEM((stage, 4, 2, nx, nz), f32),
            pltpu.VMEM((stage, 4, 2, nx * ny), f32),
            pltpu.VMEM((stage, 8, 1, nz), f32),
            pltpu.VMEM((stage, 8, 1, nx * ny), f32),
            pltpu.VMEM((stage, 8, 1, nx * ny), f32),
            pltpu.VMEM((12, tiles * SUB, LANES), f32),
            pltpu.VMEM((halo_floats // LANES, 1, LANES), f32),
            pltpu.VMEM((nx * ny, nz), f32),
            pltpu.VMEM((n, LANES), i32),
            pltpu.VMEM((n, 1, LANES), f32),
            pltpu.VMEM((n, 1, LANES), f32),
            pltpu.VMEM((n, ROWS, LANES), f32),
            pltpu.VMEM((n, ROWS, LANES), f32),
            pltpu.SemaphoreType.DMA((2 * tiles,)),
            pltpu.SemaphoreType.DMA((len(operands) - 1,)),
            pltpu.SemaphoreType.DMA((stage,)),
            pltpu.SemaphoreType.DMA((stage,)),
            pltpu.SemaphoreType.DMA,
            pltpu.SemaphoreType.DMA,
            pltpu.SemaphoreType.DMA((2,)),
            pltpu.SemaphoreType.DMA((2,)),
        ],
        compiler_params=pltpu.CompilerParams(
            collective_id=0, has_side_effects=True, vmem_limit_bytes=20 * 1024 * 1024
        ),
        name="step",
    )(*(pltpu.with_memory_space_constraint(a, pltpu.HBM) for a in operands))
    results = pl.pallas_call(
        functools.partial(write_out, seats),
        out_shape=(states_shape, fine_shape, resid_shape),
        in_specs=[vmem] * 5,
        out_specs=(hbm,) * 3,
        scratch_shapes=[
            pltpu.VMEM((3, nx, ny, nz), f32),
            pltpu.VMEM((3, node_count), f32),
            pltpu.SemaphoreType.DMA((2 + PIECES,)),
        ],
        compiler_params=pltpu.CompilerParams(vmem_limit_bytes=20 * 1024 * 1024),
        name="write",
    )(*results)
    return results[0].reshape(states.shape), results[1], results[2]


def solution(mesh):
    in_specs = (
        P(None, "gx", "gy", "gz"),
        P("gx", "gy", "gz"),
        P("gx", "gy", "gz"),
        P(),
        P(),
        P(),
        P(),
        P(),
        P(),
        P(),
        P("gx", "gy", "gz"),
        P("gx", "gy", "gz"),
        P(None, ("gx", "gy", "gz")),
        P(None, ("gx", "gy", "gz")),
        P(("gx", "gy", "gz")),
        P(),
    )
    out_specs = (P(None, "gx", "gy", "gz"), P(None, "gx", "gy", "gz"), P(None, ("gx", "gy", "gz")))
    return jax.shard_map(shards, mesh=mesh, in_specs=in_specs, out_specs=out_specs, check_vma=False)
```

```python
import functools

import jax
import jax.numpy as jnp
from jax import lax
from jax.experimental import pallas as pl
from jax.experimental.pallas import tpu as pltpu
from jax.sharding import PartitionSpec as P

NSTATE = 19
TLX = 8
SBX = 2
SBY = 2
SBZ = 32
FINE_STEPS = 2
AXES = ("gx", "gy", "gz")
MESH = pl.DeviceIdType.MESH
LANES = 128
SUB = 8
CORNERS = 8
GROUPS = 4
SPAN = 32
PIECES = 4
f32 = jnp.float32
bf16 = jnp.bfloat16
i32 = jnp.int32
calcium_keep = 0.9
tension_half = 0.09
NN = (((1,), (0,)), ((), ()))
NT = (((1,), (1,)), ((), ()))
DIRS = (
    [tuple(side if d == dim else 0 for d in range(3)) for dim in range(3) for side in (-1, 1)]
    + [(a, b, 0) for a in (-1, 1) for b in (-1, 1)]
    + [(a, 0, b) for a in (-1, 1) for b in (-1, 1)]
    + [(0, a, b) for a in (-1, 1) for b in (-1, 1)]
)
OPPOSITE = [DIRS.index(tuple(-c for c in d)) for d in DIRS]


def mm(a, b, dims=NN):
    return lax.dot_general(a, b, dims, preferred_element_type=f32)


def parts(x, count):
    out = []
    for _ in range(count):
        out.append(x.astype(bf16).astype(f32))
        x = x - out[-1]
    return out


def iota(shape, dim):
    return lax.broadcasted_iota(i32, shape, dim)


def onehot(mask):
    return jnp.where(mask, 1.0, 0.0).astype(bf16)


def pick_rows(rows, shape):
    index = iota(shape, 0)
    out = jnp.zeros(shape, f32)
    for i, row in rows.items():
        out = jnp.where(index == i, row, out)
    return out


def lane_gather(x, index):
    return jnp.take_along_axis(x, index, axis=1, mode="promise_in_bounds")


def wide(row, rows=SUB):
    return jnp.broadcast_to(row, (rows, row.shape[1]))


def gather_wide(tables, index):
    low, high = index % LANES, index // LANES
    out = lane_gather(tables[0], low)
    for h in range(1, len(tables)):
        out = jnp.where(high == h, lane_gather(tables[h], low), out)
    return out


def lane_pieces(x):
    return [x[:, h : h + LANES] for h in range(0, x.shape[1], LANES)]


def sub_sum(x):
    return jnp.sum(x, axis=0, keepdims=True)


def body(
    sizes,
    *refs,
):
    mx, my, mz, seats, nx, ny = sizes
    operands, refs = refs[:17], refs[17:]
    states = operands[0]
    out, answers_out, wanted_out, inverse, forces_out = refs[:5]
    small, refs = refs[5:21], refs[21:]
    (
        active,
        fibre_index,
        angle_s,
        angle_v,
        conduct,
        gate_half,
        gate_slope,
        gate_tau,
        conductance,
        reversal,
        ids_ref,
        weight_ref,
        node_disp,
        elem_node,
        elem_fibre,
        material,
    ) = small
    (
        held,
        vs,
        flux,
        gate_const,
        tile_const,
        sums,
        bends,
        mine_coef,
        send_y,
        send_z,
        send_xy,
        send_row,
        halo_x,
        halo_y,
        halo_z,
        edge_xy,
        edge_xz,
        edge_yz,
        halo_coef,
        tally,
        turned,
        slot_pos,
        ids_send,
        ids_got,
        ans_send,
        ans_got,
        load_sem,
        small_sem,
        face_send_sem,
        face_recv_sem,
        coef_send_sem,
        coef_recv_sem,
        all_send_sem,
        all_recv_sem,
    ) = refs
    nz = states.shape[3]
    n = mx * my * mz
    gates_n = NSTATE - 2
    strips = nx * ny // SUB
    bx, by, bz = nx // SBX, ny // SBY, nz // SBZ
    plane = bx * by
    blocks = plane * bz
    tiles = nx // TLX
    node_count = node_disp.shape[1]
    elem_count = elem_node.shape[1]
    rows_each = seats // GROUPS
    per_group = LANES // rows_each
    slot_groups = n // per_group
    per_row = LANES // seats
    slot_rows = n // per_row
    cx, cy, cz = (lax.axis_index(a) for a in AXES)
    me = (cx * my + cy) * mz + cz
    at = (cx, cy, cz)
    counts = (mx, my, mz)

    def others():
        steps = [
            (a, b, c) for a in range(mx) for b in range(my) for c in range(mz) if a or b or c
        ]

        def far(step):
            return sum(
                (1 if d == 1 else max(s, m - s)) if s else 0
                for d, (s, m) in enumerate(zip(step, counts))
            )

        return sorted(steps, key=far, reverse=True)

    wrapped = [[jnp.where(p + s >= m, p + s - m, p + s) for s in range(m)] for p, m in zip(at, counts)]

    def each_other(go):
        if n <= 64:
            for step in others():
                go(tuple(wrapped[d][s] for d, s in enumerate(step)))
        else:

            def one(k, carry):
                flat = (me + k) % n
                go((flat // (my * mz), (flat // mz) % my, flat % mz))
                return carry

            lax.fori_loop(1, n, one, 0)

    chunk = TLX * ny // SUB // 2

    def load(i):
        here = pl.ds(i * chunk, chunk)
        return pltpu.make_async_copy(states.at[:, here], held.at[:, here], load_sem.at[i])

    for ref in (halo_x, halo_y, halo_z, edge_xy, edge_xz, edge_yz):
        used = ref.shape[1] // 2
        ref[:, :used] = jnp.zeros((ref.shape[0], used) + ref.shape[2:], f32)
    halo_coef[:6] = jnp.zeros((6,) + halo_coef.shape[1:], f32)

    barrier = pltpu.get_barrier_semaphore()
    each_other(
        lambda to: pl.semaphore_signal(barrier, inc=1, device_id=to, device_id_type=MESH)
    )

    small_loads = [
        pltpu.make_async_copy(src, dst, small_sem.at[i])
        for i, (src, dst) in enumerate(zip(operands[1:], small))
    ]
    for c in small_loads:
        c.start()
    for i in range(strips // chunk):
        load(i).start()

    for c in small_loads:
        c.wait()

    def splat(value):
        return jnp.full((SUB, LANES), value, f32)

    angles = jnp.concatenate(
        [angle_v[...], jnp.zeros((2, LANES - angle_v.shape[1]), f32)], 1
    ) if angle_v.shape[1] < LANES else angle_v[...]
    rows = {0: angles[0:1], 1: angles[1:2]}
    across, spread, alive = [], [], []
    for t in range(tiles):
        index = fibre_index[0, 0, t]
        rows[2 + t] = jnp.full((1, LANES), angle_s[0, index], f32)
        rows[2 + tiles + t] = jnp.full((1, LANES), angle_s[1, index], f32)
        across.append(jnp.full((1, LANES), conduct[1, index], f32))
        spread.append(jnp.full((1, LANES), conduct[0, index], f32) - across[t])
        alive.append(jnp.where(active[0, 0, t] > 0, 1.0, 0.0).astype(f32))
    stack = pick_rows(rows, (SUB, LANES))
    cosine, sine = jnp.cos(stack), jnp.sin(stack)

    def frame_of(a, b):
        ca, sa = cosine[a : a + 1], sine[a : a + 1]
        cb, sb = cosine[b : b + 1], sine[b : b + 1]
        return ca * cb, sa * cb, sb

    for t in range(tiles):
        fx, fy, fz = frame_of(2 + t, 2 + tiles + t)
        scale = alive[t] * 0.25
        entries = [
            across[t] + spread[t] * fx * fx,
            across[t] + spread[t] * fy * fy,
            across[t] + spread[t] * fz * fz,
            spread[t] * fx * fy,
            spread[t] * fx * fz,
            spread[t] * fy * fz,
        ]
        mine_coef[t * SUB : (t + 1) * SUB] = pick_rows(
            {k: e * scale for k, e in enumerate(entries)}, (SUB, LANES)
        )

    for g in range(gates_n):
        slope = 0.5 / splat(gate_slope[g])
        gate_const[g, 0] = slope
        gate_const[g, 1] = slope * gate_half[g]
        keep = jnp.exp(-1.0 / splat(gate_tau[g]))
        share = 0.5 * (1.0 - keep)
        cond = splat(conductance[g])
        for t in range(tiles):
            live = splat(alive[t]) > 0.5
            tile_const[t, g, 0] = jnp.where(live, keep, 1.0)
            tile_const[t, g, 1] = jnp.where(live, share, 0.0)
            tile_const[t, g, 2] = jnp.where(live, cond, 0.0)
            pull = cond * reversal[g]
            tile_const[t, g, 3] = jnp.where(live, pull, 0.0)
            tile_const[t, g, 4] = jnp.where(live, cond * share, 0.0)
            tile_const[t, g, 5] = jnp.where(live, pull * share, 0.0)

    def live_calcium(t):
        live = splat(alive[t]) > 0.5
        keep = jnp.where(live, calcium_keep, 1.0)
        share = jnp.where(live, 0.5 * (1.0 - calcium_keep), 0.0)
        return keep, share

    def calcium_of(old, volt, t):
        keep, share = live_calcium(t)
        return old * keep + (jnp.tanh(4.0 * volt - 2.0) * share + share)

    def ionic(i, t):
        where = pl.ds(i * chunk, chunk)
        volt = held[0, where]
        total = jnp.zeros_like(volt)
        shift = jnp.zeros_like(volt)
        for g in range(gates_n):
            bend = jnp.tanh(volt * gate_const[g, 0] - gate_const[g, 1])
            share = tile_const[t, g, 1]
            gate = held[1 + g, where] * tile_const[t, g, 0] + (bend * share + share)
            out[1 + g, where] = gate
            total = total + gate * tile_const[t, g, 2]
            shift = shift + gate * tile_const[t, g, 3]
        star = volt - (volt * total - shift)
        vs[0, pl.ds(i * chunk * SUB, chunk * SUB)] = star.reshape(chunk * SUB, LANES)

    def ionic_before(i, t):
        where = pl.ds(i * chunk, chunk)
        total = jnp.zeros((chunk, SUB, LANES), f32)
        shift = jnp.zeros((chunk, SUB, LANES), f32)
        for g in range(gates_n):
            kept = out[1 + g, where] * tile_const[t, g, 0] + tile_const[t, g, 1]
            out[1 + g, where] = kept
            total = total + kept * tile_const[t, g, 2]
            shift = shift + kept * tile_const[t, g, 3]
        sums[0, where] = total
        sums[1, where] = shift

    def ionic_between(i, t):
        where = pl.ds(i * chunk, chunk)
        volt = out[0, where]
        total = sums[0, where]
        shift = sums[1, where]
        for g in range(gates_n):
            bend = jnp.tanh(volt * gate_const[g, 0] - gate_const[g, 1])
            bends[g, where] = bend
            total = total + bend * tile_const[t, g, 4]
            shift = shift + bend * tile_const[t, g, 5]
        star = volt - (volt * total - shift)
        vs[1, pl.ds(i * chunk * SUB, chunk * SUB)] = star.reshape(chunk * SUB, LANES)

    def ionic_after(i, t):
        where = pl.ds(i * chunk, chunk)
        for g in range(gates_n):
            out[1 + g, where] = out[1 + g, where] + bends[g, where] * tile_const[t, g, 1]

    def over_chunks(step):
        for t in range(tiles):

            def go(i, carry, t=t):
                step(i, t)
                return carry

            lax.fori_loop(2 * t, 2 * t + 2, go, 0)

    flat_in = (bx * bz, by)
    raw = jnp.concatenate(
        parts(ids_ref[...].astype(f32).reshape(flat_in), 3), 0
    ).astype(bf16)
    lane_b = iota((by, blocks), 1)
    put = onehot(lane_b % by == iota((by, blocks), 0))
    spread_ids = mm(raw, put)
    part = bx * bz
    spread_ids = spread_ids[:part] + spread_ids[part : 2 * part] + spread_ids[2 * part :]
    row_b, col_b = iota((part, blocks), 0), iota((part, blocks), 1)
    here = (row_b // bz == (col_b % plane) // by) & (row_b % bz == col_b // plane)
    ids = sub_sum(jnp.where(here, spread_ids, 0.0)).astype(i32)
    shift = elem_count.bit_length() - 1
    owner = lax.shift_right_logical(ids, shift)
    local = ids - owner * elem_count
    owned = onehot(owner == iota((n, blocks), 0))
    before = onehot(iota((blocks, blocks), 0) < iota((blocks, blocks), 1))
    seen = mm(owned, before)
    rank = sub_sum(owned.astype(f32) * seen).astype(i32)
    offset = (me % per_row) * seats
    hit = owner == iota((n, blocks), 0)
    place = onehot(iota((LANES, blocks), 0) == rank + offset)
    sent = mm(jnp.where(hit, (local + 1).astype(f32), 0.0).astype(bf16), place, NT)
    ids_send[...] = sent.reshape(n, 1, LANES)
    group, seat_row = rank % GROUPS, rank // GROUPS
    number = jnp.where(
        group == iota((SUB, blocks), 0), (iota((SUB, blocks), 1) + 1).astype(f32), 0.0
    ).astype(bf16)
    seat_place = owner * rows_each + seat_row
    for g in range(slot_groups):
        block_at = (
            mm(number, onehot(iota((LANES, blocks), 0) + g * LANES == seat_place), NT).astype(i32)
            - 1
        )
        in_plane = block_at % plane
        slot_pos[g] = jnp.where(
            block_at >= 0,
            (block_at // plane // 2) * LANES
            + (in_plane // by) * ny
            + (in_plane % by) * SBY
            + (block_at // plane) % 2,
            -1,
        )
    wanted_out[0:1] = seat_place
    wanted_out[1:2] = group

    raw = jnp.concatenate(parts(weight_ref[...].reshape(flat_in), 2), 0).astype(bf16)
    put = onehot(iota((by, bx * ny), 1) % ny == iota((by, bx * ny), 0) * SBY)
    spread_w = mm(raw, put)
    spread_w = (spread_w[:part] + spread_w[part:]).reshape(bx, bz, bx * ny)
    here = iota((bx, bz, bx * ny), 0) == iota((bx, bz, bx * ny), 2) // ny
    weights = jnp.sum(jnp.where(here, spread_w, 0.0), axis=0)
    weights = jnp.concatenate([weights, jnp.zeros((SUB - bz, bx * ny), f32)], 0)
    weights = weights * (1.0 / (SBX * SBY * SBZ))

    def first(i, t):
        load(i).wait()
        ionic(i, t)
        here = pl.ds(i * chunk, chunk)
        out[NSTATE - 1, here] = calcium_of(held[NSTATE - 1, here], held[0, here], t)

    over_chunks(first)

    def source_of(stage, i):
        d = DIRS[i]
        if i < 2:
            return vs.at[stage, pl.ds(0 if d[0] < 0 else (nx - 2) * ny, 2 * ny)]
        if i < 4:
            return send_y.at[stage, i - 2]
        if i < 6:
            return send_z.at[stage, i - 4]
        if i < 10:
            return send_xy.at[stage, i - 6]
        return send_row.at[stage, 0 if d[2] < 0 else 1]

    families = (
        [(halo_x, 0, 2), (halo_y, 2, 2), (halo_z, 4, 2)]
        + [(edge_xy, 6, 4), (edge_xz, 10, 4), (edge_yz, 14, 4)]
    )

    def exists(i):
        ok = None
        for p, step, m in zip(at, DIRS[i], counts):
            if step:
                inside = p > 0 if step < 0 else p < m - 1
                ok = inside if ok is None else ok & inside
        return ok

    def route(i):
        ok = exists(i)
        swap = next(d for d in (1, 0, 2) if DIRS[i][d] == 0)
        to = []
        for d, (p, step) in enumerate(zip(at, DIRS[i])):
            if step:
                p = jnp.where(ok, p + step, p)
            elif d == swap:
                p = jnp.where(ok, p, p + 1 - 2 * (p % 2))
            to.append(p)
        return tuple(to), ok

    order = list(range(len(DIRS) - 1, -1, -1))

    def prepare(stage):
        for side in range(2):
            for layer in range(2):
                y = layer if side == 0 else ny - 2 + layer
                send_y[stage, side, layer] = vs[stage, pl.ds(y, nx, stride=ny), :]
        for a in range(2):
            for b in range(2):
                row = (nx - 1) * a * ny + (ny - 1) * b
                send_xy[stage, 2 * a + b] = vs[stage, row : row + 1, :]
        columns = jnp.transpose(vs[stage])
        send_z[stage, 0] = columns[0:2]
        send_z[stage, 1] = columns[nz - 2 : nz]
        send_row[stage, 0] = columns[0:1]
        send_row[stage, 1] = columns[nz - 1 : nz]

    def send(stage):
        for i in order:
            ref, first, count = next(f for f in families if f[1] <= i < f[1] + f[2])
            to, ok = route(i)
            slot = jnp.where(ok, OPPOSITE[i] - first, count + i - first)
            pltpu.make_async_remote_copy(
                src_ref=source_of(stage, i),
                dst_ref=ref.at[stage, slot],
                send_sem=face_send_sem.at[stage],
                recv_sem=face_recv_sem.at[stage],
                device_id=to,
                device_id_type=MESH,
            ).start()

    def receive(stage):
        pltpu.make_async_remote_copy(
            src_ref=tally,
            dst_ref=tally,
            send_sem=face_send_sem.at[stage],
            recv_sem=face_recv_sem.at[stage],
            device_id=at,
            device_id_type=MESH,
        ).wait()

    def send_coef():
        for i in range(6):
            to, ok = route(i)
            pltpu.make_async_remote_copy(
                src_ref=mine_coef,
                dst_ref=halo_coef.at[jnp.where(ok, OPPOSITE[i], 6 + i)],
                send_sem=coef_send_sem,
                recv_sem=coef_recv_sem,
                device_id=to,
                device_id_type=MESH,
            ).start()

    def receive_coef():
        pltpu.make_async_remote_copy(
            src_ref=halo_coef.at[pl.ds(0, 6)],
            dst_ref=halo_coef.at[pl.ds(0, 6)],
            send_sem=coef_send_sem,
            recv_sem=coef_recv_sem,
            device_id=at,
            device_id_type=MESH,
        ).wait()

    def all_start(kind, src, dst):
        dst[pl.ds(me, 1)] = src[pl.ds(me, 1)]

        def go(to):
            flat = (to[0] * my + to[1]) * mz + to[2]
            pltpu.make_async_remote_copy(
                src_ref=src.at[flat],
                dst_ref=dst.at[me],
                send_sem=all_send_sem.at[kind],
                recv_sem=all_recv_sem.at[kind],
                device_id=to,
                device_id_type=MESH,
            ).start()

        each_other(go)

    def all_wait(kind, src, dst):
        pltpu.make_async_remote_copy(
            src_ref=src.at[pl.ds(0, n - 1)],
            dst_ref=dst.at[pl.ds(0, n - 1)],
            send_sem=all_send_sem.at[kind],
            recv_sem=all_recv_sem.at[kind],
            device_id=at,
            device_id_type=MESH,
        ).wait()

    def coef_row(ref, t, k):
        return ref[t * SUB + k : t * SUB + k + 1, :]

    def diffuse(stage):
        v = vs[stage].reshape(nx, ny, nz)
        lane = iota((1, nz), 1)
        flat = nx * ny
        lane_f = iota((SUB, flat), 1)

        def both(low, high):
            return pick_rows({0: low, 1: high}, (SUB, flat))

        near = both(halo_z[stage, 0, 1:2], halo_z[stage, 1, 0:1])
        gz = both(
            send_row[stage, 0] - halo_z[stage, 0, 0:1],
            halo_z[stage, 1, 1:2] - send_row[stage, 1],
        )
        xz = [both(edge_xz[stage, 2 * a], edge_xz[stage, 2 * a + 1]) for a in range(2)]
        yz = [both(edge_yz[stage, 2 * a], edge_yz[stage, 2 * a + 1]) for a in range(2)]
        up = pltpu.roll(jnp.where(lane_f < ny, xz[1], near), flat - ny, 1)
        down = pltpu.roll(jnp.where(lane_f >= flat - ny, xz[0], near), ny, 1)
        gx = up - down
        up = jnp.where(
            lane_f % ny == ny - 1, pltpu.roll(yz[1], ny - 1, 1), pltpu.roll(near, flat - 1, 1)
        )
        down = jnp.where(
            lane_f % ny == 0, pltpu.roll(yz[0], flat - ny + 1, 1), pltpu.roll(near, 1, 1)
        )
        gy = up - down

        def coef_z(k):
            return both(
                *(
                    jnp.concatenate(
                        [coef_row(halo_coef.at[4 + s], t, k) for t in range(tiles)], 1
                    )
                    for s in range(2)
                )
            )

        fz = coef_z(4) * gx + coef_z(5) * gy + coef_z(2) * gz
        blank = jnp.zeros((SUB, flat), f32)
        half = nz // 2
        pieces = [blank] * (nz // SUB)
        pieces[0] = pick_rows(
            {0: near[0:1], **{1 + i: edge_xz[stage, i] for i in range(4)}}, (SUB, flat)
        )
        pieces[half // SUB - 1] = pick_rows({SUB - 1: fz[1:2]}, (SUB, flat))
        pieces[half // SUB] = pick_rows(
            {0: fz[0:1], **{1 + i: edge_yz[stage, i] for i in range(4)}}, (SUB, flat)
        )
        pieces[-1] = pick_rows({SUB - 1: near[1:2]}, (SUB, flat))
        turned[...] = jnp.transpose(jnp.concatenate(pieces, 0))

        def along_z(a, low, high):
            return jnp.where(lane == nz - 1, high, pltpu.roll(a, nz - 1, 1)) - jnp.where(
                lane == 0, low, pltpu.roll(a, 1, 1)
            )

        def along_rows(a, low, high):
            row = iota(a.shape, 0)
            m = a.shape[0]
            return jnp.where(row == m - 1, high, pltpu.roll(a, m - 1, 0)) - jnp.where(
                row == 0, low, pltpu.roll(a, 1, 0)
            )

        px, fx_out = [], []
        for s in range(2):
            close = halo_x[stage, s, ny:] if s == 0 else halo_x[stage, s, :ny]
            distant = halo_x[stage, s, :ny] if s == 0 else halo_x[stage, s, ny:]
            gx = v[0] - distant if s == 0 else distant - v[nx - 1]
            gy = along_rows(close, edge_xy[stage, 2 * s], edge_xy[stage, 2 * s + 1])
            first = (nx - 1) * ny if s == 0 else 0
            edge = turned[first : first + ny, :]
            c = 1 + 2 * s
            gz = along_z(close, edge[:, c : c + 1], edge[:, c + 1 : c + 2])
            t = tiles - 1 if s == 0 else 0
            k = [coef_row(halo_coef.at[s], t, j) for j in (0, 3, 4)]
            px.append(close)
            fx_out.append(k[0] * gx + k[1] * gy + k[2] * gz)
        py, fy_out = [], []
        for s in range(2):
            close, distant = halo_y[stage, s, 1 - s], halo_y[stage, s, s]
            own = vs[stage, pl.ds(0 if s == 0 else ny - 1, nx, stride=ny), :]
            gy = own - distant if s == 0 else distant - own
            gx = along_rows(close, edge_xy[stage, s], edge_xy[stage, 2 + s])
            edge = turned[pl.ds(ny - 1 if s == 0 else 0, nx, stride=ny), :]
            c = half + 1 + 2 * s
            gz = along_z(close, edge[:, c : c + 1], edge[:, c + 1 : c + 2])

            def coef_y(j, s=s):
                return jnp.concatenate(
                    [wide(coef_row(halo_coef.at[2 + s], t, j), TLX) for t in range(tiles)], 0
                )

            py.append(close)
            fy_out.append(coef_y(3) * gx + coef_y(1) * gy + coef_y(5) * gz)

        def diff_x(a, low, high):
            return jnp.concatenate([a[1:], high[None]], 0) - jnp.concatenate([low[None], a[:-1]], 0)

        def diff_y(a, low, high):
            row = iota((1, ny, nz), 1)
            up = jnp.where(row == ny - 1, high.reshape(nx, 1, nz), pltpu.roll(a, ny - 1, 1))
            down = jnp.where(row == 0, low.reshape(nx, 1, nz), pltpu.roll(a, 1, 1))
            return up - down

        def diff_z(a, edge):
            lane = iota((1, 1, nz), 2)
            up = jnp.where(lane == nz - 1, edge, pltpu.roll(a, nz - 1, 2))
            down = jnp.where(lane == 0, edge, pltpu.roll(a, 1, 2))
            return up - down

        edges = turned[...].reshape(nx, ny, nz)
        gx, gy, gz = diff_x(v, *px), diff_y(v, *py), diff_z(v, edges)
        for t in range(tiles):
            span = slice(t * TLX, (t + 1) * TLX)
            xx, yy, zz, xy, xz_, yz_ = (
                coef_row(mine_coef, t, k).reshape(1, 1, LANES) for k in range(6)
            )
            a, b, c = gx[span], gy[span], gz[span]
            flux[0, span] = xx * a + xy * b + xz_ * c
            flux[1, span] = xy * a + yy * b + yz_ * c
            flux[2, span] = xz_ * a + yz_ * b + zz * c
        edges = pltpu.roll(edges, half, 2)
        lap = (
            diff_x(flux[0], *fx_out)
            + diff_y(flux[1], *fy_out)
            + diff_z(flux[2], edges)
        )
        for t in range(tiles):
            span = slice(t * TLX, (t + 1) * TLX)
            new = v[span] + lap[span] * alive[t]
            where = pl.ds(t * TLX * ny // SUB, TLX * ny // SUB)
            out[0, where] = new.reshape(TLX * ny // SUB, SUB, LANES)

    prepare(0)
    pl.semaphore_wait(barrier, n - 1)
    all_start(0, ids_send, ids_got)
    send(0)
    send_coef()


    over_chunks(ionic_before)
    nodes = elem_node[...]
    disp = []
    for c in range(3):
        table = [
            wide(node_disp[c : c + 1, g : g + LANES]) for g in range(0, node_count, LANES)
        ]
        disp.append([gather_wide(table, ix) for ix in lane_pieces(nodes)])
    fx, fy, fz = frame_of(0, 1)
    table = [pick_rows({0: fx, 1: fy, 2: fz}, (SUB, LANES))]
    frame8 = [gather_wide(table, wide(ix)) for ix in lane_pieces(elem_fibre[...])]
    corner = iota((CORNERS, LANES), 0)
    signs = [
        jnp.where((corner // (4 >> j)) % 2 == 1, 0.25, -0.25) for j in range(3)
    ]
    shear, bulk, scale = material[0], material[1], material[2]
    for h in range(elem_count // LANES):
        frame = [frame8[h][i : i + 1] for i in range(3)]
        d = [
            [
                sub_sum(disp[i][h] * signs[j]) + (1.0 if i == j else 0.0)
                for j in range(3)
            ]
            for i in range(3)
        ]
        cof = [
            [
                d[(i + 1) % 3][(j + 1) % 3] * d[(i + 2) % 3][(j + 2) % 3]
                - d[(i + 1) % 3][(j + 2) % 3] * d[(i + 2) % 3][(j + 1) % 3]
                for j in range(3)
            ]
            for i in range(3)
        ]
        volume = d[0][0] * cof[0][0] + d[0][1] * cof[0][1] + d[0][2] * cof[0][2]
        reciprocal = 1.0 / volume
        logv = jnp.log(volume)
        stress = [
            [
                shear * (d[i][j] - cof[i][j] * reciprocal)
                + bulk * logv * (cof[i][j] * reciprocal)
                for j in range(3)
            ]
            for i in range(3)
        ]
        stretch = [
            scale * (d[i][0] * frame[0] + d[i][1] * frame[1] + d[i][2] * frame[2])
            for i in range(3)
        ]
        along = sum(wide(frame[j]) * signs[j] for j in range(3))
        cut = slice(h * LANES, (h + 1) * LANES)
        for i in range(3):
            forces_out[i, :, cut] = sum(wide(stress[i][j]) * signs[j] for j in range(3))
            forces_out[3 + i, :, cut] = wide(stretch[i]) * along

    found = jnp.zeros((CORNERS, node_count), f32)
    lane_e = (iota((CORNERS, elem_count), 1) + 1).astype(f32)
    for q in range(CORNERS):
        named = onehot(iota((node_count, elem_count), 0) == nodes[q : q + 1, :])
        mine = jnp.where(iota((CORNERS, elem_count), 0) == q, lane_e, 0.0).astype(bf16)
        found = found + mm(mine, named, NT)
    inverse[...] = found.astype(i32) - 1

    receive(0)
    receive_coef()
    diffuse(0)

    pulls = []
    for t in range(tiles):
        where = pl.ds(t * TLX * ny // SUB, TLX * ny // SUB)
        calcium = calcium_of(out[NSTATE - 1, where], out[0, where], t)
        out[NSTATE - 1, where] = calcium
        square = calcium * calcium
        pulls.append(square / (square + tension_half))
    pull = jnp.concatenate(pulls, 0).reshape(bx, SBX, ny, nz)
    pull = (pull[:, 0] + pull[:, 1]).reshape(bx * ny, nz)
    strip = onehot(iota((SUB, nz), 1) // SBZ == iota((SUB, nz), 0))
    high = pull.astype(bf16)
    rest = (pull - high.astype(f32)).astype(bf16)
    pooled = mm(strip, high, NT) + mm(strip, rest, NT)
    lanes_p = bx * ny
    value = (pooled + pltpu.roll(pooled, lanes_p - 1, 1)) * weights
    even = iota((1, lanes_p), 1) % 2 == 0
    odd_value = pltpu.roll(value, 1, 1)
    tables = [
        wide(jnp.where(even, value[b : b + 1], odd_value[b + 1 : b + 2]))
        for b in range(0, bz, 2)
    ]
    value_rows = []
    for g in range(slot_groups):
        where = slot_pos[g]
        value_rows.append(
            jnp.where(where >= 0, gather_wide(tables, jnp.maximum(where, 0)), 0.0)
        )

    all_wait(0, ids_send, ids_got)
    asked = []
    for r in range(0, n, per_row):
        total = ids_got[r]
        for m in range(1, per_row):
            total = total + ids_got[r + m]
        asked.append(total)
    asked_wide = [wide(row) for row in asked]
    place = iota((SUB, LANES), 1)
    for g in range(slot_groups):
        device_at = g * per_group + place // rows_each
        rows_out = []
        for k in range(GROUPS):
            source = (device_at % per_row) * seats + (place % rows_each) * GROUPS + k
            where = None
            for r in range(g * per_group // per_row, -(-(g + 1) * per_group // per_row)):
                found = lane_gather(asked_wide[r], source)
                where = (
                    found if where is None else jnp.where(device_at // per_row == r, found, where)
                )
            where = jnp.maximum(where.astype(i32) - 1, 0)
            rows_out += [gather_wide(disp[c], where) for c in range(3)]
            rows_out.append(wide(value_rows[g][k : k + 1]))
        answer = jnp.transpose(jnp.concatenate(rows_out, 0))
        ans_send[g * per_group : (g + 1) * per_group] = answer.reshape(
            per_group, rows_each, LANES
        )
    all_start(1, ans_send, ans_got)
    over_chunks(ionic_between)
    prepare(1)
    send(1)
    over_chunks(ionic_after)

    code = jnp.zeros((LANES, elem_count), f32)
    ident = (iota((LANES, elem_count), 1) + 1).astype(f32)
    row = iota((LANES, 1), 0)

    def arrival(lane, r):
        seat = lane % seats
        lane = (r * per_row + lane // seats) * rows_each + seat // GROUPS
        return ((lane // LANES * GROUPS + seat % GROUPS) * LANES + lane % LANES).astype(f32)

    column = jnp.transpose(
        jnp.concatenate(asked + [jnp.zeros((LANES - slot_rows, LANES), f32)], 0)
    )
    for r in range(slot_rows):
        code = jnp.where(column[:, r : r + 1] == ident, arrival(row, r), code)
    wanted_out[2:3] = sub_sum(code).astype(i32)

    receive(1)
    diffuse(1)

    all_wait(1, ans_send, ans_got)
    answers_out[...] = ans_got[...]


def write_out(
    states,
    answers,
    wanted,
    inverse,
    forces,
    states_out,
    fine_out,
    resid_out,
    fine,
    resid,
    sems,
):
    n, rows_each = answers.shape[:2]
    nx, ny, nz = fine.shape[1:]
    bx, by, bz = nx // SBX, ny // SBY, nz // SBZ
    plane = bx * by
    blocks = plane * bz
    per_group = LANES // rows_each
    slot_groups = n // per_group
    elem_count = forces.shape[2]
    copies = [
        pltpu.make_async_copy(states, states_out, sems.at[0]),
        pltpu.make_async_copy(resid, resid_out, sems.at[1]),
    ]
    copies[0].start()

    def fine_copy(i):
        here = pl.ds(i * nx // PIECES, nx // PIECES)
        return pltpu.make_async_copy(fine.at[:, here], fine_out.at[:, here], sems.at[2 + i])

    columns = [
        jnp.transpose(answers[g * per_group : (g + 1) * per_group].reshape(LANES, LANES))
        for g in range(slot_groups)
    ]

    tables = [
        wide(col[k * SPAN + 3 * CORNERS : k * SPAN + 3 * CORNERS + 1])
        for col in columns
        for k in range(GROUPS)
    ]
    tension = [gather_wide(tables, wide(ix)) for ix in lane_pieces(wanted[2:3])]
    force = [
        [
            forces[i, :, h * LANES : (h + 1) * LANES]
            + tension[h] * forces[3 + i, :, h * LANES : (h + 1) * LANES]
            for h in range(elem_count // LANES)
        ]
        for i in range(3)
    ]
    for g in range(0, inverse.shape[1], LANES):
        where = inverse[:, g : g + LANES]
        index = jnp.maximum(where, 0)
        for i in range(3):
            got = jnp.where(where >= 0, gather_wide(force[i], index), 0.0)
            resid[i : i + 1, g : g + LANES] = sub_sum(got)
    copies[1].start()

    halves = []
    for h in range(blocks // LANES):
        cut = slice(h * LANES, (h + 1) * LANES)
        where, which = wide(wanted[0:1, cut]), wide(wanted[1:2, cut])
        rows_in = []
        for c in range(3):
            value = None
            for k in range(GROUPS):
                first = k * SPAN + c * CORNERS
                found = gather_wide([col[first : first + CORNERS] for col in columns], where)
                value = found if value is None else jnp.where(which == k, found, value)
            value = 0.75 * value + 0.25 * pltpu.roll(value, 4, 0)
            swapped = jnp.where(
                iota((SUB, LANES), 0) // 2 % 2 == 1,
                pltpu.roll(value, 2, 0),
                pltpu.roll(value, SUB - 2, 0),
            )
            rows_in.append(0.75 * value + 0.25 * swapped)
        rows_in.append(jnp.zeros((SUB, LANES), f32))
        halves.append(jnp.concatenate(rows_in, 0))
    stacked = []
    for b in range(bz):
        lane0 = b * plane
        piece = halves[lane0 // LANES]
        stacked.append(
            pltpu.roll(piece, LANES - lane0 % LANES, 1) if lane0 % LANES else piece
        )
    around = jnp.transpose(jnp.concatenate(stacked, 0))
    lane = iota((SUB, nz), 1)
    strip_lane = lane // SBZ * SPAN
    xi = ((lane % SBZ).astype(f32) + 0.5) / SBZ
    for p in range(bx):
        near = around[p * by : (p + 1) * by]
        for c in range(3):
            for iv in range(SBX):
                for jv in range(SBY):
                    first = c * SUB + 4 * iv + 2 * jv
                    low = lane_gather(near, strip_lane + first)
                    high = lane_gather(near, strip_lane + first + 1)
                    fine[c, SBX * p + iv, pl.ds(jv, by, stride=SBY), :] = (
                        low + (high - low) * xi
                    )
        if (p + 1) % (bx // PIECES) == 0:
            fine_copy(p // (bx // PIECES)).start()
    for i in range(PIECES):
        fine_copy(i).wait()
    for c in copies:
        c.wait()


def shards(
    states,
    active,
    fibre_index,
    fibre_angle,
    conduct,
    gate_half,
    gate_slope,
    gate_tau,
    conductance,
    reversal,
    block_elem,
    block_weight,
    node_disp,
    elem_node,
    elem_fibre,
    material,
):
    mx, my, mz = (lax.axis_size(a) for a in AXES)
    n = mx * my * mz
    elem_count = elem_node.shape[1]
    node_count = node_disp.shape[1]
    nx, ny, nz = states.shape[1:]
    bx, by, bz = block_elem.shape
    blocks = bx * by * bz
    seats = max(2 * blocks // n, 8)
    tiles = nx // TLX
    strips = nx * ny // SUB
    rows_each = seats // GROUPS
    ids = block_elem.transpose(0, 2, 1)
    weight = block_weight.transpose(0, 2, 1)
    vmem = pl.BlockSpec(memory_space=pltpu.VMEM)
    hbm = pl.BlockSpec(memory_space=pltpu.HBM)
    gates_n = NSTATE - 2
    halo_floats = 4 * (nx + ny + 1) * nz + 12 * nx * ny
    operands = (
        states.reshape(NSTATE, strips, SUB, nz),
        active.transpose(1, 2, 0),
        fibre_index.transpose(1, 2, 0),
        fibre_angle,
        fibre_angle,
        conduct,
        gate_half,
        gate_slope,
        gate_tau,
        conductance,
        reversal,
        ids,
        weight,
        node_disp,
        elem_node,
        elem_fibre.reshape(1, elem_count),
        material,
    )
    stage = FINE_STEPS
    states_shape = jax.ShapeDtypeStruct((NSTATE, strips, SUB, nz), f32)
    fine_shape = jax.ShapeDtypeStruct((3, nx, ny, nz), f32)
    resid_shape = jax.ShapeDtypeStruct((3, node_count), f32)
    in_smem = [True] * 3 + [False] + [True] * 6 + [False] * 5 + [True]
    results = pl.pallas_call(
        functools.partial(body, (mx, my, mz, seats, nx, ny)),
        out_shape=(
            states_shape,
            jax.ShapeDtypeStruct((n, rows_each, LANES), f32),
            jax.ShapeDtypeStruct((3, blocks), i32),
            jax.ShapeDtypeStruct((CORNERS, node_count), i32),
            jax.ShapeDtypeStruct((6, CORNERS, elem_count), f32),
        ),
        in_specs=[hbm] * len(operands),
        out_specs=(vmem,) * 5,
        scratch_shapes=[
            (pltpu.SMEM if scalar else pltpu.VMEM)(x.shape, x.dtype)
            for scalar, x in zip(in_smem, operands[1:])
        ]
        + [
            pltpu.VMEM((NSTATE, strips, SUB, nz), f32),
            pltpu.VMEM((stage, nx * ny, nz), f32),
            pltpu.VMEM((3, nx, ny, nz), f32),
            pltpu.VMEM((gates_n, 2, SUB, LANES), f32),
            pltpu.VMEM((tiles, gates_n, 6, SUB, LANES), f32),
            pltpu.VMEM((2, strips, SUB, nz), f32),
            pltpu.VMEM((gates_n, strips, SUB, nz), f32),
            pltpu.VMEM((tiles * SUB, LANES), f32),
            pltpu.VMEM((stage, 2, 2, nx, nz), f32),
            pltpu.VMEM((stage, 2, 2, nx * ny), f32),
            pltpu.VMEM((stage, 4, 1, nz), f32),
            pltpu.VMEM((stage, 2, 1, nx * ny), f32),
            pltpu.VMEM((stage, 4, 2 * ny, nz), f32),
            pltpu.VMEM((stage, 4, 2, nx, nz), f32),
            pltpu.VMEM((stage, 4, 2, nx * ny), f32),
            pltpu.VMEM((stage, 8, 1, nz), f32),
            pltpu.VMEM((stage, 8, 1, nx * ny), f32),
            pltpu.VMEM((stage, 8, 1, nx * ny), f32),
            pltpu.VMEM((12, tiles * SUB, LANES), f32),
            pltpu.VMEM((halo_floats // LANES, 1, LANES), f32),
            pltpu.VMEM((nx * ny, nz), f32),
            pltpu.VMEM((n * rows_each // LANES, SUB, LANES), i32),
            pltpu.VMEM((n, 1, LANES), f32),
            pltpu.VMEM((n, 1, LANES), f32),
            pltpu.VMEM((n, rows_each, LANES), f32),
            pltpu.VMEM((n, rows_each, LANES), f32),
            pltpu.SemaphoreType.DMA((2 * tiles,)),
            pltpu.SemaphoreType.DMA((len(operands) - 1,)),
            pltpu.SemaphoreType.DMA((stage,)),
            pltpu.SemaphoreType.DMA((stage,)),
            pltpu.SemaphoreType.DMA,
            pltpu.SemaphoreType.DMA,
            pltpu.SemaphoreType.DMA((2,)),
            pltpu.SemaphoreType.DMA((2,)),
        ],
        compiler_params=pltpu.CompilerParams(
            collective_id=0, has_side_effects=True, vmem_limit_bytes=20 * 1024 * 1024
        ),
        name="step",
    )(*(pltpu.with_memory_space_constraint(a, pltpu.HBM) for a in operands))
    results = pl.pallas_call(
        write_out,
        out_shape=(states_shape, fine_shape, resid_shape),
        in_specs=[vmem] * 5,
        out_specs=(hbm,) * 3,
        scratch_shapes=[
            pltpu.VMEM((3, nx, ny, nz), f32),
            pltpu.VMEM((3, node_count), f32),
            pltpu.SemaphoreType.DMA((2 + PIECES,)),
        ],
        compiler_params=pltpu.CompilerParams(vmem_limit_bytes=20 * 1024 * 1024),
        name="write",
    )(*results)
    return results[0].reshape(states.shape), results[1], results[2]


def solution(mesh):
    in_specs = (
        P(None, "gx", "gy", "gz"),
        P("gx", "gy", "gz"),
        P("gx", "gy", "gz"),
        P(),
        P(),
        P(),
        P(),
        P(),
        P(),
        P(),
        P("gx", "gy", "gz"),
        P("gx", "gy", "gz"),
        P(None, ("gx", "gy", "gz")),
        P(None, ("gx", "gy", "gz")),
        P(("gx", "gy", "gz")),
        P(),
    )
    out_specs = (P(None, "gx", "gy", "gz"), P(None, "gx", "gy", "gz"), P(None, ("gx", "gy", "gz")))
    return jax.shard_map(shards, mesh=mesh, in_specs=in_specs, out_specs=out_specs, check_vma=False)
```

```python
import functools

import jax
import jax.numpy as jnp
from jax import lax
from jax.experimental import pallas as pl
from jax.experimental.pallas import tpu as pltpu
from jax.sharding import PartitionSpec as P

NSTATE = 19
TLX = 8
SBX = 2
SBY = 2
SBZ = 32
FINE_STEPS = 2
AXES = ("gx", "gy", "gz")
MESH = pl.DeviceIdType.MESH
LANES = 128
SUB = 8
CORNERS = 8
GROUPS = 4
SPAN = 32
PIECES = 4
f32 = jnp.float32
bf16 = jnp.bfloat16
i32 = jnp.int32
calcium_keep = 0.9
tension_half = 0.09
NN = (((1,), (0,)), ((), ()))
NT = (((1,), (1,)), ((), ()))
DIRS = (
    [tuple(side if d == dim else 0 for d in range(3)) for dim in range(3) for side in (-1, 1)]
    + [(a, b, 0) for a in (-1, 1) for b in (-1, 1)]
    + [(a, 0, b) for a in (-1, 1) for b in (-1, 1)]
    + [(0, a, b) for a in (-1, 1) for b in (-1, 1)]
)
OPPOSITE = [DIRS.index(tuple(-c for c in d)) for d in DIRS]


def mm(a, b, dims=NN):
    return lax.dot_general(a, b, dims, preferred_element_type=f32)


def parts(x, count):
    out = []
    for _ in range(count):
        out.append(x.astype(bf16).astype(f32))
        x = x - out[-1]
    return out


def iota(shape, dim):
    return lax.broadcasted_iota(i32, shape, dim)


def onehot(mask):
    return jnp.where(mask, 1.0, 0.0).astype(bf16)


def pick_rows(rows, shape):
    index = iota(shape, 0)
    out = jnp.zeros(shape, f32)
    for i, row in rows.items():
        out = jnp.where(index == i, row, out)
    return out


def lane_gather(x, index):
    return jnp.take_along_axis(x, index, axis=1, mode="promise_in_bounds")


def wide(row, rows=SUB):
    return jnp.broadcast_to(row, (rows, row.shape[1]))


def gather_wide(tables, index):
    low, high = index % LANES, index // LANES
    out = lane_gather(tables[0], low)
    for h in range(1, len(tables)):
        out = jnp.where(high == h, lane_gather(tables[h], low), out)
    return out


def lane_pieces(x):
    return [x[:, h : h + LANES] for h in range(0, x.shape[1], LANES)]


def sub_sum(x):
    return jnp.sum(x, axis=0, keepdims=True)


def body(
    sizes,
    *refs,
):
    mx, my, mz, seats, nx, ny = sizes
    operands, refs = refs[:17], refs[17:]
    states = operands[0]
    out, answers_out, wanted_out, inverse, forces_out = refs[:5]
    small, refs = refs[5:21], refs[21:]
    (
        active,
        fibre_index,
        angle_s,
        angle_v,
        conduct,
        gate_half,
        gate_slope,
        gate_tau,
        conductance,
        reversal,
        ids_ref,
        weight_ref,
        node_disp,
        elem_node,
        elem_fibre,
        material,
    ) = small
    (
        held,
        vs,
        flux,
        grad,
        gate_const,
        tile_const,
        sums,
        bends,
        mine_coef,
        send_y,
        send_z,
        send_xy,
        send_row,
        halo_x,
        halo_y,
        halo_z,
        edge_xy,
        edge_xz,
        edge_yz,
        halo_coef,
        tally,
        turned,
        slot_pos,
        ids_send,
        ids_got,
        ans_send,
        ans_got,
        load_sem,
        small_sem,
        face_send_sem,
        face_recv_sem,
        coef_send_sem,
        coef_recv_sem,
        all_send_sem,
        all_recv_sem,
    ) = refs
    nz = states.shape[3]
    n = mx * my * mz
    gates_n = NSTATE - 2
    strips = nx * ny // SUB
    bx, by, bz = nx // SBX, ny // SBY, nz // SBZ
    plane = bx * by
    blocks = plane * bz
    tiles = nx // TLX
    node_count = node_disp.shape[1]
    elem_count = elem_node.shape[1]
    rows_each = seats // GROUPS
    per_group = LANES // rows_each
    slot_groups = n // per_group
    per_row = LANES // seats
    slot_rows = n // per_row
    cx, cy, cz = (lax.axis_index(a) for a in AXES)
    me = (cx * my + cy) * mz + cz
    at = (cx, cy, cz)
    counts = (mx, my, mz)

    def others():
        steps = [
            (a, b, c) for a in range(mx) for b in range(my) for c in range(mz) if a or b or c
        ]

        def far(step):
            return sum(
                (1 if d == 1 else max(s, m - s)) if s else 0
                for d, (s, m) in enumerate(zip(step, counts))
            )

        return sorted(steps, key=far, reverse=True)

    wrapped = [[jnp.where(p + s >= m, p + s - m, p + s) for s in range(m)] for p, m in zip(at, counts)]

    def each_other(go):
        if n <= 64:
            for step in others():
                go(tuple(wrapped[d][s] for d, s in enumerate(step)))
        else:

            def one(k, carry):
                flat = (me + k) % n
                go((flat // (my * mz), (flat // mz) % my, flat % mz))
                return carry

            lax.fori_loop(1, n, one, 0)

    chunk = TLX * ny // SUB // 2

    def load(i):
        here = pl.ds(i * chunk, chunk)
        return pltpu.make_async_copy(states.at[:, here], held.at[:, here], load_sem.at[i])

    for ref in (halo_x, halo_y, halo_z, edge_xy, edge_xz, edge_yz):
        used = ref.shape[1] // 2
        ref[:, :used] = jnp.zeros((ref.shape[0], used) + ref.shape[2:], f32)
    halo_coef[:6] = jnp.zeros((6,) + halo_coef.shape[1:], f32)

    barrier = pltpu.get_barrier_semaphore()
    each_other(
        lambda to: pl.semaphore_signal(barrier, inc=1, device_id=to, device_id_type=MESH)
    )

    small_loads = [
        pltpu.make_async_copy(src, dst, small_sem.at[i])
        for i, (src, dst) in enumerate(zip(operands[1:], small))
    ]
    for c in small_loads:
        c.start()
    for i in range(strips // chunk):
        load(i).start()

    for c in small_loads:
        c.wait()

    def splat(value):
        return jnp.full((SUB, LANES), value, f32)

    angles = jnp.concatenate(
        [angle_v[...], jnp.zeros((2, LANES - angle_v.shape[1]), f32)], 1
    ) if angle_v.shape[1] < LANES else angle_v[...]
    rows = {0: angles[0:1], 1: angles[1:2]}
    across, spread, alive = [], [], []
    for t in range(tiles):
        index = fibre_index[0, 0, t]
        rows[2 + t] = jnp.full((1, LANES), angle_s[0, index], f32)
        rows[2 + tiles + t] = jnp.full((1, LANES), angle_s[1, index], f32)
        across.append(jnp.full((1, LANES), conduct[1, index], f32))
        spread.append(jnp.full((1, LANES), conduct[0, index], f32) - across[t])
        alive.append(jnp.where(active[0, 0, t] > 0, 1.0, 0.0).astype(f32))
    stack = pick_rows(rows, (SUB, LANES))
    cosine, sine = jnp.cos(stack), jnp.sin(stack)

    def frame_of(a, b):
        ca, sa = cosine[a : a + 1], sine[a : a + 1]
        cb, sb = cosine[b : b + 1], sine[b : b + 1]
        return ca * cb, sa * cb, sb

    for t in range(tiles):
        fx, fy, fz = frame_of(2 + t, 2 + tiles + t)
        scale = alive[t] * 0.25
        entries = [
            across[t] + spread[t] * fx * fx,
            across[t] + spread[t] * fy * fy,
            across[t] + spread[t] * fz * fz,
            spread[t] * fx * fy,
            spread[t] * fx * fz,
            spread[t] * fy * fz,
        ]
        mine_coef[t * SUB : (t + 1) * SUB] = pick_rows(
            {k: e * scale for k, e in enumerate(entries)}, (SUB, LANES)
        )

    for g in range(gates_n):
        slope = 0.5 / splat(gate_slope[g])
        gate_const[g, 0] = slope
        gate_const[g, 1] = slope * gate_half[g]
        keep = jnp.exp(-1.0 / splat(gate_tau[g]))
        share = 0.5 * (1.0 - keep)
        cond = splat(conductance[g])
        for t in range(tiles):
            live = splat(alive[t]) > 0.5
            tile_const[t, g, 0] = jnp.where(live, keep, 1.0)
            tile_const[t, g, 1] = jnp.where(live, share, 0.0)
            tile_const[t, g, 2] = jnp.where(live, cond, 0.0)
            pull = cond * reversal[g]
            tile_const[t, g, 3] = jnp.where(live, pull, 0.0)
            tile_const[t, g, 4] = jnp.where(live, cond * share, 0.0)
            tile_const[t, g, 5] = jnp.where(live, pull * share, 0.0)

    def live_calcium(t):
        live = splat(alive[t]) > 0.5
        keep = jnp.where(live, calcium_keep, 1.0)
        share = jnp.where(live, 0.5 * (1.0 - calcium_keep), 0.0)
        return keep, share

    def calcium_of(old, volt, t):
        keep, share = live_calcium(t)
        return old * keep + (jnp.tanh(4.0 * volt - 2.0) * share + share)

    def ionic(i, t):
        where = pl.ds(i * chunk, chunk)
        volt = held[0, where]
        total = jnp.zeros_like(volt)
        shift = jnp.zeros_like(volt)
        for g in range(gates_n):
            bend = jnp.tanh(volt * gate_const[g, 0] - gate_const[g, 1])
            share = tile_const[t, g, 1]
            gate = held[1 + g, where] * tile_const[t, g, 0] + (bend * share + share)
            out[1 + g, where] = gate
            total = total + gate * tile_const[t, g, 2]
            shift = shift + gate * tile_const[t, g, 3]
        star = volt - (volt * total - shift)
        vs[0, pl.ds(i * chunk * SUB, chunk * SUB)] = star.reshape(chunk * SUB, LANES)

    def ionic_before(i, t):
        where = pl.ds(i * chunk, chunk)
        total = jnp.zeros((chunk, SUB, LANES), f32)
        shift = jnp.zeros((chunk, SUB, LANES), f32)
        for g in range(gates_n):
            kept = out[1 + g, where] * tile_const[t, g, 0] + tile_const[t, g, 1]
            out[1 + g, where] = kept
            total = total + kept * tile_const[t, g, 2]
            shift = shift + kept * tile_const[t, g, 3]
        sums[0, where] = total
        sums[1, where] = shift

    def ionic_between(i, t):
        where = pl.ds(i * chunk, chunk)
        volt = out[0, where]
        total = sums[0, where]
        shift = sums[1, where]
        for g in range(gates_n):
            bend = jnp.tanh(volt * gate_const[g, 0] - gate_const[g, 1])
            bends[g, where] = bend
            total = total + bend * tile_const[t, g, 4]
            shift = shift + bend * tile_const[t, g, 5]
        star = volt - (volt * total - shift)
        vs[1, pl.ds(i * chunk * SUB, chunk * SUB)] = star.reshape(chunk * SUB, LANES)

    def ionic_after(i, t):
        where = pl.ds(i * chunk, chunk)
        for g in range(gates_n):
            out[1 + g, where] = out[1 + g, where] + bends[g, where] * tile_const[t, g, 1]

    def over_chunks(step):
        for t in range(tiles):

            def go(i, carry, t=t):
                step(i, t)
                return carry

            lax.fori_loop(2 * t, 2 * t + 2, go, 0)

    flat_in = (bx * bz, by)
    raw = jnp.concatenate(
        parts(ids_ref[...].astype(f32).reshape(flat_in), 3), 0
    ).astype(bf16)
    lane_b = iota((by, blocks), 1)
    put = onehot(lane_b % by == iota((by, blocks), 0))
    spread_ids = mm(raw, put)
    part = bx * bz
    spread_ids = spread_ids[:part] + spread_ids[part : 2 * part] + spread_ids[2 * part :]
    row_b, col_b = iota((part, blocks), 0), iota((part, blocks), 1)
    here = (row_b // bz == (col_b % plane) // by) & (row_b % bz == col_b // plane)
    ids = sub_sum(jnp.where(here, spread_ids, 0.0)).astype(i32)
    shift = elem_count.bit_length() - 1
    owner = lax.shift_right_logical(ids, shift)
    local = ids - owner * elem_count
    owned = onehot(owner == iota((n, blocks), 0))
    before = onehot(iota((blocks, blocks), 0) < iota((blocks, blocks), 1))
    seen = mm(owned, before)
    rank = sub_sum(owned.astype(f32) * seen).astype(i32)
    offset = (me % per_row) * seats
    hit = owner == iota((n, blocks), 0)
    place = onehot(iota((LANES, blocks), 0) == rank + offset)
    sent = mm(jnp.where(hit, (local + 1).astype(f32), 0.0).astype(bf16), place, NT)
    ids_send[...] = sent.reshape(n, 1, LANES)
    group, seat_row = rank % GROUPS, rank // GROUPS
    number = jnp.where(
        group == iota((SUB, blocks), 0), (iota((SUB, blocks), 1) + 1).astype(f32), 0.0
    ).astype(bf16)
    seat_place = owner * rows_each + seat_row
    for g in range(slot_groups):
        block_at = (
            mm(number, onehot(iota((LANES, blocks), 0) + g * LANES == seat_place), NT).astype(i32)
            - 1
        )
        in_plane = block_at % plane
        slot_pos[g] = jnp.where(
            block_at >= 0,
            (block_at // plane // 2) * LANES
            + (in_plane // by) * ny
            + (in_plane % by) * SBY
            + (block_at // plane) % 2,
            -1,
        )
    wanted_out[0:1] = seat_place
    wanted_out[1:2] = group

    raw = jnp.concatenate(parts(weight_ref[...].reshape(flat_in), 2), 0).astype(bf16)
    put = onehot(iota((by, bx * ny), 1) % ny == iota((by, bx * ny), 0) * SBY)
    spread_w = mm(raw, put)
    spread_w = (spread_w[:part] + spread_w[part:]).reshape(bx, bz, bx * ny)
    here = iota((bx, bz, bx * ny), 0) == iota((bx, bz, bx * ny), 2) // ny
    weights = jnp.sum(jnp.where(here, spread_w, 0.0), axis=0)
    weights = jnp.concatenate([weights, jnp.zeros((SUB - bz, bx * ny), f32)], 0)
    weights = weights * (1.0 / (SBX * SBY * SBZ))

    def first(i, t):
        load(i).wait()
        ionic(i, t)
        here = pl.ds(i * chunk, chunk)
        out[NSTATE - 1, here] = calcium_of(held[NSTATE - 1, here], held[0, here], t)

    over_chunks(first)

    def source_of(stage, i):
        d = DIRS[i]
        if i < 2:
            return vs.at[stage, pl.ds(0 if d[0] < 0 else (nx - 2) * ny, 2 * ny)]
        if i < 4:
            return send_y.at[stage, i - 2]
        if i < 6:
            return send_z.at[stage, i - 4]
        if i < 10:
            return send_xy.at[stage, i - 6]
        return send_row.at[stage, 0 if d[2] < 0 else 1]

    families = (
        [(halo_x, 0, 2), (halo_y, 2, 2), (halo_z, 4, 2)]
        + [(edge_xy, 6, 4), (edge_xz, 10, 4), (edge_yz, 14, 4)]
    )

    def exists(i):
        ok = None
        for p, step, m in zip(at, DIRS[i], counts):
            if step:
                inside = p > 0 if step < 0 else p < m - 1
                ok = inside if ok is None else ok & inside
        return ok

    def route(i):
        ok = exists(i)
        swap = next(d for d in (1, 0, 2) if DIRS[i][d] == 0)
        to = []
        for d, (p, step) in enumerate(zip(at, DIRS[i])):
            if step:
                p = jnp.where(ok, p + step, p)
            elif d == swap:
                p = jnp.where(ok, p, p + 1 - 2 * (p % 2))
            to.append(p)
        return tuple(to), ok

    order = list(range(len(DIRS) - 1, -1, -1))

    def prepare(stage):
        for side in range(2):
            for layer in range(2):
                y = layer if side == 0 else ny - 2 + layer
                send_y[stage, side, layer] = vs[stage, pl.ds(y, nx, stride=ny), :]
        for a in range(2):
            for b in range(2):
                row = (nx - 1) * a * ny + (ny - 1) * b
                send_xy[stage, 2 * a + b] = vs[stage, row : row + 1, :]
        columns = jnp.transpose(vs[stage])
        send_z[stage, 0] = columns[0:2]
        send_z[stage, 1] = columns[nz - 2 : nz]
        send_row[stage, 0] = columns[0:1]
        send_row[stage, 1] = columns[nz - 1 : nz]

    def send(stage):
        for i in order:
            ref, first, count = next(f for f in families if f[1] <= i < f[1] + f[2])
            to, ok = route(i)
            slot = jnp.where(ok, OPPOSITE[i] - first, count + i - first)
            pltpu.make_async_remote_copy(
                src_ref=source_of(stage, i),
                dst_ref=ref.at[stage, slot],
                send_sem=face_send_sem.at[stage],
                recv_sem=face_recv_sem.at[stage],
                device_id=to,
                device_id_type=MESH,
            ).start()

    def receive(stage):
        pltpu.make_async_remote_copy(
            src_ref=tally,
            dst_ref=tally,
            send_sem=face_send_sem.at[stage],
            recv_sem=face_recv_sem.at[stage],
            device_id=at,
            device_id_type=MESH,
        ).wait()

    def send_coef():
        for i in range(6):
            to, ok = route(i)
            pltpu.make_async_remote_copy(
                src_ref=mine_coef,
                dst_ref=halo_coef.at[jnp.where(ok, OPPOSITE[i], 6 + i)],
                send_sem=coef_send_sem,
                recv_sem=coef_recv_sem,
                device_id=to,
                device_id_type=MESH,
            ).start()

    def receive_coef():
        pltpu.make_async_remote_copy(
            src_ref=halo_coef.at[pl.ds(0, 6)],
            dst_ref=halo_coef.at[pl.ds(0, 6)],
            send_sem=coef_send_sem,
            recv_sem=coef_recv_sem,
            device_id=at,
            device_id_type=MESH,
        ).wait()

    def all_start(kind, src, dst):
        dst[pl.ds(me, 1)] = src[pl.ds(me, 1)]

        def go(to):
            flat = (to[0] * my + to[1]) * mz + to[2]
            pltpu.make_async_remote_copy(
                src_ref=src.at[flat],
                dst_ref=dst.at[me],
                send_sem=all_send_sem.at[kind],
                recv_sem=all_recv_sem.at[kind],
                device_id=to,
                device_id_type=MESH,
            ).start()

        each_other(go)

    def all_wait(kind, src, dst):
        pltpu.make_async_remote_copy(
            src_ref=src.at[pl.ds(0, n - 1)],
            dst_ref=dst.at[pl.ds(0, n - 1)],
            send_sem=all_send_sem.at[kind],
            recv_sem=all_recv_sem.at[kind],
            device_id=at,
            device_id_type=MESH,
        ).wait()

    def coef_row(ref, t, k):
        return ref[t * SUB + k : t * SUB + k + 1, :]

    def slopes(stage):
        v = vs[stage].reshape(nx, ny, nz)
        zero = jnp.zeros((1, ny, nz), f32)
        row, lane = iota((1, ny, nz), 1), iota((1, 1, nz), 2)
        grad[0] = jnp.concatenate([v[1:], zero], 0) - jnp.concatenate([zero, v[:-1]], 0)
        grad[1] = jnp.where(row == ny - 1, 0.0, pltpu.roll(v, ny - 1, 1)) - jnp.where(
            row == 0, 0.0, pltpu.roll(v, 1, 1)
        )
        grad[2] = jnp.where(lane == nz - 1, 0.0, pltpu.roll(v, nz - 1, 2)) - jnp.where(
            lane == 0, 0.0, pltpu.roll(v, 1, 2)
        )

    def diffuse(stage):
        v = vs[stage].reshape(nx, ny, nz)
        lane = iota((1, nz), 1)
        flat = nx * ny
        lane_f = iota((SUB, flat), 1)

        def both(low, high):
            return pick_rows({0: low, 1: high}, (SUB, flat))

        near = both(halo_z[stage, 0, 1:2], halo_z[stage, 1, 0:1])
        gz = both(
            send_row[stage, 0] - halo_z[stage, 0, 0:1],
            halo_z[stage, 1, 1:2] - send_row[stage, 1],
        )
        xz = [both(edge_xz[stage, 2 * a], edge_xz[stage, 2 * a + 1]) for a in range(2)]
        yz = [both(edge_yz[stage, 2 * a], edge_yz[stage, 2 * a + 1]) for a in range(2)]
        up = pltpu.roll(jnp.where(lane_f < ny, xz[1], near), flat - ny, 1)
        down = pltpu.roll(jnp.where(lane_f >= flat - ny, xz[0], near), ny, 1)
        gx = up - down
        up = jnp.where(
            lane_f % ny == ny - 1, pltpu.roll(yz[1], ny - 1, 1), pltpu.roll(near, flat - 1, 1)
        )
        down = jnp.where(
            lane_f % ny == 0, pltpu.roll(yz[0], flat - ny + 1, 1), pltpu.roll(near, 1, 1)
        )
        gy = up - down

        def coef_z(k):
            return both(
                *(
                    jnp.concatenate(
                        [coef_row(halo_coef.at[4 + s], t, k) for t in range(tiles)], 1
                    )
                    for s in range(2)
                )
            )

        fz = coef_z(4) * gx + coef_z(5) * gy + coef_z(2) * gz
        blank = jnp.zeros((SUB, flat), f32)
        half = nz // 2
        pieces = [blank] * (nz // SUB)
        pieces[0] = pick_rows(
            {0: near[0:1], **{1 + i: edge_xz[stage, i] for i in range(4)}}, (SUB, flat)
        )
        pieces[half // SUB - 1] = pick_rows({SUB - 1: fz[1:2]}, (SUB, flat))
        pieces[half // SUB] = pick_rows(
            {0: fz[0:1], **{1 + i: edge_yz[stage, i] for i in range(4)}}, (SUB, flat)
        )
        pieces[-1] = pick_rows({SUB - 1: near[1:2]}, (SUB, flat))
        turned[...] = jnp.transpose(jnp.concatenate(pieces, 0))

        def along_z(a, low, high):
            return jnp.where(lane == nz - 1, high, pltpu.roll(a, nz - 1, 1)) - jnp.where(
                lane == 0, low, pltpu.roll(a, 1, 1)
            )

        def along_rows(a, low, high):
            row = iota(a.shape, 0)
            m = a.shape[0]
            return jnp.where(row == m - 1, high, pltpu.roll(a, m - 1, 0)) - jnp.where(
                row == 0, low, pltpu.roll(a, 1, 0)
            )

        px, fx_out = [], []
        for s in range(2):
            close = halo_x[stage, s, ny:] if s == 0 else halo_x[stage, s, :ny]
            distant = halo_x[stage, s, :ny] if s == 0 else halo_x[stage, s, ny:]
            gx = v[0] - distant if s == 0 else distant - v[nx - 1]
            gy = along_rows(close, edge_xy[stage, 2 * s], edge_xy[stage, 2 * s + 1])
            first = (nx - 1) * ny if s == 0 else 0
            edge = turned[first : first + ny, :]
            c = 1 + 2 * s
            gz = along_z(close, edge[:, c : c + 1], edge[:, c + 1 : c + 2])
            t = tiles - 1 if s == 0 else 0
            k = [coef_row(halo_coef.at[s], t, j) for j in (0, 3, 4)]
            px.append(close)
            fx_out.append(k[0] * gx + k[1] * gy + k[2] * gz)
        py, fy_out = [], []
        for s in range(2):
            close, distant = halo_y[stage, s, 1 - s], halo_y[stage, s, s]
            own = vs[stage, pl.ds(0 if s == 0 else ny - 1, nx, stride=ny), :]
            gy = own - distant if s == 0 else distant - own
            gx = along_rows(close, edge_xy[stage, s], edge_xy[stage, 2 + s])
            edge = turned[pl.ds(ny - 1 if s == 0 else 0, nx, stride=ny), :]
            c = half + 1 + 2 * s
            gz = along_z(close, edge[:, c : c + 1], edge[:, c + 1 : c + 2])

            def coef_y(j, s=s):
                return jnp.concatenate(
                    [wide(coef_row(halo_coef.at[2 + s], t, j), TLX) for t in range(tiles)], 0
                )

            py.append(close)
            fy_out.append(coef_y(3) * gx + coef_y(1) * gy + coef_y(5) * gz)

        def diff_x(a, low, high):
            return jnp.concatenate([a[1:], high[None]], 0) - jnp.concatenate([low[None], a[:-1]], 0)

        def diff_y(a, low, high):
            row = iota((1, ny, nz), 1)
            up = jnp.where(row == ny - 1, high.reshape(nx, 1, nz), pltpu.roll(a, ny - 1, 1))
            down = jnp.where(row == 0, low.reshape(nx, 1, nz), pltpu.roll(a, 1, 1))
            return up - down

        def diff_z(a, edge):
            lane = iota((1, 1, nz), 2)
            up = jnp.where(lane == nz - 1, edge, pltpu.roll(a, nz - 1, 2))
            down = jnp.where(lane == 0, edge, pltpu.roll(a, 1, 2))
            return up - down

        edges = turned[...].reshape(nx, ny, nz)
        row, lane3 = iota((1, ny, nz), 1), iota((1, 1, nz), 2)
        first_x, last_x = grad[0, 0] - px[0], grad[0, nx - 1] + px[1]
        gx = jnp.concatenate([first_x[None], grad[0, 1 : nx - 1], last_x[None]], 0)
        gy = grad[1] + jnp.where(
            row == ny - 1,
            py[1].reshape(nx, 1, nz),
            jnp.where(row == 0, -py[0].reshape(nx, 1, nz), 0.0),
        )
        side = jnp.where(lane3 == nz - 1, 1.0, jnp.where(lane3 == 0, -1.0, 0.0))
        gz = grad[2] + edges * side
        for t in range(tiles):
            span = slice(t * TLX, (t + 1) * TLX)
            xx, yy, zz, xy, xz_, yz_ = (
                coef_row(mine_coef, t, k).reshape(1, 1, LANES) for k in range(6)
            )
            a, b, c = gx[span], gy[span], gz[span]
            flux[0, span] = xx * a + xy * b + xz_ * c
            flux[1, span] = xy * a + yy * b + yz_ * c
            flux[2, span] = xz_ * a + yz_ * b + zz * c
        edges = pltpu.roll(edges, half, 2)
        lap = (
            diff_x(flux[0], *fx_out)
            + diff_y(flux[1], *fy_out)
            + diff_z(flux[2], edges)
        )
        for t in range(tiles):
            span = slice(t * TLX, (t + 1) * TLX)
            new = v[span] + lap[span] * alive[t]
            where = pl.ds(t * TLX * ny // SUB, TLX * ny // SUB)
            out[0, where] = new.reshape(TLX * ny // SUB, SUB, LANES)

    prepare(0)
    pl.semaphore_wait(barrier, n - 1)
    all_start(0, ids_send, ids_got)
    send(0)
    send_coef()


    slopes(0)
    over_chunks(ionic_before)
    nodes = elem_node[...]
    disp = []
    for c in range(3):
        table = [
            wide(node_disp[c : c + 1, g : g + LANES]) for g in range(0, node_count, LANES)
        ]
        disp.append([gather_wide(table, ix) for ix in lane_pieces(nodes)])
    fx, fy, fz = frame_of(0, 1)
    table = [pick_rows({0: fx, 1: fy, 2: fz}, (SUB, LANES))]
    frame8 = [gather_wide(table, wide(ix)) for ix in lane_pieces(elem_fibre[...])]
    corner = iota((CORNERS, LANES), 0)
    signs = [
        jnp.where((corner // (4 >> j)) % 2 == 1, 0.25, -0.25) for j in range(3)
    ]
    shear, bulk, scale = material[0], material[1], material[2]
    for h in range(elem_count // LANES):
        frame = [frame8[h][i : i + 1] for i in range(3)]
        d = [
            [
                sub_sum(disp[i][h] * signs[j]) + (1.0 if i == j else 0.0)
                for j in range(3)
            ]
            for i in range(3)
        ]
        cof = [
            [
                d[(i + 1) % 3][(j + 1) % 3] * d[(i + 2) % 3][(j + 2) % 3]
                - d[(i + 1) % 3][(j + 2) % 3] * d[(i + 2) % 3][(j + 1) % 3]
                for j in range(3)
            ]
            for i in range(3)
        ]
        volume = d[0][0] * cof[0][0] + d[0][1] * cof[0][1] + d[0][2] * cof[0][2]
        reciprocal = 1.0 / volume
        logv = jnp.log(volume)
        stress = [
            [
                shear * (d[i][j] - cof[i][j] * reciprocal)
                + bulk * logv * (cof[i][j] * reciprocal)
                for j in range(3)
            ]
            for i in range(3)
        ]
        stretch = [
            scale * (d[i][0] * frame[0] + d[i][1] * frame[1] + d[i][2] * frame[2])
            for i in range(3)
        ]
        along = sum(wide(frame[j]) * signs[j] for j in range(3))
        cut = slice(h * LANES, (h + 1) * LANES)
        for i in range(3):
            forces_out[i, :, cut] = sum(wide(stress[i][j]) * signs[j] for j in range(3))
            forces_out[3 + i, :, cut] = wide(stretch[i]) * along

    found = jnp.zeros((CORNERS, node_count), f32)
    lane_e = (iota((CORNERS, elem_count), 1) + 1).astype(f32)
    for q in range(CORNERS):
        named = onehot(iota((node_count, elem_count), 0) == nodes[q : q + 1, :])
        mine = jnp.where(iota((CORNERS, elem_count), 0) == q, lane_e, 0.0).astype(bf16)
        found = found + mm(mine, named, NT)
    inverse[...] = found.astype(i32) - 1

    receive(0)
    receive_coef()
    diffuse(0)

    pulls = []
    for t in range(tiles):
        where = pl.ds(t * TLX * ny // SUB, TLX * ny // SUB)
        calcium = calcium_of(out[NSTATE - 1, where], out[0, where], t)
        out[NSTATE - 1, where] = calcium
        square = calcium * calcium
        pulls.append(square / (square + tension_half))
    pull = jnp.concatenate(pulls, 0).reshape(bx, SBX, ny, nz)
    pull = (pull[:, 0] + pull[:, 1]).reshape(bx * ny, nz)
    strip = onehot(iota((SUB, nz), 1) // SBZ == iota((SUB, nz), 0))
    high = pull.astype(bf16)
    rest = (pull - high.astype(f32)).astype(bf16)
    pooled = mm(strip, high, NT) + mm(strip, rest, NT)
    lanes_p = bx * ny
    value = (pooled + pltpu.roll(pooled, lanes_p - 1, 1)) * weights
    even = iota((1, lanes_p), 1) % 2 == 0
    odd_value = pltpu.roll(value, 1, 1)
    tables = [
        wide(jnp.where(even, value[b : b + 1], odd_value[b + 1 : b + 2]))
        for b in range(0, bz, 2)
    ]
    value_rows = []
    for g in range(slot_groups):
        where = slot_pos[g]
        value_rows.append(
            jnp.where(where >= 0, gather_wide(tables, jnp.maximum(where, 0)), 0.0)
        )

    all_wait(0, ids_send, ids_got)
    asked = []
    for r in range(0, n, per_row):
        total = ids_got[r]
        for m in range(1, per_row):
            total = total + ids_got[r + m]
        asked.append(total)
    asked_wide = [wide(row) for row in asked]
    place = iota((SUB, LANES), 1)
    for g in range(slot_groups):
        device_at = g * per_group + place // rows_each
        rows_out = []
        for k in range(GROUPS):
            source = (device_at % per_row) * seats + (place % rows_each) * GROUPS + k
            where = None
            for r in range(g * per_group // per_row, -(-(g + 1) * per_group // per_row)):
                found = lane_gather(asked_wide[r], source)
                where = (
                    found if where is None else jnp.where(device_at // per_row == r, found, where)
                )
            where = jnp.maximum(where.astype(i32) - 1, 0)
            rows_out += [gather_wide(disp[c], where) for c in range(3)]
            rows_out.append(wide(value_rows[g][k : k + 1]))
        answer = jnp.transpose(jnp.concatenate(rows_out, 0))
        ans_send[g * per_group : (g + 1) * per_group] = answer.reshape(
            per_group, rows_each, LANES
        )
    all_start(1, ans_send, ans_got)
    over_chunks(ionic_between)
    prepare(1)
    send(1)
    slopes(1)
    over_chunks(ionic_after)

    code = jnp.zeros((LANES, elem_count), f32)
    ident = (iota((LANES, elem_count), 1) + 1).astype(f32)
    row = iota((LANES, 1), 0)

    def arrival(lane, r):
        seat = lane % seats
        lane = (r * per_row + lane // seats) * rows_each + seat // GROUPS
        return ((lane // LANES * GROUPS + seat % GROUPS) * LANES + lane % LANES).astype(f32)

    column = jnp.transpose(
        jnp.concatenate(asked + [jnp.zeros((LANES - slot_rows, LANES), f32)], 0)
    )
    for r in range(slot_rows):
        code = jnp.where(column[:, r : r + 1] == ident, arrival(row, r), code)
    wanted_out[2:3] = sub_sum(code).astype(i32)

    receive(1)
    diffuse(1)

    all_wait(1, ans_send, ans_got)
    answers_out[...] = ans_got[...]


def write_out(
    states,
    answers,
    wanted,
    inverse,
    forces,
    states_out,
    fine_out,
    resid_out,
    fine,
    resid,
    sems,
):
    n, rows_each = answers.shape[:2]
    nx, ny, nz = fine.shape[1:]
    bx, by, bz = nx // SBX, ny // SBY, nz // SBZ
    plane = bx * by
    blocks = plane * bz
    per_group = LANES // rows_each
    slot_groups = n // per_group
    elem_count = forces.shape[2]
    copies = [
        pltpu.make_async_copy(states, states_out, sems.at[0]),
        pltpu.make_async_copy(resid, resid_out, sems.at[1]),
    ]
    copies[0].start()

    def fine_copy(i):
        here = pl.ds(i * nx // PIECES, nx // PIECES)
        return pltpu.make_async_copy(fine.at[:, here], fine_out.at[:, here], sems.at[2 + i])

    columns = [
        jnp.transpose(answers[g * per_group : (g + 1) * per_group].reshape(LANES, LANES))
        for g in range(slot_groups)
    ]

    tables = [
        wide(col[k * SPAN + 3 * CORNERS : k * SPAN + 3 * CORNERS + 1])
        for col in columns
        for k in range(GROUPS)
    ]
    tension = [gather_wide(tables, wide(ix)) for ix in lane_pieces(wanted[2:3])]
    force = [
        [
            forces[i, :, h * LANES : (h + 1) * LANES]
            + tension[h] * forces[3 + i, :, h * LANES : (h + 1) * LANES]
            for h in range(elem_count // LANES)
        ]
        for i in range(3)
    ]
    for g in range(0, inverse.shape[1], LANES):
        where = inverse[:, g : g + LANES]
        index = jnp.maximum(where, 0)
        for i in range(3):
            got = jnp.where(where >= 0, gather_wide(force[i], index), 0.0)
            resid[i : i + 1, g : g + LANES] = sub_sum(got)
    copies[1].start()

    halves = []
    for h in range(blocks // LANES):
        cut = slice(h * LANES, (h + 1) * LANES)
        where, which = wide(wanted[0:1, cut]), wide(wanted[1:2, cut])
        rows_in = []
        for c in range(3):
            value = None
            for k in range(GROUPS):
                first = k * SPAN + c * CORNERS
                found = gather_wide([col[first : first + CORNERS] for col in columns], where)
                value = found if value is None else jnp.where(which == k, found, value)
            value = 0.75 * value + 0.25 * pltpu.roll(value, 4, 0)
            swapped = jnp.where(
                iota((SUB, LANES), 0) // 2 % 2 == 1,
                pltpu.roll(value, 2, 0),
                pltpu.roll(value, SUB - 2, 0),
            )
            rows_in.append(0.75 * value + 0.25 * swapped)
        rows_in.append(jnp.zeros((SUB, LANES), f32))
        halves.append(jnp.concatenate(rows_in, 0))
    stacked = []
    for b in range(bz):
        lane0 = b * plane
        piece = halves[lane0 // LANES]
        stacked.append(
            pltpu.roll(piece, LANES - lane0 % LANES, 1) if lane0 % LANES else piece
        )
    around = jnp.transpose(jnp.concatenate(stacked, 0))
    lane = iota((SUB, nz), 1)
    strip_lane = lane // SBZ * SPAN
    xi = ((lane % SBZ).astype(f32) + 0.5) / SBZ
    for p in range(bx):
        near = around[p * by : (p + 1) * by]
        for c in range(3):
            for iv in range(SBX):
                for jv in range(SBY):
                    first = c * SUB + 4 * iv + 2 * jv
                    low = lane_gather(near, strip_lane + first)
                    high = lane_gather(near, strip_lane + first + 1)
                    fine[c, SBX * p + iv, pl.ds(jv, by, stride=SBY), :] = (
                        low + (high - low) * xi
                    )
        if (p + 1) % (bx // PIECES) == 0:
            fine_copy(p // (bx // PIECES)).start()
    for i in range(PIECES):
        fine_copy(i).wait()
    for c in copies:
        c.wait()


def shards(
    states,
    active,
    fibre_index,
    fibre_angle,
    conduct,
    gate_half,
    gate_slope,
    gate_tau,
    conductance,
    reversal,
    block_elem,
    block_weight,
    node_disp,
    elem_node,
    elem_fibre,
    material,
):
    mx, my, mz = (lax.axis_size(a) for a in AXES)
    n = mx * my * mz
    elem_count = elem_node.shape[1]
    node_count = node_disp.shape[1]
    nx, ny, nz = states.shape[1:]
    bx, by, bz = block_elem.shape
    blocks = bx * by * bz
    seats = max(2 * blocks // n, 8)
    tiles = nx // TLX
    strips = nx * ny // SUB
    rows_each = seats // GROUPS
    ids = block_elem.transpose(0, 2, 1)
    weight = block_weight.transpose(0, 2, 1)
    vmem = pl.BlockSpec(memory_space=pltpu.VMEM)
    hbm = pl.BlockSpec(memory_space=pltpu.HBM)
    gates_n = NSTATE - 2
    halo_floats = 4 * (nx + ny + 1) * nz + 12 * nx * ny
    operands = (
        states.reshape(NSTATE, strips, SUB, nz),
        active.transpose(1, 2, 0),
        fibre_index.transpose(1, 2, 0),
        fibre_angle,
        fibre_angle,
        conduct,
        gate_half,
        gate_slope,
        gate_tau,
        conductance,
        reversal,
        ids,
        weight,
        node_disp,
        elem_node,
        elem_fibre.reshape(1, elem_count),
        material,
    )
    stage = FINE_STEPS
    states_shape = jax.ShapeDtypeStruct((NSTATE, strips, SUB, nz), f32)
    fine_shape = jax.ShapeDtypeStruct((3, nx, ny, nz), f32)
    resid_shape = jax.ShapeDtypeStruct((3, node_count), f32)
    in_smem = [True] * 3 + [False] + [True] * 6 + [False] * 5 + [True]
    results = pl.pallas_call(
        functools.partial(body, (mx, my, mz, seats, nx, ny)),
        out_shape=(
            states_shape,
            jax.ShapeDtypeStruct((n, rows_each, LANES), f32),
            jax.ShapeDtypeStruct((3, blocks), i32),
            jax.ShapeDtypeStruct((CORNERS, node_count), i32),
            jax.ShapeDtypeStruct((6, CORNERS, elem_count), f32),
        ),
        in_specs=[hbm] * len(operands),
        out_specs=(vmem,) * 5,
        scratch_shapes=[
            (pltpu.SMEM if scalar else pltpu.VMEM)(x.shape, x.dtype)
            for scalar, x in zip(in_smem, operands[1:])
        ]
        + [
            pltpu.VMEM((NSTATE, strips, SUB, nz), f32),
            pltpu.VMEM((stage, nx * ny, nz), f32),
            pltpu.VMEM((3, nx, ny, nz), f32),
            pltpu.VMEM((3, nx, ny, nz), f32),
            pltpu.VMEM((gates_n, 2, SUB, LANES), f32),
            pltpu.VMEM((tiles, gates_n, 6, SUB, LANES), f32),
            pltpu.VMEM((2, strips, SUB, nz), f32),
            pltpu.VMEM((gates_n, strips, SUB, nz), f32),
            pltpu.VMEM((tiles * SUB, LANES), f32),
            pltpu.VMEM((stage, 2, 2, nx, nz), f32),
            pltpu.VMEM((stage, 2, 2, nx * ny), f32),
            pltpu.VMEM((stage, 4, 1, nz), f32),
            pltpu.VMEM((stage, 2, 1, nx * ny), f32),
            pltpu.VMEM((stage, 4, 2 * ny, nz), f32),
            pltpu.VMEM((stage, 4, 2, nx, nz), f32),
            pltpu.VMEM((stage, 4, 2, nx * ny), f32),
            pltpu.VMEM((stage, 8, 1, nz), f32),
            pltpu.VMEM((stage, 8, 1, nx * ny), f32),
            pltpu.VMEM((stage, 8, 1, nx * ny), f32),
            pltpu.VMEM((12, tiles * SUB, LANES), f32),
            pltpu.VMEM((halo_floats // LANES, 1, LANES), f32),
            pltpu.VMEM((nx * ny, nz), f32),
            pltpu.VMEM((n * rows_each // LANES, SUB, LANES), i32),
            pltpu.VMEM((n, 1, LANES), f32),
            pltpu.VMEM((n, 1, LANES), f32),
            pltpu.VMEM((n, rows_each, LANES), f32),
            pltpu.VMEM((n, rows_each, LANES), f32),
            pltpu.SemaphoreType.DMA((2 * tiles,)),
            pltpu.SemaphoreType.DMA((len(operands) - 1,)),
            pltpu.SemaphoreType.DMA((stage,)),
            pltpu.SemaphoreType.DMA((stage,)),
            pltpu.SemaphoreType.DMA,
            pltpu.SemaphoreType.DMA,
            pltpu.SemaphoreType.DMA((2,)),
            pltpu.SemaphoreType.DMA((2,)),
        ],
        compiler_params=pltpu.CompilerParams(
            collective_id=0, has_side_effects=True, vmem_limit_bytes=20 * 1024 * 1024
        ),
        name="step",
    )(*(pltpu.with_memory_space_constraint(a, pltpu.HBM) for a in operands))
    results = pl.pallas_call(
        write_out,
        out_shape=(states_shape, fine_shape, resid_shape),
        in_specs=[vmem] * 5,
        out_specs=(hbm,) * 3,
        scratch_shapes=[
            pltpu.VMEM((3, nx, ny, nz), f32),
            pltpu.VMEM((3, node_count), f32),
            pltpu.SemaphoreType.DMA((2 + PIECES,)),
        ],
        compiler_params=pltpu.CompilerParams(vmem_limit_bytes=20 * 1024 * 1024),
        name="write",
    )(*results)
    return results[0].reshape(states.shape), results[1], results[2]


def solution(mesh):
    in_specs = (
        P(None, "gx", "gy", "gz"),
        P("gx", "gy", "gz"),
        P("gx", "gy", "gz"),
        P(),
        P(),
        P(),
        P(),
        P(),
        P(),
        P(),
        P("gx", "gy", "gz"),
        P("gx", "gy", "gz"),
        P(None, ("gx", "gy", "gz")),
        P(None, ("gx", "gy", "gz")),
        P(("gx", "gy", "gz")),
        P(),
    )
    out_specs = (P(None, "gx", "gy", "gz"), P(None, "gx", "gy", "gz"), P(None, ("gx", "gy", "gz")))
    return jax.shard_map(shards, mesh=mesh, in_specs=in_specs, out_specs=out_specs, check_vma=False)
```

```python
import functools

import jax
import jax.numpy as jnp
from jax import lax
from jax.experimental import pallas as pl
from jax.experimental.pallas import tpu as pltpu
from jax.sharding import PartitionSpec as P

NSTATE = 19
TLX = 8
SBX = 2
SBY = 2
SBZ = 32
FINE_STEPS = 2
AXES = ("gx", "gy", "gz")
MESH = pl.DeviceIdType.MESH
LANES = 128
SUB = 8
CORNERS = 8
GROUPS = 4
SPAN = 32
PIECES = 4
f32 = jnp.float32
bf16 = jnp.bfloat16
i32 = jnp.int32
calcium_keep = 0.9
tension_half = 0.09
NN = (((1,), (0,)), ((), ()))
NT = (((1,), (1,)), ((), ()))
DIRS = (
    [tuple(side if d == dim else 0 for d in range(3)) for dim in range(3) for side in (-1, 1)]
    + [(a, b, 0) for a in (-1, 1) for b in (-1, 1)]
    + [(a, 0, b) for a in (-1, 1) for b in (-1, 1)]
    + [(0, a, b) for a in (-1, 1) for b in (-1, 1)]
)
OPPOSITE = [DIRS.index(tuple(-c for c in d)) for d in DIRS]


def mm(a, b, dims=NN):
    return lax.dot_general(a, b, dims, preferred_element_type=f32)


def parts(x, count):
    out = []
    for _ in range(count):
        out.append(x.astype(bf16).astype(f32))
        x = x - out[-1]
    return out


def iota(shape, dim):
    return lax.broadcasted_iota(i32, shape, dim)


def onehot(mask):
    return jnp.where(mask, 1.0, 0.0).astype(bf16)


def pick_rows(rows, shape):
    index = iota(shape, 0)
    out = jnp.zeros(shape, f32)
    for i, row in rows.items():
        out = jnp.where(index == i, row, out)
    return out


def lane_gather(x, index):
    return jnp.take_along_axis(x, index, axis=1, mode="promise_in_bounds")


def wide(row, rows=SUB):
    return jnp.broadcast_to(row, (rows, row.shape[1]))


def gather_wide(tables, index):
    low, high = index % LANES, index // LANES
    out = lane_gather(tables[0], low)
    for h in range(1, len(tables)):
        out = jnp.where(high == h, lane_gather(tables[h], low), out)
    return out


def lane_pieces(x):
    return [x[:, h : h + LANES] for h in range(0, x.shape[1], LANES)]


def sub_sum(x):
    return jnp.sum(x, axis=0, keepdims=True)


def body(
    sizes,
    *refs,
):
    mx, my, mz, seats, nx, ny = sizes
    operands, refs = refs[:17], refs[17:]
    states = operands[0]
    out, answers_out, wanted_out, inverse, forces_out = refs[:5]
    small, refs = refs[5:21], refs[21:]
    (
        active,
        fibre_index,
        angle_s,
        angle_v,
        conduct,
        gate_half,
        gate_slope,
        gate_tau,
        conductance,
        reversal,
        ids_ref,
        weight_ref,
        node_disp,
        elem_node,
        elem_fibre,
        material,
    ) = small
    (
        held,
        vs,
        flux,
        gate_const,
        tile_const,
        sums,
        bends,
        mine_coef,
        send_y,
        send_z,
        send_xy,
        send_row,
        halo_x,
        halo_y,
        halo_z,
        edge_xy,
        edge_xz,
        edge_yz,
        halo_coef,
        tally,
        turned,
        slot_pos,
        ids_send,
        ids_got,
        ans_send,
        ans_got,
        load_sem,
        small_sem,
        face_send_sem,
        face_recv_sem,
        coef_send_sem,
        coef_recv_sem,
        all_send_sem,
        all_recv_sem,
    ) = refs
    nz = states.shape[3]
    n = mx * my * mz
    gates_n = NSTATE - 2
    strips = nx * ny // SUB
    bx, by, bz = nx // SBX, ny // SBY, nz // SBZ
    plane = bx * by
    blocks = plane * bz
    tiles = nx // TLX
    node_count = node_disp.shape[1]
    elem_count = elem_node.shape[1]
    rows_each = seats // GROUPS
    per_group = LANES // rows_each
    slot_groups = n // per_group
    per_row = LANES // seats
    slot_rows = n // per_row
    cx, cy, cz = (lax.axis_index(a) for a in AXES)
    me = (cx * my + cy) * mz + cz
    at = (cx, cy, cz)
    counts = (mx, my, mz)

    def others():
        steps = [
            (a, b, c) for a in range(mx) for b in range(my) for c in range(mz) if a or b or c
        ]

        def far(step):
            return sum(
                (1 if d == 1 else max(s, m - s)) if s else 0
                for d, (s, m) in enumerate(zip(step, counts))
            )

        return sorted(steps, key=far, reverse=True)

    wrapped = [[jnp.where(p + s >= m, p + s - m, p + s) for s in range(m)] for p, m in zip(at, counts)]

    def each_other(go, keep=lambda k: True):
        if n <= 64:
            for step in (x for k, x in enumerate(others()) if keep(k)):
                go(tuple(wrapped[d][s] for d, s in enumerate(step)))
        elif keep(0):

            def one(k, carry):
                flat = (me + k) % n
                go((flat // (my * mz), (flat // mz) % my, flat % mz))
                return carry

            lax.fori_loop(1, n, one, 0)

    chunk = TLX * ny // SUB // 2

    def load(i):
        here = pl.ds(i * chunk, chunk)
        return pltpu.make_async_copy(states.at[:, here], held.at[:, here], load_sem.at[i])

    for ref in (halo_x, halo_y, halo_z, edge_xy, edge_xz, edge_yz):
        used = ref.shape[1] // 2
        ref[:, :used] = jnp.zeros((ref.shape[0], used) + ref.shape[2:], f32)
    halo_coef[:6] = jnp.zeros((6,) + halo_coef.shape[1:], f32)

    barrier = pltpu.get_barrier_semaphore()
    each_other(
        lambda to: pl.semaphore_signal(barrier, inc=1, device_id=to, device_id_type=MESH)
    )

    small_loads = [
        pltpu.make_async_copy(src, dst, small_sem.at[i])
        for i, (src, dst) in enumerate(zip(operands[1:], small))
    ]
    for c in small_loads:
        c.start()
    for i in range(strips // chunk):
        load(i).start()

    for c in small_loads:
        c.wait()

    def splat(value):
        return jnp.full((SUB, LANES), value, f32)

    angles = jnp.concatenate(
        [angle_v[...], jnp.zeros((2, LANES - angle_v.shape[1]), f32)], 1
    ) if angle_v.shape[1] < LANES else angle_v[...]
    rows = {0: angles[0:1], 1: angles[1:2]}
    across, spread, alive = [], [], []
    for t in range(tiles):
        index = fibre_index[0, 0, t]
        rows[2 + t] = jnp.full((1, LANES), angle_s[0, index], f32)
        rows[2 + tiles + t] = jnp.full((1, LANES), angle_s[1, index], f32)
        across.append(jnp.full((1, LANES), conduct[1, index], f32))
        spread.append(jnp.full((1, LANES), conduct[0, index], f32) - across[t])
        alive.append(jnp.where(active[0, 0, t] > 0, 1.0, 0.0).astype(f32))
    stack = pick_rows(rows, (SUB, LANES))
    cosine, sine = jnp.cos(stack), jnp.sin(stack)

    def frame_of(a, b):
        ca, sa = cosine[a : a + 1], sine[a : a + 1]
        cb, sb = cosine[b : b + 1], sine[b : b + 1]
        return ca * cb, sa * cb, sb

    for t in range(tiles):
        fx, fy, fz = frame_of(2 + t, 2 + tiles + t)
        scale = alive[t] * 0.25
        entries = [
            across[t] + spread[t] * fx * fx,
            across[t] + spread[t] * fy * fy,
            across[t] + spread[t] * fz * fz,
            spread[t] * fx * fy,
            spread[t] * fx * fz,
            spread[t] * fy * fz,
        ]
        mine_coef[t * SUB : (t + 1) * SUB] = pick_rows(
            {k: e * scale for k, e in enumerate(entries)}, (SUB, LANES)
        )

    for g in range(gates_n):
        slope = 0.5 / splat(gate_slope[g])
        gate_const[g, 0] = slope
        gate_const[g, 1] = slope * gate_half[g]
        keep = jnp.exp(-1.0 / splat(gate_tau[g]))
        share = 0.5 * (1.0 - keep)
        cond = splat(conductance[g])
        for t in range(tiles):
            live = splat(alive[t]) > 0.5
            tile_const[t, g, 0] = jnp.where(live, keep, 1.0)
            tile_const[t, g, 1] = jnp.where(live, share, 0.0)
            tile_const[t, g, 2] = jnp.where(live, cond, 0.0)
            pull = cond * reversal[g]
            tile_const[t, g, 3] = jnp.where(live, pull, 0.0)
            tile_const[t, g, 4] = jnp.where(live, cond * share, 0.0)
            tile_const[t, g, 5] = jnp.where(live, pull * share, 0.0)

    def live_calcium(t):
        live = splat(alive[t]) > 0.5
        keep = jnp.where(live, calcium_keep, 1.0)
        share = jnp.where(live, 0.5 * (1.0 - calcium_keep), 0.0)
        return keep, share

    def calcium_of(old, volt, t):
        keep, share = live_calcium(t)
        return old * keep + (jnp.tanh(4.0 * volt - 2.0) * share + share)

    def ionic(i, t):
        where = pl.ds(i * chunk, chunk)
        volt = held[0, where]
        total = jnp.zeros_like(volt)
        shift = jnp.zeros_like(volt)
        for g in range(gates_n):
            bend = jnp.tanh(volt * gate_const[g, 0] - gate_const[g, 1])
            share = tile_const[t, g, 1]
            gate = held[1 + g, where] * tile_const[t, g, 0] + (bend * share + share)
            out[1 + g, where] = gate
            total = total + gate * tile_const[t, g, 2]
            shift = shift + gate * tile_const[t, g, 3]
        star = volt - (volt * total - shift)
        vs[0, pl.ds(i * chunk * SUB, chunk * SUB)] = star.reshape(chunk * SUB, LANES)

    def ionic_before(i, t):
        where = pl.ds(i * chunk, chunk)
        total = jnp.zeros((chunk, SUB, LANES), f32)
        shift = jnp.zeros((chunk, SUB, LANES), f32)
        for g in range(gates_n):
            kept = out[1 + g, where] * tile_const[t, g, 0] + tile_const[t, g, 1]
            out[1 + g, where] = kept
            total = total + kept * tile_const[t, g, 2]
            shift = shift + kept * tile_const[t, g, 3]
        sums[0, where] = total
        sums[1, where] = shift

    def ionic_between(i, t):
        where = pl.ds(i * chunk, chunk)
        volt = out[0, where]
        total = sums[0, where]
        shift = sums[1, where]
        for g in range(gates_n):
            bend = jnp.tanh(volt * gate_const[g, 0] - gate_const[g, 1])
            bends[g, where] = bend
            total = total + bend * tile_const[t, g, 4]
            shift = shift + bend * tile_const[t, g, 5]
        star = volt - (volt * total - shift)
        vs[1, pl.ds(i * chunk * SUB, chunk * SUB)] = star.reshape(chunk * SUB, LANES)

    def ionic_after(i, t):
        where = pl.ds(i * chunk, chunk)
        for g in range(gates_n):
            out[1 + g, where] = out[1 + g, where] + bends[g, where] * tile_const[t, g, 1]

    def over_chunks(step):
        for t in range(tiles):

            def go(i, carry, t=t):
                step(i, t)
                return carry

            lax.fori_loop(2 * t, 2 * t + 2, go, 0)

    flat_in = (bx * bz, by)
    raw = jnp.concatenate(
        parts(ids_ref[...].astype(f32).reshape(flat_in), 3), 0
    ).astype(bf16)
    lane_b = iota((by, blocks), 1)
    put = onehot(lane_b % by == iota((by, blocks), 0))
    spread_ids = mm(raw, put)
    part = bx * bz
    spread_ids = spread_ids[:part] + spread_ids[part : 2 * part] + spread_ids[2 * part :]
    row_b, col_b = iota((part, blocks), 0), iota((part, blocks), 1)
    here = (row_b // bz == (col_b % plane) // by) & (row_b % bz == col_b // plane)
    ids = sub_sum(jnp.where(here, spread_ids, 0.0)).astype(i32)
    shift = elem_count.bit_length() - 1
    owner = lax.shift_right_logical(ids, shift)
    local = ids - owner * elem_count
    owned = onehot(owner == iota((n, blocks), 0))
    before = onehot(iota((blocks, blocks), 0) < iota((blocks, blocks), 1))
    seen = mm(owned, before)
    rank = sub_sum(owned.astype(f32) * seen).astype(i32)
    offset = (me % per_row) * seats
    hit = owner == iota((n, blocks), 0)
    place = onehot(iota((LANES, blocks), 0) == rank + offset)
    sent = mm(jnp.where(hit, (local + 1).astype(f32), 0.0).astype(bf16), place, NT)
    ids_send[...] = sent.reshape(n, 1, LANES)
    group, seat_row = rank % GROUPS, rank // GROUPS
    number = jnp.where(
        group == iota((SUB, blocks), 0), (iota((SUB, blocks), 1) + 1).astype(f32), 0.0
    ).astype(bf16)
    seat_place = owner * rows_each + seat_row
    for g in range(slot_groups):
        block_at = (
            mm(number, onehot(iota((LANES, blocks), 0) + g * LANES == seat_place), NT).astype(i32)
            - 1
        )
        in_plane = block_at % plane
        slot_pos[g] = jnp.where(
            block_at >= 0,
            (block_at // plane // 2) * LANES
            + (in_plane // by) * ny
            + (in_plane % by) * SBY
            + (block_at // plane) % 2,
            -1,
        )
    wanted_out[0:1] = seat_place
    wanted_out[1:2] = group

    raw = jnp.concatenate(parts(weight_ref[...].reshape(flat_in), 2), 0).astype(bf16)
    put = onehot(iota((by, bx * ny), 1) % ny == iota((by, bx * ny), 0) * SBY)
    spread_w = mm(raw, put)
    spread_w = (spread_w[:part] + spread_w[part:]).reshape(bx, bz, bx * ny)
    here = iota((bx, bz, bx * ny), 0) == iota((bx, bz, bx * ny), 2) // ny
    weights = jnp.sum(jnp.where(here, spread_w, 0.0), axis=0)
    weights = jnp.concatenate([weights, jnp.zeros((SUB - bz, bx * ny), f32)], 0)
    weights = weights * (1.0 / (SBX * SBY * SBZ))

    def first(i, t):
        load(i).wait()
        ionic(i, t)
        here = pl.ds(i * chunk, chunk)
        out[NSTATE - 1, here] = calcium_of(held[NSTATE - 1, here], held[0, here], t)

    over_chunks(first)

    def source_of(stage, i):
        d = DIRS[i]
        if i < 2:
            return vs.at[stage, pl.ds(0 if d[0] < 0 else (nx - 2) * ny, 2 * ny)]
        if i < 4:
            return send_y.at[stage, i - 2]
        if i < 6:
            return send_z.at[stage, i - 4]
        if i < 10:
            return send_xy.at[stage, i - 6]
        return send_row.at[stage, 0 if d[2] < 0 else 1]

    families = (
        [(halo_x, 0, 2), (halo_y, 2, 2), (halo_z, 4, 2)]
        + [(edge_xy, 6, 4), (edge_xz, 10, 4), (edge_yz, 14, 4)]
    )

    def exists(i):
        ok = None
        for p, step, m in zip(at, DIRS[i], counts):
            if step:
                inside = p > 0 if step < 0 else p < m - 1
                ok = inside if ok is None else ok & inside
        return ok

    def route(i):
        ok = exists(i)
        swap = next(d for d in (1, 0, 2) if DIRS[i][d] == 0)
        to = []
        for d, (p, step) in enumerate(zip(at, DIRS[i])):
            if step:
                p = jnp.where(ok, p + step, p)
            elif d == swap:
                p = jnp.where(ok, p, p + 1 - 2 * (p % 2))
            to.append(p)
        return tuple(to), ok

    order = list(range(len(DIRS) - 1, -1, -1))

    def prepare(stage):
        for side in range(2):
            for layer in range(2):
                y = layer if side == 0 else ny - 2 + layer
                send_y[stage, side, layer] = vs[stage, pl.ds(y, nx, stride=ny), :]
        for a in range(2):
            for b in range(2):
                row = (nx - 1) * a * ny + (ny - 1) * b
                send_xy[stage, 2 * a + b] = vs[stage, row : row + 1, :]
        columns = jnp.transpose(vs[stage])
        send_z[stage, 0] = columns[0:2]
        send_z[stage, 1] = columns[nz - 2 : nz]
        send_row[stage, 0] = columns[0:1]
        send_row[stage, 1] = columns[nz - 1 : nz]

    def send(stage):
        for i in order:
            ref, first, count = next(f for f in families if f[1] <= i < f[1] + f[2])
            to, ok = route(i)
            slot = jnp.where(ok, OPPOSITE[i] - first, count + i - first)
            pltpu.make_async_remote_copy(
                src_ref=source_of(stage, i),
                dst_ref=ref.at[stage, slot],
                send_sem=face_send_sem.at[stage],
                recv_sem=face_recv_sem.at[stage],
                device_id=to,
                device_id_type=MESH,
            ).start()

    def receive(stage):
        pltpu.make_async_remote_copy(
            src_ref=tally,
            dst_ref=tally,
            send_sem=face_send_sem.at[stage],
            recv_sem=face_recv_sem.at[stage],
            device_id=at,
            device_id_type=MESH,
        ).wait()

    def send_coef():
        for i in range(6):
            to, ok = route(i)
            pltpu.make_async_remote_copy(
                src_ref=mine_coef,
                dst_ref=halo_coef.at[jnp.where(ok, OPPOSITE[i], 6 + i)],
                send_sem=coef_send_sem,
                recv_sem=coef_recv_sem,
                device_id=to,
                device_id_type=MESH,
            ).start()

    def receive_coef():
        pltpu.make_async_remote_copy(
            src_ref=halo_coef.at[pl.ds(0, 6)],
            dst_ref=halo_coef.at[pl.ds(0, 6)],
            send_sem=coef_send_sem,
            recv_sem=coef_recv_sem,
            device_id=at,
            device_id_type=MESH,
        ).wait()

    def all_start(kind, src, dst, keep=lambda k: True):
        if keep(0):
            dst[pl.ds(me, 1)] = src[pl.ds(me, 1)]

        def go(to):
            flat = (to[0] * my + to[1]) * mz + to[2]
            pltpu.make_async_remote_copy(
                src_ref=src.at[flat],
                dst_ref=dst.at[me],
                send_sem=all_send_sem.at[kind],
                recv_sem=all_recv_sem.at[kind],
                device_id=to,
                device_id_type=MESH,
            ).start()

        each_other(go, keep)

    def all_wait(kind, src, dst):
        pltpu.make_async_remote_copy(
            src_ref=src.at[pl.ds(0, n - 1)],
            dst_ref=dst.at[pl.ds(0, n - 1)],
            send_sem=all_send_sem.at[kind],
            recv_sem=all_recv_sem.at[kind],
            device_id=at,
            device_id_type=MESH,
        ).wait()

    def coef_row(ref, t, k):
        return ref[t * SUB + k : t * SUB + k + 1, :]

    def diffuse(stage):
        v = vs[stage].reshape(nx, ny, nz)
        lane = iota((1, nz), 1)
        flat = nx * ny
        lane_f = iota((SUB, flat), 1)

        def both(low, high):
            return pick_rows({0: low, 1: high}, (SUB, flat))

        near = both(halo_z[stage, 0, 1:2], halo_z[stage, 1, 0:1])
        gz = both(
            send_row[stage, 0] - halo_z[stage, 0, 0:1],
            halo_z[stage, 1, 1:2] - send_row[stage, 1],
        )
        xz = [both(edge_xz[stage, 2 * a], edge_xz[stage, 2 * a + 1]) for a in range(2)]
        yz = [both(edge_yz[stage, 2 * a], edge_yz[stage, 2 * a + 1]) for a in range(2)]
        up = pltpu.roll(jnp.where(lane_f < ny, xz[1], near), flat - ny, 1)
        down = pltpu.roll(jnp.where(lane_f >= flat - ny, xz[0], near), ny, 1)
        gx = up - down
        up = jnp.where(
            lane_f % ny == ny - 1, pltpu.roll(yz[1], ny - 1, 1), pltpu.roll(near, flat - 1, 1)
        )
        down = jnp.where(
            lane_f % ny == 0, pltpu.roll(yz[0], flat - ny + 1, 1), pltpu.roll(near, 1, 1)
        )
        gy = up - down

        def coef_z(k):
            return both(
                *(
                    jnp.concatenate(
                        [coef_row(halo_coef.at[4 + s], t, k) for t in range(tiles)], 1
                    )
                    for s in range(2)
                )
            )

        fz = coef_z(4) * gx + coef_z(5) * gy + coef_z(2) * gz
        blank = jnp.zeros((SUB, flat), f32)
        half = nz // 2
        pieces = [blank] * (nz // SUB)
        pieces[0] = pick_rows(
            {0: near[0:1], **{1 + i: edge_xz[stage, i] for i in range(4)}}, (SUB, flat)
        )
        pieces[half // SUB - 1] = pick_rows({SUB - 1: fz[1:2]}, (SUB, flat))
        pieces[half // SUB] = pick_rows(
            {0: fz[0:1], **{1 + i: edge_yz[stage, i] for i in range(4)}}, (SUB, flat)
        )
        pieces[-1] = pick_rows({SUB - 1: near[1:2]}, (SUB, flat))
        turned[...] = jnp.transpose(jnp.concatenate(pieces, 0))

        def along_z(a, low, high):
            return jnp.where(lane == nz - 1, high, pltpu.roll(a, nz - 1, 1)) - jnp.where(
                lane == 0, low, pltpu.roll(a, 1, 1)
            )

        def along_rows(a, low, high):
            row = iota(a.shape, 0)
            m = a.shape[0]
            return jnp.where(row == m - 1, high, pltpu.roll(a, m - 1, 0)) - jnp.where(
                row == 0, low, pltpu.roll(a, 1, 0)
            )

        px, fx_out = [], []
        for s in range(2):
            close = halo_x[stage, s, ny:] if s == 0 else halo_x[stage, s, :ny]
            distant = halo_x[stage, s, :ny] if s == 0 else halo_x[stage, s, ny:]
            gx = v[0] - distant if s == 0 else distant - v[nx - 1]
            gy = along_rows(close, edge_xy[stage, 2 * s], edge_xy[stage, 2 * s + 1])
            first = (nx - 1) * ny if s == 0 else 0
            edge = turned[first : first + ny, :]
            c = 1 + 2 * s
            gz = along_z(close, edge[:, c : c + 1], edge[:, c + 1 : c + 2])
            t = tiles - 1 if s == 0 else 0
            k = [coef_row(halo_coef.at[s], t, j) for j in (0, 3, 4)]
            px.append(close)
            fx_out.append(k[0] * gx + k[1] * gy + k[2] * gz)
        py, fy_out = [], []
        for s in range(2):
            close, distant = halo_y[stage, s, 1 - s], halo_y[stage, s, s]
            own = vs[stage, pl.ds(0 if s == 0 else ny - 1, nx, stride=ny), :]
            gy = own - distant if s == 0 else distant - own
            gx = along_rows(close, edge_xy[stage, s], edge_xy[stage, 2 + s])
            edge = turned[pl.ds(ny - 1 if s == 0 else 0, nx, stride=ny), :]
            c = half + 1 + 2 * s
            gz = along_z(close, edge[:, c : c + 1], edge[:, c + 1 : c + 2])

            def coef_y(j, s=s):
                return jnp.concatenate(
                    [wide(coef_row(halo_coef.at[2 + s], t, j), TLX) for t in range(tiles)], 0
                )

            py.append(close)
            fy_out.append(coef_y(3) * gx + coef_y(1) * gy + coef_y(5) * gz)

        def diff_x(a, low, high):
            return jnp.concatenate([a[1:], high[None]], 0) - jnp.concatenate([low[None], a[:-1]], 0)

        def diff_y(a, low, high):
            row = iota((1, ny, nz), 1)
            up = jnp.where(row == ny - 1, high.reshape(nx, 1, nz), pltpu.roll(a, ny - 1, 1))
            down = jnp.where(row == 0, low.reshape(nx, 1, nz), pltpu.roll(a, 1, 1))
            return up - down

        def diff_z(a, edge):
            lane = iota((1, 1, nz), 2)
            up = jnp.where(lane == nz - 1, edge, pltpu.roll(a, nz - 1, 2))
            down = jnp.where(lane == 0, edge, pltpu.roll(a, 1, 2))
            return up - down

        edges = turned[...].reshape(nx, ny, nz)
        gx, gy, gz = diff_x(v, *px), diff_y(v, *py), diff_z(v, edges)
        for t in range(tiles):
            span = slice(t * TLX, (t + 1) * TLX)
            xx, yy, zz, xy, xz_, yz_ = (
                coef_row(mine_coef, t, k).reshape(1, 1, LANES) for k in range(6)
            )
            a, b, c = gx[span], gy[span], gz[span]
            flux[0, span] = xx * a + xy * b + xz_ * c
            flux[1, span] = xy * a + yy * b + yz_ * c
            flux[2, span] = xz_ * a + yz_ * b + zz * c
        edges = pltpu.roll(edges, half, 2)
        lap = (
            diff_x(flux[0], *fx_out)
            + diff_y(flux[1], *fy_out)
            + diff_z(flux[2], edges)
        )
        for t in range(tiles):
            span = slice(t * TLX, (t + 1) * TLX)
            new = v[span] + lap[span] * alive[t]
            where = pl.ds(t * TLX * ny // SUB, TLX * ny // SUB)
            out[0, where] = new.reshape(TLX * ny // SUB, SUB, LANES)

    prepare(0)
    pl.semaphore_wait(barrier, n - 1)
    half = n // 2
    all_start(0, ids_send, ids_got, lambda k: k < half)
    send(0)
    all_start(0, ids_send, ids_got, lambda k: k >= half)
    send_coef()


    over_chunks(ionic_before)
    nodes = elem_node[...]
    disp = []
    for c in range(3):
        table = [
            wide(node_disp[c : c + 1, g : g + LANES]) for g in range(0, node_count, LANES)
        ]
        disp.append([gather_wide(table, ix) for ix in lane_pieces(nodes)])
    fx, fy, fz = frame_of(0, 1)
    table = [pick_rows({0: fx, 1: fy, 2: fz}, (SUB, LANES))]
    frame8 = [gather_wide(table, wide(ix)) for ix in lane_pieces(elem_fibre[...])]
    corner = iota((CORNERS, LANES), 0)
    signs = [
        jnp.where((corner // (4 >> j)) % 2 == 1, 0.25, -0.25) for j in range(3)
    ]
    shear, bulk, scale = material[0], material[1], material[2]
    for h in range(elem_count // LANES):
        frame = [frame8[h][i : i + 1] for i in range(3)]
        d = [
            [
                sub_sum(disp[i][h] * signs[j]) + (1.0 if i == j else 0.0)
                for j in range(3)
            ]
            for i in range(3)
        ]
        cof = [
            [
                d[(i + 1) % 3][(j + 1) % 3] * d[(i + 2) % 3][(j + 2) % 3]
                - d[(i + 1) % 3][(j + 2) % 3] * d[(i + 2) % 3][(j + 1) % 3]
                for j in range(3)
            ]
            for i in range(3)
        ]
        volume = d[0][0] * cof[0][0] + d[0][1] * cof[0][1] + d[0][2] * cof[0][2]
        reciprocal = 1.0 / volume
        logv = jnp.log(volume)
        stress = [
            [
                shear * (d[i][j] - cof[i][j] * reciprocal)
                + bulk * logv * (cof[i][j] * reciprocal)
                for j in range(3)
            ]
            for i in range(3)
        ]
        stretch = [
            scale * (d[i][0] * frame[0] + d[i][1] * frame[1] + d[i][2] * frame[2])
            for i in range(3)
        ]
        along = sum(wide(frame[j]) * signs[j] for j in range(3))
        cut = slice(h * LANES, (h + 1) * LANES)
        for i in range(3):
            forces_out[i, :, cut] = sum(wide(stress[i][j]) * signs[j] for j in range(3))
            forces_out[3 + i, :, cut] = wide(stretch[i]) * along

    found = jnp.zeros((CORNERS, node_count), f32)
    lane_e = (iota((CORNERS, elem_count), 1) + 1).astype(f32)
    for q in range(CORNERS):
        named = onehot(iota((node_count, elem_count), 0) == nodes[q : q + 1, :])
        mine = jnp.where(iota((CORNERS, elem_count), 0) == q, lane_e, 0.0).astype(bf16)
        found = found + mm(mine, named, NT)
    inverse[...] = found.astype(i32) - 1

    receive(0)
    receive_coef()
    diffuse(0)

    pulls = []
    for t in range(tiles):
        where = pl.ds(t * TLX * ny // SUB, TLX * ny // SUB)
        calcium = calcium_of(out[NSTATE - 1, where], out[0, where], t)
        out[NSTATE - 1, where] = calcium
        square = calcium * calcium
        pulls.append(square / (square + tension_half))
    pull = jnp.concatenate(pulls, 0).reshape(bx, SBX, ny, nz)
    pull = (pull[:, 0] + pull[:, 1]).reshape(bx * ny, nz)
    strip = onehot(iota((SUB, nz), 1) // SBZ == iota((SUB, nz), 0))
    high = pull.astype(bf16)
    rest = (pull - high.astype(f32)).astype(bf16)
    pooled = mm(strip, high, NT) + mm(strip, rest, NT)
    lanes_p = bx * ny
    value = (pooled + pltpu.roll(pooled, lanes_p - 1, 1)) * weights
    even = iota((1, lanes_p), 1) % 2 == 0
    odd_value = pltpu.roll(value, 1, 1)
    tables = [
        wide(jnp.where(even, value[b : b + 1], odd_value[b + 1 : b + 2]))
        for b in range(0, bz, 2)
    ]
    value_rows = []
    for g in range(slot_groups):
        where = slot_pos[g]
        value_rows.append(
            jnp.where(where >= 0, gather_wide(tables, jnp.maximum(where, 0)), 0.0)
        )

    all_wait(0, ids_send, ids_got)
    asked = []
    for r in range(0, n, per_row):
        total = ids_got[r]
        for m in range(1, per_row):
            total = total + ids_got[r + m]
        asked.append(total)
    asked_wide = [wide(row) for row in asked]
    place = iota((SUB, LANES), 1)
    for g in range(slot_groups):
        device_at = g * per_group + place // rows_each
        rows_out = []
        for k in range(GROUPS):
            source = (device_at % per_row) * seats + (place % rows_each) * GROUPS + k
            where = None
            for r in range(g * per_group // per_row, -(-(g + 1) * per_group // per_row)):
                found = lane_gather(asked_wide[r], source)
                where = (
                    found if where is None else jnp.where(device_at // per_row == r, found, where)
                )
            where = jnp.maximum(where.astype(i32) - 1, 0)
            rows_out += [gather_wide(disp[c], where) for c in range(3)]
            rows_out.append(wide(value_rows[g][k : k + 1]))
        answer = jnp.transpose(jnp.concatenate(rows_out, 0))
        ans_send[g * per_group : (g + 1) * per_group] = answer.reshape(
            per_group, rows_each, LANES
        )
    all_start(1, ans_send, ans_got)
    over_chunks(ionic_between)
    prepare(1)
    send(1)
    over_chunks(ionic_after)

    code = jnp.zeros((LANES, elem_count), f32)
    ident = (iota((LANES, elem_count), 1) + 1).astype(f32)
    row = iota((LANES, 1), 0)

    def arrival(lane, r):
        seat = lane % seats
        lane = (r * per_row + lane // seats) * rows_each + seat // GROUPS
        return ((lane // LANES * GROUPS + seat % GROUPS) * LANES + lane % LANES).astype(f32)

    column = jnp.transpose(
        jnp.concatenate(asked + [jnp.zeros((LANES - slot_rows, LANES), f32)], 0)
    )
    for r in range(slot_rows):
        code = jnp.where(column[:, r : r + 1] == ident, arrival(row, r), code)
    wanted_out[2:3] = sub_sum(code).astype(i32)

    receive(1)
    diffuse(1)

    all_wait(1, ans_send, ans_got)
    answers_out[...] = ans_got[...]


def write_out(
    states,
    answers,
    wanted,
    inverse,
    forces,
    states_out,
    fine_out,
    resid_out,
    fine,
    resid,
    sems,
):
    n, rows_each = answers.shape[:2]
    nx, ny, nz = fine.shape[1:]
    bx, by, bz = nx // SBX, ny // SBY, nz // SBZ
    plane = bx * by
    blocks = plane * bz
    per_group = LANES // rows_each
    slot_groups = n // per_group
    elem_count = forces.shape[2]
    copies = [
        pltpu.make_async_copy(states, states_out, sems.at[0]),
        pltpu.make_async_copy(resid, resid_out, sems.at[1]),
    ]
    copies[0].start()

    def fine_copy(i):
        here = pl.ds(i * nx // PIECES, nx // PIECES)
        return pltpu.make_async_copy(fine.at[:, here], fine_out.at[:, here], sems.at[2 + i])

    columns = [
        jnp.transpose(answers[g * per_group : (g + 1) * per_group].reshape(LANES, LANES))
        for g in range(slot_groups)
    ]

    tables = [
        wide(col[k * SPAN + 3 * CORNERS : k * SPAN + 3 * CORNERS + 1])
        for col in columns
        for k in range(GROUPS)
    ]
    tension = [gather_wide(tables, wide(ix)) for ix in lane_pieces(wanted[2:3])]
    force = [
        [
            forces[i, :, h * LANES : (h + 1) * LANES]
            + tension[h] * forces[3 + i, :, h * LANES : (h + 1) * LANES]
            for h in range(elem_count // LANES)
        ]
        for i in range(3)
    ]
    for g in range(0, inverse.shape[1], LANES):
        where = inverse[:, g : g + LANES]
        index = jnp.maximum(where, 0)
        for i in range(3):
            got = jnp.where(where >= 0, gather_wide(force[i], index), 0.0)
            resid[i : i + 1, g : g + LANES] = sub_sum(got)
    copies[1].start()

    halves = []
    for h in range(blocks // LANES):
        cut = slice(h * LANES, (h + 1) * LANES)
        where, which = wide(wanted[0:1, cut]), wide(wanted[1:2, cut])
        rows_in = []
        for c in range(3):
            value = None
            for k in range(GROUPS):
                first = k * SPAN + c * CORNERS
                found = gather_wide([col[first : first + CORNERS] for col in columns], where)
                value = found if value is None else jnp.where(which == k, found, value)
            value = 0.75 * value + 0.25 * pltpu.roll(value, 4, 0)
            swapped = jnp.where(
                iota((SUB, LANES), 0) // 2 % 2 == 1,
                pltpu.roll(value, 2, 0),
                pltpu.roll(value, SUB - 2, 0),
            )
            rows_in.append(0.75 * value + 0.25 * swapped)
        rows_in.append(jnp.zeros((SUB, LANES), f32))
        halves.append(jnp.concatenate(rows_in, 0))
    stacked = []
    for b in range(bz):
        lane0 = b * plane
        piece = halves[lane0 // LANES]
        stacked.append(
            pltpu.roll(piece, LANES - lane0 % LANES, 1) if lane0 % LANES else piece
        )
    around = jnp.transpose(jnp.concatenate(stacked, 0))
    lane = iota((SUB, nz), 1)
    strip_lane = lane // SBZ * SPAN
    xi = ((lane % SBZ).astype(f32) + 0.5) / SBZ
    for p in range(bx):
        near = around[p * by : (p + 1) * by]
        for c in range(3):
            for iv in range(SBX):
                for jv in range(SBY):
                    first = c * SUB + 4 * iv + 2 * jv
                    low = lane_gather(near, strip_lane + first)
                    high = lane_gather(near, strip_lane + first + 1)
                    fine[c, SBX * p + iv, pl.ds(jv, by, stride=SBY), :] = (
                        low + (high - low) * xi
                    )
        if (p + 1) % (bx // PIECES) == 0:
            fine_copy(p // (bx // PIECES)).start()
    for i in range(PIECES):
        fine_copy(i).wait()
    for c in copies:
        c.wait()


def shards(
    states,
    active,
    fibre_index,
    fibre_angle,
    conduct,
    gate_half,
    gate_slope,
    gate_tau,
    conductance,
    reversal,
    block_elem,
    block_weight,
    node_disp,
    elem_node,
    elem_fibre,
    material,
):
    mx, my, mz = (lax.axis_size(a) for a in AXES)
    n = mx * my * mz
    elem_count = elem_node.shape[1]
    node_count = node_disp.shape[1]
    nx, ny, nz = states.shape[1:]
    bx, by, bz = block_elem.shape
    blocks = bx * by * bz
    seats = max(2 * blocks // n, 8)
    tiles = nx // TLX
    strips = nx * ny // SUB
    rows_each = seats // GROUPS
    ids = block_elem.transpose(0, 2, 1)
    weight = block_weight.transpose(0, 2, 1)
    vmem = pl.BlockSpec(memory_space=pltpu.VMEM)
    hbm = pl.BlockSpec(memory_space=pltpu.HBM)
    gates_n = NSTATE - 2
    halo_floats = 4 * (nx + ny + 1) * nz + 12 * nx * ny
    operands = (
        states.reshape(NSTATE, strips, SUB, nz),
        active.transpose(1, 2, 0),
        fibre_index.transpose(1, 2, 0),
        fibre_angle,
        fibre_angle,
        conduct,
        gate_half,
        gate_slope,
        gate_tau,
        conductance,
        reversal,
        ids,
        weight,
        node_disp,
        elem_node,
        elem_fibre.reshape(1, elem_count),
        material,
    )
    stage = FINE_STEPS
    states_shape = jax.ShapeDtypeStruct((NSTATE, strips, SUB, nz), f32)
    fine_shape = jax.ShapeDtypeStruct((3, nx, ny, nz), f32)
    resid_shape = jax.ShapeDtypeStruct((3, node_count), f32)
    in_smem = [True] * 3 + [False] + [True] * 6 + [False] * 5 + [True]
    results = pl.pallas_call(
        functools.partial(body, (mx, my, mz, seats, nx, ny)),
        out_shape=(
            states_shape,
            jax.ShapeDtypeStruct((n, rows_each, LANES), f32),
            jax.ShapeDtypeStruct((3, blocks), i32),
            jax.ShapeDtypeStruct((CORNERS, node_count), i32),
            jax.ShapeDtypeStruct((6, CORNERS, elem_count), f32),
        ),
        in_specs=[hbm] * len(operands),
        out_specs=(vmem,) * 5,
        scratch_shapes=[
            (pltpu.SMEM if scalar else pltpu.VMEM)(x.shape, x.dtype)
            for scalar, x in zip(in_smem, operands[1:])
        ]
        + [
            pltpu.VMEM((NSTATE, strips, SUB, nz), f32),
            pltpu.VMEM((stage, nx * ny, nz), f32),
            pltpu.VMEM((3, nx, ny, nz), f32),
            pltpu.VMEM((gates_n, 2, SUB, LANES), f32),
            pltpu.VMEM((tiles, gates_n, 6, SUB, LANES), f32),
            pltpu.VMEM((2, strips, SUB, nz), f32),
            pltpu.VMEM((gates_n, strips, SUB, nz), f32),
            pltpu.VMEM((tiles * SUB, LANES), f32),
            pltpu.VMEM((stage, 2, 2, nx, nz), f32),
            pltpu.VMEM((stage, 2, 2, nx * ny), f32),
            pltpu.VMEM((stage, 4, 1, nz), f32),
            pltpu.VMEM((stage, 2, 1, nx * ny), f32),
            pltpu.VMEM((stage, 4, 2 * ny, nz), f32),
            pltpu.VMEM((stage, 4, 2, nx, nz), f32),
            pltpu.VMEM((stage, 4, 2, nx * ny), f32),
            pltpu.VMEM((stage, 8, 1, nz), f32),
            pltpu.VMEM((stage, 8, 1, nx * ny), f32),
            pltpu.VMEM((stage, 8, 1, nx * ny), f32),
            pltpu.VMEM((12, tiles * SUB, LANES), f32),
            pltpu.VMEM((halo_floats // LANES, 1, LANES), f32),
            pltpu.VMEM((nx * ny, nz), f32),
            pltpu.VMEM((n * rows_each // LANES, SUB, LANES), i32),
            pltpu.VMEM((n, 1, LANES), f32),
            pltpu.VMEM((n, 1, LANES), f32),
            pltpu.VMEM((n, rows_each, LANES), f32),
            pltpu.VMEM((n, rows_each, LANES), f32),
            pltpu.SemaphoreType.DMA((2 * tiles,)),
            pltpu.SemaphoreType.DMA((len(operands) - 1,)),
            pltpu.SemaphoreType.DMA((stage,)),
            pltpu.SemaphoreType.DMA((stage,)),
            pltpu.SemaphoreType.DMA,
            pltpu.SemaphoreType.DMA,
            pltpu.SemaphoreType.DMA((2,)),
            pltpu.SemaphoreType.DMA((2,)),
        ],
        compiler_params=pltpu.CompilerParams(
            collective_id=0, has_side_effects=True, vmem_limit_bytes=20 * 1024 * 1024
        ),
        name="step",
    )(*(pltpu.with_memory_space_constraint(a, pltpu.HBM) for a in operands))
    results = pl.pallas_call(
        write_out,
        out_shape=(states_shape, fine_shape, resid_shape),
        in_specs=[vmem] * 5,
        out_specs=(hbm,) * 3,
        scratch_shapes=[
            pltpu.VMEM((3, nx, ny, nz), f32),
            pltpu.VMEM((3, node_count), f32),
            pltpu.SemaphoreType.DMA((2 + PIECES,)),
        ],
        compiler_params=pltpu.CompilerParams(vmem_limit_bytes=20 * 1024 * 1024),
        name="write",
    )(*results)
    return results[0].reshape(states.shape), results[1], results[2]


def solution(mesh):
    in_specs = (
        P(None, "gx", "gy", "gz"),
        P("gx", "gy", "gz"),
        P("gx", "gy", "gz"),
        P(),
        P(),
        P(),
        P(),
        P(),
        P(),
        P(),
        P("gx", "gy", "gz"),
        P("gx", "gy", "gz"),
        P(None, ("gx", "gy", "gz")),
        P(None, ("gx", "gy", "gz")),
        P(("gx", "gy", "gz")),
        P(),
    )
    out_specs = (P(None, "gx", "gy", "gz"), P(None, "gx", "gy", "gz"), P(None, ("gx", "gy", "gz")))
    return jax.shard_map(shards, mesh=mesh, in_specs=in_specs, out_specs=out_specs, check_vma=False)
```
